32 devices in a mesh: gx: 8 (over z, core), gy: 4 (over y, x).
Axes of the slice: x: 2, y: 2, z: 4, core: 2. Of those that a mesh axis runs over, the one named last changes fastest.
Arguments:
- tangent_e: float32 [3, 64, 64, 256], P(None, 'gx', 'gy'), may hold values from -6 to 6
- tangent_h: float32 [3, 64, 64, 256], P(None, 'gx', 'gy'), may hold values from -6 to 6
- forward_e: float32 [3, 64, 64, 4], P(None, 'gx', 'gy'), may hold values from -6 to 6
- forward_h: float32 [3, 64, 64, 4], P(None, 'gx', 'gy'), may hold values from -6 to 6
- class_map: int32 [64, 64, 4], P('gx', 'gy'), may hold values from 0 to 63
- material: int32 [64, 64, 4], P('gx', 'gy'), may hold values from 0 to 3
- permittivity: float32 [4], replicated, may hold values from 1 to 4
- contrast: float32 [4], replicated, may hold values from 0.5 to 2
- order_list: int32 [1024, 2], replicated, may hold values from -16 to 16
Outputs:
- new_tangent_e: float32 [3, 64, 64, 256], P(None, 'gx', 'gy')
- new_tangent_h: float32 [3, 64, 64, 256], P(None, 'gx', 'gy')
- order_sens: float32 [1024, 256], P(('gx', 'gy'))
The draws below stay inside these ranges and needn't reach their ends.
Inputs may be any that keep to these rules, and one draw needn't show every extreme that they name: `class_map`: feature class of each cell, naming its tangent direction.
All inputs are finite; a program needn't handle non-finite values.
Results may differ from the reference program's by a relative error of at most 0.0003.
Values sent between devices are 32-bit elements; how exact they have to be, the bound alone decides.
A program may use at most 64 MiB of HBM per device.

```python
import math
import jax
import jax.numpy as jnp
from jax import lax

NZ = 4
DIRS = 64
NMAT = 4
ORDERS = 1024
ORDER_MAX = 16
STEPS = 2
NX = 64
NY = 64


def with_ends(result, key, least, largest):
    extent = result.shape
    index_at = [jax.random.randint(jax.random.fold_in(key, axis), (), 0, extent[axis]) for axis in range(len(extent))]
    result = result.at[tuple(index_at)].set(least)
    longest = extent.index(max(extent))
    index_at[longest] = (index_at[longest] + 1) % extent[longest]
    return result.at[tuple(index_at)].set(largest)


def levels(key, extent, pieces, smallest, top_value):
    factor_of = 1.0
    for dim, shards_of in pieces:
        steps = jax.random.uniform(jax.random.fold_in(jax.random.fold_in(key, 6), dim), (shards_of,), jnp.float32, smallest / len(pieces), top_value / len(pieces))
        factor_of = factor_of * jnp.repeat(jnp.exp(steps), extent[dim] // shards_of).reshape((-1,) + (1,) * (len(extent) - 1 - dim))
    return factor_of


def centred(key, extent, deviation, most, cuts=(), kind=jnp.bfloat16):
    entries = deviation * jax.random.normal(key, extent, jnp.float32)
    if cuts:
        entries = entries * levels(key, extent, cuts, -0.22, 0.18)
    return jnp.clip(entries, -most, most).astype(kind)


def setup_inputs(seed: int = 0) -> dict:
    streams_of = jax.random.split(jax.random.key(seed), 10)
    return {
        "tangent_e": centred(streams_of[0], (3, NX, NY, NZ * DIRS), 1.0, 6.0, ((1, 8), (2, 4)), jnp.float32),
        "tangent_h": centred(streams_of[1], (3, NX, NY, NZ * DIRS), 1.0, 6.0, ((1, 8), (2, 4)), jnp.float32),
        "forward_e": centred(streams_of[2], (3, NX, NY, NZ), 1.0, 6.0, ((1, 8), (2, 4)), jnp.float32),
        "forward_h": centred(streams_of[3], (3, NX, NY, NZ), 1.0, 6.0, ((1, 8), (2, 4)), jnp.float32),
        "class_map": with_ends(jax.random.randint(streams_of[4], (NX, NY, NZ), 0, DIRS), jax.random.fold_in(streams_of[4], 1), 0, DIRS - 1).astype(jnp.int32),
        "material": with_ends(jax.random.randint(streams_of[5], (NX, NY, NZ), 0, NMAT), jax.random.fold_in(streams_of[5], 1), 0, NMAT - 1).astype(jnp.int32),
        "permittivity": jnp.clip(jnp.exp(jax.random.uniform(streams_of[6], (NMAT,), jnp.float32, math.log(1.0), math.log(4.0))), 1.0, 4.0),
        "contrast": jnp.clip(jnp.exp(jax.random.uniform(streams_of[7], (NMAT,), jnp.float32, math.log(0.5), math.log(2.0))), 0.5, 2.0),
        "order_list": with_ends(jax.random.randint(streams_of[8], (ORDERS, 2), -ORDER_MAX, ORDER_MAX + 1), jax.random.fold_in(streams_of[8], 1), -ORDER_MAX, ORDER_MAX).astype(jnp.int32),
    }


time_step = 0.5

def next_z(field, unit):
    return jnp.concatenate([field[..., unit:], jnp.zeros_like(field[..., :unit])], -1)

def prev_z(field, unit):
    return jnp.concatenate([jnp.zeros_like(field[..., :unit]), field[..., :-unit]], -1)

def curl_forward(field, unit):
    field_x, field_y, field_z = (field[0], field[1], field[2])
    curl_x = jnp.roll(field_z, -1, 1) - field_z - (next_z(field_y, unit) - field_y)
    curl_y = next_z(field_x, unit) - field_x - (jnp.roll(field_z, -1, 0) - field_z)
    curl_z = jnp.roll(field_y, -1, 0) - field_y - (jnp.roll(field_x, -1, 1) - field_x)
    return jnp.stack([curl_x, curl_y, curl_z])

def curl_backward(field, unit):
    field_x, field_y, field_z = (field[0], field[1], field[2])
    curl_x = field_z - jnp.roll(field_z, 1, 1) - (field_y - prev_z(field_y, unit))
    curl_y = field_x - prev_z(field_x, unit) - (field_z - jnp.roll(field_z, 1, 0))
    curl_z = field_y - jnp.roll(field_y, 1, 0) - (field_x - jnp.roll(field_x, 1, 1))
    return jnp.stack([curl_x, curl_y, curl_z])

def cell_values(material, table):
    hits = (material[..., None] == jnp.arange(table.shape[0], dtype=jnp.int32)).astype(jnp.float32)
    return lax.optimization_barrier(jnp.sum(hits * table, -1))

def reference(tangent_e, tangent_h, forward_e, forward_h, class_map, material, permittivity, contrast, order_list):
    eps_cell = cell_values(material, permittivity)
    inverse = time_step / eps_cell
    coef = time_step * cell_values(material, contrast) / (eps_cell * eps_cell)
    inverse_wide = jnp.repeat(inverse, DIRS, axis=-1)
    onehot = (class_map[..., None] == jnp.arange(DIRS, dtype=jnp.int32)).astype(jnp.float32)
    for step in range(STEPS):
        forward_h = forward_h - time_step * curl_forward(forward_e, 1)
        tangent_h = tangent_h - time_step * curl_forward(tangent_e, DIRS)
        curl_fwd = curl_backward(forward_h, 1)
        forward_e = forward_e + inverse[None] * curl_fwd
        curl_tan = curl_backward(tangent_h, DIRS)
        source = ((coef[None] * curl_fwd)[..., None] * onehot[None]).reshape(tangent_e.shape)
        tangent_e = tangent_e + inverse_wide[None] * curl_tan - source
    top = tangent_e[0:2, :, :, (NZ - 1) * DIRS:]
    top = jnp.transpose(top, (1, 2, 0, 3)).reshape(NX * NY, 2 * DIRS)
    xs = jnp.arange(NX, dtype=jnp.int32)
    ys = jnp.arange(NY, dtype=jnp.int32)
    factor = 2.0 * math.pi / (NX * NY)
    scale = 1.0 / math.sqrt(NX * NY)

    def block(pairs):
        order_m = pairs[:, 0]
        order_n = pairs[:, 1]
        count = pairs.shape[0]
        index = order_m[:, None, None] * xs[None, :, None] * NY + order_n[:, None, None] * ys[None, None, :] * NX
        index = jnp.mod(index, NX * NY).reshape(count, NX * NY)
        theta = index.astype(jnp.float32) * factor
        real = jnp.dot(jnp.cos(theta), top, precision=lax.Precision.HIGHEST, preferred_element_type=jnp.float32)
        imag = -jnp.dot(jnp.sin(theta), top, precision=lax.Precision.HIGHEST, preferred_element_type=jnp.float32)
        both = jnp.stack([real.reshape(count, 2, DIRS), imag.reshape(count, 2, DIRS)], 2)
        return both.reshape(count, 4 * DIRS) * scale
    order_sens = lax.map(block, order_list.reshape(ORDERS // 128, 128, 2)).reshape(ORDERS, 4 * DIRS)
    return (tangent_e, tangent_h, order_sens)
```

```python
import functools
import math

import jax
import jax.numpy as jnp
from jax import lax
from jax.experimental import pallas as pl
from jax.experimental.pallas import tpu as pltpu
from jax.sharding import PartitionSpec as P

DIRS = 64
STEPS = 2
LAYERS = 4
WIDE = LAYERS * DIRS
HALF = WIDE // 2
time_step = 0.5


def lanes_of(shape):
    return lax.broadcasted_iota(jnp.int32, shape, len(shape) - 1)


def sublanes_of(shape):
    return lax.broadcasted_iota(jnp.int32, shape, len(shape) - 2)


def next_z(f):
    wide = f.shape[-1]
    return jnp.where(lanes_of(f.shape) < wide - DIRS, pltpu.roll(f, wide - DIRS, f.ndim - 1), 0.0)


def prev_z(f):
    return jnp.where(lanes_of(f.shape) >= DIRS, pltpu.roll(f, DIRS, f.ndim - 1), 0.0)


def after_rows(f, row):
    n = f.shape[-2]
    return jnp.where(sublanes_of(f.shape) == n - 1, row, pltpu.roll(f, n - 1, f.ndim - 2))


def before_rows(f, row):
    return jnp.where(sublanes_of(f.shape) == 0, row, pltpu.roll(f, 1, f.ndim - 2))


def after_x(f, plane):
    return jnp.concatenate([f[1:], plane[None]], 0)


def before_x(f, plane):
    return jnp.concatenate([plane[None], f[:-1]], 0)


def packed(v):
    low, high = v[..., :HALF], v[..., HALF:]
    return jnp.where(lanes_of(low.shape) % DIRS < DIRS // 2, low, high)


def unpacked(v):
    near = lanes_of(v.shape) % DIRS < DIRS // 2
    axis = v.ndim - 1
    low = jnp.where(near, v, pltpu.roll(v, DIRS // 2, axis))
    high = jnp.where(near, pltpu.roll(v, HALF - DIRS // 2, axis), v)
    return jnp.concatenate([low, high], axis)


def take(buf, at, n):
    tangent = [jnp.concatenate([buf[at, 2 * k], buf[at, 2 * k + 1]], -1) for k in range(n)]
    forward = [unpacked(buf[at, 2 * n + k]) for k in range(n)]
    return (tangent, forward)


def sine(turn):
    u = turn * (2.0 * math.pi)
    s = u * u
    poly = -1.0 / 39916800.0
    for c in (1.0 / 362880.0, -1.0 / 5040.0, 1.0 / 120.0, -1.0 / 6.0):
        poly = poly * s + c
    return u + u * (s * poly)


def half_step_h(e, h, rim):
    ex, ey, ez = e
    hx, hy, hz = h
    xp, yp, xm, ym, cx, cy = rim
    new = (
        hx - time_step * ((after_rows(ez, yp[1][:, None, :]) - ez) - (next_z(ey) - ey)),
        hy - time_step * ((next_z(ex) - ex) - (after_x(ez, xp[1]) - ez)),
        hz - time_step * ((after_x(ey, xp[0]) - ey) - (after_rows(ex, yp[0][:, None, :]) - ex)),
    )
    x_y = xm[3] - time_step * ((next_z(xm[0]) - xm[0]) - (ez[0] - xm[2]))
    x_z = xm[4] - time_step * ((ey[0] - xm[1]) - (after_rows(xm[0], cx) - xm[0]))
    y_x = ym[3] - time_step * ((ez[:, 0, :] - ym[2]) - (next_z(ym[1]) - ym[1]))
    y_z = ym[4] - time_step * ((after_rows(ym[1], cy) - ym[1]) - (ex[:, 0, :] - ym[0]))
    return new, (x_y, x_z, y_x, y_z)


def curl_b(h, rim):
    hx, hy, hz = h
    x_y, x_z, y_x, y_z = rim
    return (
        (hz - before_rows(hz, y_z[:, None, :])) - (hy - prev_z(hy)),
        (hx - prev_z(hx)) - (hz - before_x(hz, x_z)),
        (hy - before_x(hy, x_y)) - (hx - before_rows(hx, y_x[:, None, :])),
    )


def advance(e, h, rims, fwd_e, fwd_h, fwd_rims, inverse, coef):
    fwd_h, rim = half_step_h(fwd_e, fwd_h, fwd_rims)
    fwd_c = curl_b(fwd_h, rim)
    fwd_e = [fwd_e[c] + inverse * fwd_c[c] for c in range(3)]
    h, rim = half_step_h(e, h, rims)
    tan_c = curl_b(h, rim)
    e = [e[c] + inverse * tan_c[c] - coef * fwd_c[c] for c in range(3)]
    return e, h, fwd_e, fwd_h


def split(v):
    parts = []
    for _ in range(3):
        parts.append(v.astype(jnp.bfloat16))
        v = v - parts[-1].astype(jnp.float32)
    return parts


def widened(layers, ny):
    lead = layers[0].shape[0]
    flat = LAYERS * ny
    total = 0.0
    for z in range(LAYERS):
        for k, part in enumerate(split(layers[z])):
            place = (
                lax.broadcasted_iota(jnp.int32, (ny, 3 * flat), 1)
                == lax.broadcasted_iota(jnp.int32, (ny, 3 * flat), 0) + (k * flat + z * ny)
            ).astype(jnp.float32)
            total = total + jnp.dot(part, place.astype(jnp.bfloat16), preferred_element_type=jnp.float32)
    rows = jnp.broadcast_to(total[:, None, :], (lead, ny, 3 * flat))
    rows = jnp.where(lanes_of(rows.shape) % ny == sublanes_of(rows.shape), rows, 0.0)
    spread = (
        (lax.broadcasted_iota(jnp.int32, (3 * flat, WIDE), 0) // ny) % LAYERS
        == lax.broadcasted_iota(jnp.int32, (3 * flat, WIDE), 1) // DIRS
    ).astype(jnp.float32)
    wide = jnp.dot(
        rows.reshape(lead * ny, 3 * flat).astype(jnp.bfloat16),
        spread.astype(jnp.bfloat16),
        preferred_element_type=jnp.float32,
    )
    return wide.reshape(lead, ny, WIDE)


def kernel(
    nx, ny, own,
    te_at, th_at, fe_at, fh_at, classes_at, material_at, permittivity_at, contrast_at, orders_at,
    out_e, out_h, out_s,
    s_xm, r_xm, s_xp, r_xp, s_ym, r_ym, s_yp, r_yp, s_cx, r_cx, s_cy, r_cy,
    tops, gathered, partial, arrived, table,
    rim_send, rim_recv, g_send, g_recv, p_send, p_recv,
    te, th, fe, fh, classes, material, permittivity, contrast, orders, load,
):
    loads = [
        pltpu.make_async_copy(src, dst, load.at[k])
        for k, (src, dst) in enumerate((
            *[(src.at[c], dst.at[c]) for c in range(3) for src, dst in ((te_at, te), (th_at, th))],
            (fe_at, fe), (fh_at, fh), (classes_at, classes),
            (material_at, material), (permittivity_at, permittivity), (contrast_at, contrast),
            (orders_at, orders),
        ))
    ]
    for c in loads:
        c.start()
    wx, wy = te.shape[1], te.shape[2]
    i, j = lax.axis_index("gx"), lax.axis_index("gy")
    up, down = lax.rem(i + 1, nx), lax.rem(i + nx - 1, nx)
    right, left = lax.rem(j + 1, ny), lax.rem(j + ny - 1, ny)
    barrier = pltpu.get_barrier_semaphore()
    core = lax.rem(i, 2)
    mate = i + 1 - 2 * core
    line = [(lax.rem(i + d, nx), j) for d in range(1, nx)]
    sheet = [(mate, j)] + [(k, lax.rem(j + d, ny)) for d in range(1, ny) for k in (i, mate)]
    peers = line + sheet[1:] + [(up, left), (down, right)]
    for peer in peers:
        pl.semaphore_signal(barrier, inc=1, device_id=peer, device_id_type=pl.DeviceIdType.MESH)

    def copy(src, dst, send, recv, device):
        return pltpu.make_async_remote_copy(
            src_ref=src, dst_ref=dst, send_sem=send, recv_sem=recv,
            device_id=device, device_id_type=pl.DeviceIdType.MESH,
        )

    def planes_of(e, h):
        return (
            [f[:, wy - 1, :] for f in (e[0], e[1], e[2], h[0], h[2])],
            [f[wx - 1] for f in (e[0], e[1], e[2], h[1], h[2])],
            [e[0][:, 0, :], e[2][:, 0, :]],
            [e[1][0], e[2][0]],
            [e[0][wx - 1, 0:1, :]],
            [e[1][0, wy - 1:wy, :]],
        )

    rims = (
        (s_ym, r_ym, (i, right)), (s_xm, r_xm, (up, j)), (s_yp, r_yp, (i, left)),
        (s_xp, r_xp, (down, j)), (s_cx, r_cx, (up, left)), (s_cy, r_cy, (down, right)),
    )

    def put_tangent(step, e, h):
        for (buf, _, _), planes in zip(rims, planes_of(e, h)):
            for k, plane in enumerate(planes):
                buf[step, 2 * k] = plane[:, :HALF]
                buf[step, 2 * k + 1] = plane[:, HALF:]

    def put_forward(step, e, h):
        for (buf, _, _), planes in zip(rims, planes_of(e, h)):
            for k, plane in enumerate(planes):
                buf[step, 2 * len(planes) + k] = packed(plane)

    def send(step, first, part):
        copies = []
        for k, (s, r, device) in enumerate(rims):
            n = s.shape[1] // 3
            span = (pl.ds(0, 3 * n), pl.ds(0, 2 * n), pl.ds(2 * n, n))[part]
            copies.append(copy(
                s.at[step, span], r.at[step, span], rim_send.at[first + k], rim_recv.at[first + k], device
            ))
        for c in copies:
            c.start()
        return copies

    for c in loads[:6]:
        c.wait()
    e = [te[c] for c in range(3)]
    h = [th[c] for c in range(3)]
    put_tangent(0, e, h)
    pl.semaphore_wait(barrier, len(peers))
    waiting = send(0, 0, 1)
    for c in loads[6:]:
        c.wait()
    layers = []
    for z in range(LAYERS):
        layers.append(jnp.concatenate([
            fe[:, :, z, :].reshape(3 * wx, wy), fh[:, :, z, :].reshape(3 * wx, wy),
            classes[:, z, :].astype(jnp.float32), material[:, z, :].astype(jnp.float32),
        ], 0))
    wide = widened(layers, wy)
    fwd_e = [wide[c * wx:(c + 1) * wx] for c in range(3)]
    fwd_h = [wide[c * wx:(c + 1) * wx] for c in range(3, 6)]
    put_forward(0, fwd_e, fwd_h)
    waiting += send(0, 6, 2)

    kind = wide[7 * wx:]
    eps = jnp.zeros_like(kind)
    slope = jnp.zeros_like(kind)
    for k in range(permittivity.shape[0]):
        eps = jnp.where(kind == float(k), permittivity[k], eps)
        slope = jnp.where(kind == float(k), contrast[k], slope)
    inverse = time_step / eps
    coef = time_step * slope / (eps * eps)
    hot = wide[6 * wx:7 * wx] == (lanes_of(kind.shape) % DIRS).astype(jnp.float32)
    coef = jnp.where(hot, coef, 0.0)

    rows, half = nx * own, wx // 2
    block = 2 * half * wy
    cells = ny * block
    count = orders.shape[1]
    row = lax.broadcasted_iota(jnp.int32, (rows, 1), 0)
    target = (row // own) * (ny * own) + j * own + row % own
    pick = (lax.broadcasted_iota(jnp.int32, (rows, count), 1) == target).astype(jnp.float32)
    pair = lax.dot_general(
        pick.astype(jnp.bfloat16), orders[...].astype(jnp.float32).astype(jnp.bfloat16),
        (((1,), (1,)), ((), ())), preferred_element_type=jnp.float32,
    )
    cell = lax.broadcasted_iota(jnp.int32, (1, cells), 1)
    all_x, all_y = nx * wx, ny * wy
    all_cells = float(all_x * all_y)
    x_in = ((cell // (half * wy)) % 2) * wx + (cell // wy) % half
    x_at = (((i - core) * wx + x_in) * all_y).astype(jnp.float32)
    y_at = (((cell // block) * wy + cell % wy) * all_x).astype(jnp.float32)

    def waves(index):
        index = index - all_cells * jnp.round(index * (1.0 / all_cells))
        turn = index * (1.0 / all_cells)
        cosine = sine(0.25 - jnp.abs(turn))
        sines = sine(jnp.where(turn > 0.25, 0.5 - turn, jnp.where(turn < -0.25, -0.5 - turn, turn)))
        return cosine, sines

    for at, value in zip((0, rows), waves(pair[:, 0:1] * x_at + pair[:, 1:2] * y_at)):
        near, far = split(value)[:2]
        for k in range(ny):
            for q, part in enumerate((near, far, near)):
                table[k, at:at + rows, q * block:(q + 1) * block] = part[:, k * block:(k + 1) * block]
    lower = lax.broadcasted_iota(jnp.int32, (rows, 2 * DIRS), 1) < DIRS
    ahead = jnp.where(lower, 0.0, pair[:, 0:1] * float(half * all_y))
    turn_c, turn_s = waves(ahead)
    scale = 1.0 / math.sqrt(all_x * all_y)
    turn_c, turn_s = turn_c * scale, turn_s * scale

    copies = []

    def send_tops(e):
        for q in range(2):
            top = jnp.where(
                lanes_of((half, wy, 2 * DIRS)) < DIRS, pltpu.roll(e[q][:half], DIRS, 2), e[q][half:]
            ).reshape(half * wy, 2 * DIRS)
            tops[q] = top
        for k in reversed(range(len(sheet))):
            to = mate if k % 2 == 0 else i
            q = 1 - core if k % 2 == 0 else core
            c = copy(tops.at[q], gathered.at[(k + 1) // 2, core], g_send.at[k], g_recv.at[k], (to, sheet[k][1]))
            c.start()
            copies.append(c)
        gathered[0, core] = tops[core]

    for step in range(STEPS):
        for c in waiting:
            c.wait()
        xm, ym = take(r_xm, step, 5), take(r_ym, step, 5)
        xp, yp = take(r_xp, step, 2), take(r_yp, step, 2)
        cx, cy = take(r_cx, step, 1), take(r_cy, step, 1)
        rims_f = (xp[1], yp[1], xm[1], ym[1], cx[1][0], cy[1][0])
        rims_t = (xp[0], yp[0], xm[0], ym[0], cx[0][0], cy[0][0])
        if step == STEPS - 1:
            upper = [
                [[f[..., HALF:] for f in v] if isinstance(v, (list, tuple)) else v[..., HALF:] for v in part]
                for part in (e, h, rims_t, fwd_e, fwd_h, rims_f)
            ]
            send_tops(advance(*upper, inverse[..., HALF:], coef[..., HALF:])[0])
        e, h, fwd_e, fwd_h = advance(e, h, rims_t, fwd_e, fwd_h, rims_f, inverse, coef)
        if step < STEPS - 1:
            put_tangent(step + 1, e, h)
            put_forward(step + 1, fwd_e, fwd_h)
            waiting = send(step + 1, 12 + 6 * step, 0)

    for c in range(3):
        out_e[c] = e[c]
        out_h[c] = h[c]

    def product(distance):
        near, far = split(gathered[distance].reshape(block, 2 * DIRS))[:2]
        return jnp.dot(
            table[lax.rem(j + ny - distance, ny)], jnp.concatenate([near, near, far], 0),
            preferred_element_type=jnp.float32,
        )

    copies = copies[::-1]
    copies[0].wait_recv()
    sums = product(0)
    for d in range(1, ny):
        copies[2 * d - 1].wait_recv()
        copies[2 * d].wait_recv()
        sums = sums + product(d)
    cosines, sines = sums[:rows], sums[rows:]
    real = cosines * turn_c - sines * turn_s
    imag = sines * turn_c + cosines * turn_s
    real = real + pltpu.roll(real, DIRS, 1)
    imag = imag + pltpu.roll(imag, DIRS, 1)
    both = jnp.where(lower, real, -imag)
    partial[...] = both.reshape(nx, own, 2 * DIRS)
    out = []
    for d in sorted(range(1, nx), key=lambda d: -min(d, nx - d)):
        to = lax.rem(i + d, nx)
        c = copy(partial.at[to], arrived.at[d], p_send.at[d], p_recv.at[d], (to, j))
        c.start()
        out.append((d, c))
    totals = [partial[i], None]
    for d, c in out[::-1]:
        c.wait_recv()
        totals[d % 2] = arrived[d] if totals[d % 2] is None else totals[d % 2] + arrived[d]
    out_s[:, :2 * DIRS] = jnp.where(core == 0, totals[0], totals[1])
    out_s[:, 2 * DIRS:] = jnp.where(core == 0, totals[1], totals[0])
    for c in copies + [c for _, c in out]:
        c.wait_send()


def hand_over(from_e, from_h, from_s, to_e, to_h, to_s, sem):
    copies = [
        pltpu.make_async_copy(src, dst, sem.at[k])
        for k, (src, dst) in enumerate(((from_e, to_e), (from_h, to_h), (from_s, to_s)))
    ]
    for c in copies:
        c.start()
    for c in copies:
        c.wait()


def local(nx, ny, te, th, fe, fh, classes, material, permittivity, contrast, orders):
    wx, wy = te.shape[1], te.shape[2]
    own = orders.shape[0] // (nx * ny)
    rows = nx * own
    f32 = jnp.float32
    vmem = pl.BlockSpec(memory_space=pltpu.VMEM)
    args = (
        te, th, jnp.transpose(fe, (0, 1, 3, 2)), jnp.transpose(fh, (0, 1, 3, 2)),
        jnp.transpose(classes, (0, 2, 1)), jnp.transpose(material, (0, 2, 1)),
        permittivity, contrast, jnp.transpose(orders),
    )

    def two(*shape):
        return [pltpu.VMEM((STEPS,) + shape, f32)] * 2

    hbm = pl.BlockSpec(memory_space=pltpu.HBM)
    out_shape = (
        jax.ShapeDtypeStruct(te.shape, f32),
        jax.ShapeDtypeStruct(th.shape, f32),
        jax.ShapeDtypeStruct((own, 4 * DIRS), f32),
    )
    args = tuple(pltpu.with_memory_space_constraint(v, pltpu.HBM) for v in args)
    results = pl.pallas_call(
        functools.partial(kernel, nx, ny, own),
        out_shape=out_shape,
        in_specs=[hbm] * 9,
        out_specs=(vmem, vmem, vmem),
        scratch_shapes=[
            *two(15, wy, HALF), *two(6, wy, HALF), *two(15, wx, HALF), *two(6, wx, HALF),
            *two(3, 1, HALF), *two(3, 1, HALF),
            pltpu.VMEM((2, wx // 2 * wy, 2 * DIRS), f32),
            pltpu.VMEM((ny, 2, wx // 2 * wy, 2 * DIRS), f32),
            *[pltpu.VMEM((nx, own, 2 * DIRS), f32)] * 2,
            pltpu.VMEM((ny, 2 * rows, 3 * wx * wy), jnp.bfloat16),
            pltpu.SemaphoreType.DMA((6 * STEPS + 6,)), pltpu.SemaphoreType.DMA((6 * STEPS + 6,)),
            pltpu.SemaphoreType.DMA((2 * ny,)), pltpu.SemaphoreType.DMA((2 * ny,)),
            pltpu.SemaphoreType.DMA((nx,)), pltpu.SemaphoreType.DMA((nx,)),
            *[pltpu.VMEM(v.shape, v.dtype) for v in args[:6]],
            *[pltpu.SMEM(v.shape, v.dtype) for v in args[6:8]],
            pltpu.VMEM(args[8].shape, args[8].dtype),
            pltpu.SemaphoreType.DMA((13,)),
        ],
        compiler_params=pltpu.CompilerParams(
            collective_id=0, has_side_effects=True, vmem_limit_bytes=48 * 1024 * 1024
        ),
        name="slab",
    )(*args)
    return pl.pallas_call(
        hand_over,
        out_shape=out_shape,
        in_specs=[vmem] * 3,
        out_specs=(hbm, hbm, hbm),
        scratch_shapes=[pltpu.SemaphoreType.DMA((3,))],
        compiler_params=pltpu.CompilerParams(vmem_limit_bytes=16 * 1024 * 1024),
        name="hand_over",
    )(*results)


def solution(mesh):
    in_specs = (
        P(None, "gx", "gy", None),
        P(None, "gx", "gy", None),
        P(None, "gx", "gy", None),
        P(None, "gx", "gy", None),
        P("gx", "gy", None),
        P("gx", "gy", None),
        P(),
        P(),
        P(),
    )
    out_specs = (P(None, "gx", "gy", None), P(None, "gx", "gy", None), P(("gx", "gy"), None))
    body = functools.partial(local, mesh.shape["gx"], mesh.shape["gy"])
    return jax.shard_map(body, mesh=mesh, in_specs=in_specs, out_specs=out_specs, check_vma=False)
```

```python
import functools
import math

import jax
import jax.numpy as jnp
from jax import lax
from jax.experimental import pallas as pl
from jax.experimental.pallas import tpu as pltpu
from jax.sharding import PartitionSpec as P

DIRS = 64
STEPS = 2
LAYERS = 4
WIDE = LAYERS * DIRS
HALF = WIDE // 2
time_step = 0.5


REACH = 2
PAD = 8
GROUP = 32


def lanes_of(shape):
    return lax.broadcasted_iota(jnp.int32, shape, len(shape) - 1)


def sublanes_of(shape):
    return lax.broadcasted_iota(jnp.int32, shape, len(shape) - 2)


def next_y(f):
    return pltpu.roll(f, f.shape[0] - 1, 0)


def prev_y(f):
    return pltpu.roll(f, 1, 0)


def next_z(f):
    wide = f.shape[-1]
    return jnp.where(lanes_of(f.shape) < wide - DIRS, pltpu.roll(f, wide - DIRS, 1), 0.0)


def prev_z(f):
    return jnp.where(lanes_of(f.shape) >= DIRS, pltpu.roll(f, DIRS, 1), 0.0)


def curl_f(f, x_next, ny, nz):
    fx, fy, fz = f
    return (
        (ny(fz) - fz) - (nz(fy) - fy),
        (nz(fx) - fx) - (x_next(2) - fz),
        (x_next(1) - fy) - (ny(fx) - fx),
    )


def curl_b(f, x_prev, py, pz):
    fx, fy, fz = f
    return (
        (fz - py(fz)) - (fy - pz(fy)),
        (fx - pz(fx)) - (fz - x_prev(2)),
        (fy - x_prev(1)) - (fx - py(fx)),
    )


def sine(turn):
    u = turn * (2.0 * math.pi)
    s = u * u
    poly = -1.0 / 39916800.0
    for c in (1.0 / 362880.0, -1.0 / 5040.0, 1.0 / 120.0, -1.0 / 6.0):
        poly = poly * s + c
    return u + u * (s * poly)


def split(v):
    parts = []
    for _ in range(3):
        parts.append(v.astype(jnp.bfloat16))
        v = v - parts[-1].astype(jnp.float32)
    return parts


def stacked(v):
    parts = [part.astype(jnp.float32) for part in split(v)]
    return parts


def selected(v, choice):
    n = v.shape[0]
    parts = stacked(v)
    if 3 * n % 16:
        parts.append(jnp.zeros_like(v))
    got = jnp.dot(
        jnp.concatenate(parts, 0).astype(jnp.bfloat16), choice, preferred_element_type=jnp.float32
    )
    return got[:n] + got[n:2 * n] + got[2 * n:3 * n]


def ones_where(hit):
    return hit.astype(jnp.float32).astype(jnp.bfloat16)


def kernel(
    nx, ny, own,
    te_at, th_at, fe_at, fh_at, classes_at, material_at, permittivity_at, contrast_at, orders_at,
    out_e, out_h, out_s,
    te, th, source_1, source_2, inverse, block_out, block_in, strip_out, strip_in,
    tops, gathered, partial, arrived, table,
    rim_send, rim_recv, f_send, f_recv, g_send, g_recv, p_send, p_recv,
    fe, fh, classes, material, permittivity, contrast, orders, load,
):
    wx, wy = te_at.shape[1], te_at.shape[2]
    rows_y = te.shape[2]
    inside = (pl.ds(REACH, wx), pl.ds(0, wy))
    small = [
        pltpu.make_async_copy(src, dst, load.at[6 + k])
        for k, (src, dst) in enumerate((
            (fe_at, fe), (fh_at, fh), (classes_at, classes), (material_at, material),
            (permittivity_at, permittivity), (contrast_at, contrast), (orders_at, orders),
        ))
    ]
    large = [
        pltpu.make_async_copy(src.at[c], dst.at[(c, *inside)], load.at[2 * c + k])
        for c in range(3) for k, (src, dst) in enumerate(((te_at, te), (th_at, th)))
    ]
    for c in small[:4] + large + small[4:]:
        c.start()
    i, j = lax.axis_index("gx"), lax.axis_index("gy")
    core = lax.rem(i, 2)
    mate = i + 1 - 2 * core
    beyond = lax.rem(i + nx - 1 + 2 * core, nx)

    def at(dx, dy):
        return (lax.rem(i + nx + dx, nx), lax.rem(j + ny + dy, ny))

    line = [(lax.rem(i + d, nx), j) for d in range(1, nx)]
    sheet = [(mate, j)] + [(k, lax.rem(j + d, ny)) for d in range(1, ny) for k in (i, mate)]
    peers = line + sheet[1:] + [(beyond, at(0, -1)[1]), (beyond, at(0, 1)[1])]
    barrier = pltpu.get_barrier_semaphore()
    for peer in peers:
        pl.semaphore_signal(barrier, inc=1, device_id=peer, device_id_type=pl.DeviceIdType.MESH)

    def copy(src, dst, send, recv, device):
        return pltpu.make_async_remote_copy(
            src_ref=src, dst_ref=dst, send_sem=send, recv_sem=recv,
            device_id=device, device_id_type=pl.DeviceIdType.MESH,
        )

    spots = wx * wy
    lane = lax.broadcasted_iota(jnp.int32, (1, 128), 1)
    group, in_group = lane // GROUP, lane % GROUP
    k = in_group % 4
    from_lane = group * spots + (in_group // 4) * wy + jnp.where(k < 2, k, wy - 4 + k)
    strip_choice = ones_where(lax.broadcasted_iota(jnp.int32, (4 * spots, 128), 0) == from_lane)
    for c in small[:4]:
        c.wait()
    for x in range(wx):
        cells = slice(x * wy, (x + 1) * wy)
        for c in range(3):
            block_out[4 * c:4 * c + 4, cells] = fe[c, x]
            block_out[12 + 4 * c:16 + 4 * c, cells] = fh[c, x]
        block_out[24:28, cells] = classes[x].astype(jnp.float32)
        block_out[28:32, cells] = material[x].astype(jnp.float32)
    mine = block_out[...]
    strip_out[...] = selected(jnp.concatenate([mine[8 * g:8 * g + 8] for g in range(4)], 1), strip_choice)

    pl.semaphore_wait(barrier, len(peers))
    strips = [(0, -1), (0, 1), (-1, -1), (-1, 1), (1, -1), (1, 1)]
    f_copies = []
    for n, (dx, dy) in enumerate(strips):
        f_copies.append(copy(strip_out, strip_in.at[n], f_send.at[n], f_recv.at[n], at(-dx, -dy)))
    for n, dx in enumerate((-1, 1)):
        f_copies.append(copy(block_out, block_in.at[n], f_send.at[6 + n], f_recv.at[6 + n], at(-dx, 0)))
    for c in f_copies[2:] + f_copies[:2]:
        c.start()

    def span(d, size, before, after, n):
        if d > 0:
            return pl.ds(before[0] + size - n, n), pl.ds(before[1] - n, n)
        if d < 0:
            return pl.ds(before[0], n), pl.ds(after, n)
        return pl.ds(before[0], size), pl.ds(before[0], size)

    r_copies = []
    for c in large:
        c.wait()
    for dx, dy in ((1, 1), (1, -1), (-1, 1), (-1, -1), (0, 1), (0, -1), (1, 0), (-1, 0)):
        for field in range(2):
            if field == 1 and dx < 0 and dy < 0:
                continue
            one = dx * dy > 0
            px = 1 if one or (field == 1 and dx < 0) else REACH
            py = 1 if one or (field == 1 and dy < 0) else REACH
            sx, tx = span(dx, wx, (REACH, REACH), REACH + wx, px)
            sy, ty = span(dy, wy, (0, rows_y), wy, py)
            f = (te, th)[field]
            n = len(r_copies)
            c = copy(f.at[:, sx, sy, :], f.at[:, tx, ty, :], rim_send.at[n], rim_recv.at[n], at(dx, dy))
            c.start()
            r_copies.append(c)

    for c in small[4:]:
        c.wait()
    rows, half = nx * own, wx // 2
    block = 2 * half * wy
    cells = ny * block
    count = orders.shape[1]
    row = lax.broadcasted_iota(jnp.int32, (rows, 1), 0)
    target = (row // own) * (ny * own) + j * own + row % own
    pick = ones_where(lax.broadcasted_iota(jnp.int32, (rows, count), 1) == target)
    pair = lax.dot_general(
        pick, orders[...].astype(jnp.float32).astype(jnp.bfloat16),
        (((1,), (1,)), ((), ())), preferred_element_type=jnp.float32,
    )
    cell = lax.broadcasted_iota(jnp.int32, (1, cells), 1)
    all_x, all_y = nx * wx, ny * wy
    all_cells = float(all_x * all_y)
    x_in = ((cell // (half * wy)) % 2) * wx + 2 * ((cell // wy) % half)
    x_at = (((i - core) * wx + x_in) * all_y).astype(jnp.float32)
    y_at = (((cell // block) * wy + cell % wy) * all_x).astype(jnp.float32)

    def waves(index):
        index = index - all_cells * jnp.round(index * (1.0 / all_cells))
        turn = index * (1.0 / all_cells)
        cosine = sine(0.25 - jnp.abs(turn))
        sines = sine(jnp.where(turn > 0.25, 0.5 - turn, jnp.where(turn < -0.25, -0.5 - turn, turn)))
        return cosine, sines

    for place, value in zip((0, rows), waves(pair[:, 0:1] * x_at + pair[:, 1:2] * y_at)):
        near, far = split(value)[:2]
        for k in range(ny):
            for q, part in enumerate((near, far, near)):
                table[k, place:place + rows, q * block:(q + 1) * block] = part[:, k * block:(k + 1) * block]
    lower = lax.broadcasted_iota(jnp.int32, (rows, 2 * DIRS), 1) < DIRS
    turn_c, turn_s = waves(jnp.where(lower, 0.0, pair[:, 0:1] * float(all_y)))
    scale = 1.0 / math.sqrt(all_x * all_y)
    turn_c, turn_s = turn_c * scale, turn_s * scale

    span_l = (wx + 2 * REACH) * GROUP
    spot = lax.broadcasted_iota(jnp.int32, (1, span_l), 1)
    p = spot % GROUP
    x = spot // GROUP - REACH
    y = jnp.where(p < wy + REACH, p, p - rows_y)
    valid = (p < wy + REACH) | ((p >= rows_y - REACH) & (p < rows_y))
    side_x = jnp.where(x < 0, -1, jnp.where(x >= wx, 1, 0))
    side_y = jnp.where(y < 0, -1, jnp.where(y >= wy, 1, 0))
    lx, ly = x - side_x * wx, y - side_y * wy
    whole = jnp.where(side_x == 0, 0, jnp.where(side_x < 0, 1, 2)) * spots + lx * wy + ly
    which = jnp.where(side_x == 0, 0, jnp.where(side_x < 0, 2, 4)) + jnp.where(side_y > 0, 1, 0)
    strip = 3 * spots + which * GROUP + lx * 4 + jnp.where(ly < 2, ly, ly - (wy - 4))
    origin = jnp.where(valid, jnp.where(side_y == 0, whole, strip), -1)
    choice = ones_where(lax.broadcasted_iota(jnp.int32, (3 * spots + 256, span_l), 0) == origin)
    spread = ones_where(
        lax.broadcasted_iota(jnp.int32, (32, WIDE), 0) % 8 == lax.broadcasted_iota(jnp.int32, (32, WIDE), 1) // DIRS
    )

    for c in f_copies:
        c.wait()
    gathered_strips = []
    for first in (0, 4):
        groups = []
        for g in range(4):
            got = None
            for n in range(first, min(first + 4, 6)):
                v = strip_in[n]
                shift = (GROUP * (n - first - g)) % 128
                v = pltpu.roll(v, shift, 1) if shift else v
                got = v if got is None else jnp.where(lane // GROUP == n - first, v, got)
            groups.append(got)
        gathered_strips.append(jnp.concatenate(groups, 0))
    around = selected(
        jnp.concatenate([mine, block_in[0], block_in[1], *gathered_strips], 1), choice
    )
    pairs = [around[8 * g:8 * g + 8] for g in range(4)]
    fields = [f for v in pairs for f in (v, pltpu.roll(v, 4, 0))]
    f_e, f_h, kind, matter = fields[:3], fields[3:6], fields[6], fields[7]
    layer = sublanes_of((8, span_l))

    def f_next_x(f):
        return pltpu.roll(f, span_l - GROUP, 1)

    def f_prev_x(f):
        return pltpu.roll(f, GROUP, 1)

    def f_next_y(f):
        return jnp.where(p == rows_y - 1, pltpu.roll(f, rows_y - 1, 1), pltpu.roll(f, span_l - 1, 1))

    def f_prev_y(f):
        return jnp.where(p == 0, pltpu.roll(f, span_l - rows_y + 1, 1), pltpu.roll(f, 1, 1))

    def f_next_z(f):
        return jnp.where(layer < LAYERS - 1, pltpu.roll(f, 7, 0), 0.0)

    def f_prev_z(f):
        return jnp.where(layer >= 1, pltpu.roll(f, 1, 0), 0.0)

    eps = jnp.full((8, span_l), permittivity[0])
    slope = jnp.full((8, span_l), contrast[0])
    for k in range(1, permittivity.shape[0]):
        eps = jnp.where(matter == float(k), permittivity[k], eps)
        slope = jnp.where(matter == float(k), contrast[k], slope)
    ratio = time_step / eps
    coef = time_step * slope / (eps * eps)
    sources = []
    for step in range(STEPS):
        curl = curl_f(f_e, lambda c: f_next_x(f_e[c]), f_next_y, f_next_z)
        f_h = [f_h[c] - time_step * curl[c] for c in range(3)]
        curl = curl_b(f_h, lambda c: f_prev_x(f_h[c]), f_prev_y, f_prev_z)
        sources.append([coef * curl[c] for c in range(3)])
        f_e = [f_e[c] + ratio * curl[c] for c in range(3)]

    def wide(v, exact=True):
        v = jnp.where(layer < LAYERS, v, 0.0)
        zero = jnp.zeros_like(v)
        parts = stacked(v) + [zero] if exact else [v, zero, zero, zero]
        return lax.dot_general(
            jnp.concatenate(parts, 0).astype(jnp.bfloat16), spread, (((0,), (0,)), ((), ())),
            preferred_element_type=jnp.float32,
        )

    hot = wide(kind, False) == (lax.broadcasted_iota(jnp.int32, (1, WIDE), 1) % DIRS).astype(jnp.float32)
    v = wide(ratio)
    for x in range(1, wx + 3):
        inverse[x] = v[GROUP * x:GROUP * x + rows_y]
    for c in range(3):
        v = jnp.where(hot, wide(sources[0][c]), 0.0)
        for x in range(1, wx + 3):
            source_1[c, x] = v[GROUP * x:GROUP * x + rows_y]
        v = jnp.where(hot, wide(sources[1][c]), 0.0)
        for x in range(wx):
            source_2[c, x] = v[GROUP * (x + REACH):GROUP * (x + REACH) + wy]

    for c in r_copies:
        c.wait_send()
    arrivals = list(r_copies)
    for c in arrivals:
        c.wait_recv()

    def plane(f, x, lanes=slice(None)):
        return [f[c, x, :, lanes] for c in range(3)]

    low, high = slice(0, HALF), slice(HALF, WIDE)

    def h_first(x):
        f, g = plane(te, x), plane(th, x)
        curl = curl_f(f, lambda c: te[c, x + 1], next_y, next_z)
        for c in range(3):
            th[c, x] = g[c] - time_step * curl[c]

    def e_first(x, lanes):
        f, g = plane(te, x, lanes), plane(th, x, lanes)
        below = [th[c, x, :, :] for c in range(3)]

        def pz(v):
            if lanes is low:
                return prev_z(v)
            n = [k for k in range(3) if g[k] is v][0]
            return prev_z(below[n])[:, HALF:]

        curl = curl_b(g, lambda c: th[c, x - 1, :, lanes], prev_y, pz)
        ratio = inverse[x, :, lanes]
        for c in range(3):
            te[c, x, :, lanes] = f[c] + ratio * curl[c] - source_1[c, x, :, lanes]

    def h_second(x, lanes):
        f, g = plane(te, x, lanes), plane(th, x, lanes)
        above = [te[c, x, :, :] for c in range(3)]

        def nz(v):
            if lanes is high:
                return next_z(v)
            n = [k for k in range(3) if f[k] is v][0]
            return next_z(above[n])[:, :HALF]

        curl = curl_f(f, lambda c: te[c, x + 1, :, lanes], next_y, nz)
        for c in range(3):
            th[c, x, :, lanes] = g[c] - time_step * curl[c]

    def e_second(x, lanes, comps):
        g = plane(th, x, lanes)
        curl = curl_b(g, lambda c: th[c, x - 1, :, lanes], prev_y, prev_z)
        return [
            te[c, x, :wy, lanes] + inverse[x, :wy, lanes] * curl[c][:wy] - source_2[c, x - REACH, :, lanes]
            for c in range(comps)
        ]

    h_first(0)
    h_first(1)
    e_first(1, high)
    h_first(2)
    e_first(2, high)
    h_second(1, high)

    def top_pair(u, carry):
        got = []
        for n in range(2):
            x = 2 * u + 3 + n
            h_first(x)
            e_first(x, high)
            h_second(x - 1, high)
            got.append(e_second(x - 1, high, 2))
        for q in range(2):
            tops[q, pl.ds(pl.multiple_of(u * wy, wy), wy)] = jnp.where(
                lanes_of(got[0][q].shape) < DIRS, pltpu.roll(got[0][q], DIRS, 1), got[1][q]
            )
        return carry

    lax.fori_loop(0, half, top_pair, 0)

    copies = []
    for k in reversed(range(len(sheet))):
        to = mate if k % 2 == 0 else i
        q = 1 - core if k % 2 == 0 else core
        c = copy(tops.at[q], gathered.at[(k + 1) // 2, core], g_send.at[k], g_recv.at[k], (to, sheet[k][1]))
        c.start()
        copies.append(c)
    gathered[0, core] = tops[core]

    e_first(1, low)
    e_first(2, low)
    h_second(1, low)

    def rest(u, carry):
        x = u + 3
        e_first(x, low)
        h_second(x - 1, low)
        new = e_second(x - 1, slice(None), 3)
        for c in range(3):
            out_e[c, u] = new[c]
            out_h[c, u] = th[c, x - 1, :wy]
        return carry

    lax.fori_loop(0, wx, rest, 0)

    def product(distance):
        near, far = split(gathered[distance].reshape(block, 2 * DIRS))[:2]
        return jnp.dot(
            table[lax.rem(j + ny - distance, ny)], jnp.concatenate([near, near, far], 0),
            preferred_element_type=jnp.float32,
        )

    copies = copies[::-1]
    copies[0].wait_recv()
    sums = product(0)
    for d in range(1, ny):
        copies[2 * d - 1].wait_recv()
        copies[2 * d].wait_recv()
        sums = sums + product(d)
    cosines, sines = sums[:rows], sums[rows:]
    real = cosines * turn_c - sines * turn_s
    imag = sines * turn_c + cosines * turn_s
    real = real + pltpu.roll(real, DIRS, 1)
    imag = imag + pltpu.roll(imag, DIRS, 1)
    both = jnp.where(lower, real, -imag)
    partial[...] = both.reshape(nx, own, 2 * DIRS)
    out = []
    for d in sorted(range(1, nx), key=lambda d: -min(d, nx - d)):
        to = lax.rem(i + d, nx)
        c = copy(partial.at[to], arrived.at[d], p_send.at[d], p_recv.at[d], (to, j))
        c.start()
        out.append((d, c))
    totals = [partial[i], None]
    for d, c in out[::-1]:
        c.wait_recv()
        totals[d % 2] = arrived[d] if totals[d % 2] is None else totals[d % 2] + arrived[d]
    out_s[:, :2 * DIRS] = jnp.where(core == 0, totals[0], totals[1])
    out_s[:, 2 * DIRS:] = jnp.where(core == 0, totals[1], totals[0])
    for c in copies + [c for _, c in out]:
        c.wait_send()


def hand_over(from_e, from_h, from_s, to_e, to_h, to_s, sem):
    copies = [
        pltpu.make_async_copy(src, dst, sem.at[k])
        for k, (src, dst) in enumerate(((from_e, to_e), (from_h, to_h), (from_s, to_s)))
    ]
    for c in copies:
        c.start()
    for c in copies:
        c.wait()


def local(nx, ny, te, th, fe, fh, classes, material, permittivity, contrast, orders):
    wx, wy = te.shape[1], te.shape[2]
    own = orders.shape[0] // (nx * ny)
    rows = nx * own
    f32 = jnp.float32
    vmem = pl.BlockSpec(memory_space=pltpu.VMEM)
    hbm = pl.BlockSpec(memory_space=pltpu.HBM)
    args = (
        te, th, jnp.transpose(fe, (0, 1, 3, 2)), jnp.transpose(fh, (0, 1, 3, 2)),
        jnp.transpose(classes, (0, 2, 1)), jnp.transpose(material, (0, 2, 1)),
        permittivity, contrast, jnp.transpose(orders),
    )
    args = tuple(pltpu.with_memory_space_constraint(v, pltpu.HBM) for v in args)
    out_shape = (
        jax.ShapeDtypeStruct(te.shape, f32),
        jax.ShapeDtypeStruct(th.shape, f32),
        jax.ShapeDtypeStruct((own, 4 * DIRS), f32),
    )
    wide_x, wide_y = wx + 2 * REACH, wy + PAD

    def pair_of(n):
        return [pltpu.SemaphoreType.DMA((n,))] * 2

    results = pl.pallas_call(
        functools.partial(kernel, nx, ny, own),
        out_shape=out_shape,
        in_specs=[hbm] * 9,
        out_specs=(vmem, vmem, vmem),
        scratch_shapes=[
            *[pltpu.VMEM((3, wide_x, wide_y, WIDE), f32)] * 3,
            pltpu.VMEM((3, wx, wy, WIDE), f32),
            pltpu.VMEM((wide_x, wide_y, WIDE), f32),
            pltpu.VMEM((32, wx * wy), f32), pltpu.VMEM((2, 32, wx * wy), f32),
            pltpu.VMEM((8, 128), f32), pltpu.VMEM((6, 8, 128), f32),
            pltpu.VMEM((2, wx // 2 * wy, 2 * DIRS), f32),
            pltpu.VMEM((ny, 2, wx // 2 * wy, 2 * DIRS), f32),
            *[pltpu.VMEM((nx, own, 2 * DIRS), f32)] * 2,
            pltpu.VMEM((ny, 2 * rows, 3 * wx * wy), jnp.bfloat16),
            *pair_of(16), *pair_of(8), *pair_of(2 * ny), *pair_of(nx),
            *[pltpu.VMEM(v.shape, v.dtype) for v in args[2:6]],
            *[pltpu.SMEM(v.shape, v.dtype) for v in args[6:8]],
            pltpu.VMEM(args[8].shape, args[8].dtype),
            pltpu.SemaphoreType.DMA((13,)),
        ],
        compiler_params=pltpu.CompilerParams(
            collective_id=0, has_side_effects=True, vmem_limit_bytes=48 * 1024 * 1024
        ),
        name="slab",
    )(*args)
    return pl.pallas_call(
        hand_over,
        out_shape=out_shape,
        in_specs=[vmem] * 3,
        out_specs=(hbm, hbm, hbm),
        scratch_shapes=[pltpu.SemaphoreType.DMA((3,))],
        compiler_params=pltpu.CompilerParams(vmem_limit_bytes=16 * 1024 * 1024),
        name="hand_over",
    )(*results)


def solution(mesh):
    in_specs = (
        P(None, "gx", "gy", None),
        P(None, "gx", "gy", None),
        P(None, "gx", "gy", None),
        P(None, "gx", "gy", None),
        P("gx", "gy", None),
        P("gx", "gy", None),
        P(),
        P(),
        P(),
    )
    out_specs = (P(None, "gx", "gy", None), P(None, "gx", "gy", None), P(("gx", "gy"), None))
    body = functools.partial(local, mesh.shape["gx"], mesh.shape["gy"])
    return jax.shard_map(body, mesh=mesh, in_specs=in_specs, out_specs=out_specs, check_vma=False)
```

```python
import functools
import math

import jax
import jax.numpy as jnp
from jax import lax
from jax.experimental import pallas as pl
from jax.experimental.pallas import tpu as pltpu
from jax.sharding import PartitionSpec as P

DIRS = 64
STEPS = 2
LAYERS = 4
WIDE = LAYERS * DIRS
HALF = WIDE // 2
time_step = 0.5


REACH = 2
PAD = 8
GROUP = 32


def lanes_of(shape):
    return lax.broadcasted_iota(jnp.int32, shape, len(shape) - 1)


def sublanes_of(shape):
    return lax.broadcasted_iota(jnp.int32, shape, len(shape) - 2)


def next_y(f):
    return pltpu.roll(f, f.shape[0] - 1, 0)


def prev_y(f):
    return pltpu.roll(f, 1, 0)


def next_z(f):
    wide = f.shape[-1]
    return jnp.where(lanes_of(f.shape) < wide - DIRS, pltpu.roll(f, wide - DIRS, 1), 0.0)


def prev_z(f):
    return jnp.where(lanes_of(f.shape) >= DIRS, pltpu.roll(f, DIRS, 1), 0.0)


def curl_f(f, x_next, ny, nz):
    fx, fy, fz = f
    return (
        (ny(fz) - fz) - (nz(fy) - fy),
        (nz(fx) - fx) - (x_next(2) - fz),
        (x_next(1) - fy) - (ny(fx) - fx),
    )


def curl_b(f, x_prev, py, pz):
    fx, fy, fz = f
    return (
        (fz - py(fz)) - (fy - pz(fy)),
        (fx - pz(fx)) - (fz - x_prev(2)),
        (fy - x_prev(1)) - (fx - py(fx)),
    )


def sine(turn):
    u = turn * (2.0 * math.pi)
    s = u * u
    poly = -1.0 / 39916800.0
    for c in (1.0 / 362880.0, -1.0 / 5040.0, 1.0 / 120.0, -1.0 / 6.0):
        poly = poly * s + c
    return u + u * (s * poly)


def split(v):
    parts = []
    for _ in range(3):
        parts.append(v.astype(jnp.bfloat16))
        v = v - parts[-1].astype(jnp.float32)
    return parts


def stacked(v):
    parts = [part.astype(jnp.float32) for part in split(v)]
    return parts


def selected(v, choice):
    n = v.shape[0]
    parts = stacked(v)
    if 3 * n % 16:
        parts.append(jnp.zeros_like(v))
    got = jnp.dot(
        jnp.concatenate(parts, 0).astype(jnp.bfloat16), choice, preferred_element_type=jnp.float32
    )
    return got[:n] + got[n:2 * n] + got[2 * n:3 * n]


def ones_where(hit):
    return hit.astype(jnp.float32).astype(jnp.bfloat16)


def paired(n, k, size):
    out, bit = 0, 1
    while bit < size:
        out = out + bit * ((n // bit + k // bit) % 2)
        bit *= 2
    return out


def kernel(
    nx, ny, own,
    te_at, th_at, fe_at, fh_at, classes_at, material_at, permittivity_at, contrast_at, orders_at,
    out_e, out_h, out_s,
    te, th, source_1, source_2, inverse, block_out, block_in, strip_out, strip_in,
    tops, gathered, partial, arrived, table,
    rim_send, rim_recv, f_send, f_recv, g_send, g_recv, p_send, p_recv,
    fe, fh, classes, material, permittivity, contrast, orders, load,
):
    wx, wy = te_at.shape[1], te_at.shape[2]
    rows_y = te.shape[2]
    inside = (pl.ds(REACH, wx), pl.ds(0, wy))
    i, j = lax.axis_index("gx"), lax.axis_index("gy")
    core = lax.rem(i, 2)
    mate = i + 1 - 2 * core
    beyond = lax.rem(i + nx - 1 + 2 * core, nx)

    def at(dx, dy):
        return (lax.rem(i + nx + dx, nx), lax.rem(j + ny + dy, ny))

    line = [(paired(i, k, nx), j) for k in range(1, nx)]
    sheet = [(mate, j)] + [(n, paired(j, k, ny)) for k in range(1, ny) for n in (i, mate)]
    left, right = at(0, -1)[1], at(0, 1)[1]
    peers = [(beyond, left), (beyond, right), (beyond, j)] + sheet[1:] + line
    barrier = pltpu.get_barrier_semaphore()
    for peer in peers:
        pl.semaphore_signal(barrier, inc=1, device_id=peer, device_id_type=pl.DeviceIdType.MESH)

    def copy(src, dst, send, recv, device):
        return pltpu.make_async_remote_copy(
            src_ref=src, dst_ref=dst, send_sem=send, recv_sem=recv,
            device_id=device, device_id_type=pl.DeviceIdType.MESH,
        )

    small = [
        pltpu.make_async_copy(src, dst, load.at[6 + k])
        for k, (src, dst) in enumerate((
            (fe_at, fe), (fh_at, fh), (classes_at, classes), (material_at, material),
            (permittivity_at, permittivity), (contrast_at, contrast), (orders_at, orders),
        ))
    ]
    large = [
        pltpu.make_async_copy(src.at[c], dst.at[(c, *inside)], load.at[2 * c + k])
        for c in range(3) for k, (src, dst) in enumerate(((te_at, te), (th_at, th)))
    ]
    for c in small[:4] + large + small[4:]:
        c.start()

    spots = wx * wy
    lane = lax.broadcasted_iota(jnp.int32, (1, 128), 1)
    group, in_group = lane // GROUP, lane % GROUP
    k = in_group % 4
    from_lane = group * spots + (in_group // 4) * wy + jnp.where(k < 2, k, wy - 4 + k)
    strip_choice = ones_where(lax.broadcasted_iota(jnp.int32, (4 * spots, 128), 0) == from_lane)
    for c in small[:4]:
        c.wait()
    for x in range(wx):
        cells = slice(x * wy, (x + 1) * wy)
        for c in range(3):
            block_out[4 * c:4 * c + 4, cells] = fe[c, x]
            block_out[12 + 4 * c:16 + 4 * c, cells] = fh[c, x]
        block_out[24:28, cells] = classes[x].astype(jnp.float32)
        block_out[28:32, cells] = material[x].astype(jnp.float32)
    mine = block_out[...]
    strip_out[...] = selected(jnp.concatenate([mine[8 * g:8 * g + 8] for g in range(4)], 1), strip_choice)

    pl.semaphore_wait(barrier, len(peers))
    strips = [(0, -1), (0, 1), (-1, -1), (-1, 1), (1, -1), (1, 1)]
    f_copies = []
    for n, (dx, dy) in enumerate(strips):
        f_copies.append(copy(strip_out, strip_in.at[n], f_send.at[n], f_recv.at[n], at(-dx, -dy)))
    for n, dx in enumerate((-1, 1)):
        f_copies.append(copy(block_out, block_in.at[n], f_send.at[6 + n], f_recv.at[6 + n], at(-dx, 0)))
    for c in f_copies[2:] + f_copies[:2]:
        c.start()

    def span(d, size, before, after, n):
        if d > 0:
            return pl.ds(before[0] + size - n, n), pl.ds(before[1] - n, n)
        if d < 0:
            return pl.ds(before[0], n), pl.ds(after, n)
        return pl.ds(before[0], size), pl.ds(before[0], size)

    r_copies = []
    for c in large:
        c.wait()
    for dx, dy in ((1, 1), (1, -1), (-1, 1), (-1, -1), (0, 1), (0, -1), (1, 0), (-1, 0)):
        for field in range(2):
            if field == 1 and dx < 0 and dy < 0:
                continue
            one = dx * dy > 0
            px = 1 if one or (field == 1 and dx < 0) else REACH
            py = 1 if one or (field == 1 and dy < 0) else REACH
            sx, tx = span(dx, wx, (REACH, REACH), REACH + wx, px)
            sy, ty = span(dy, wy, (0, rows_y), wy, py)
            f = (te, th)[field]
            n = len(r_copies)
            c = copy(f.at[:, sx, sy, :], f.at[:, tx, ty, :], rim_send.at[n], rim_recv.at[n], at(dx, dy))
            c.start()
            r_copies.append(c)

    for c in small[4:]:
        c.wait()
    rows, half = nx * own, wx // 2
    block = 2 * half * wy
    cells = ny * block
    count = orders.shape[1]
    row = lax.broadcasted_iota(jnp.int32, (rows, 1), 0)
    target = paired(i, nx - 1 - row // own, nx) * (ny * own) + j * own + row % own
    pick = ones_where(lax.broadcasted_iota(jnp.int32, (rows, count), 1) == target)
    pair = lax.dot_general(
        pick, orders[...].astype(jnp.float32).astype(jnp.bfloat16),
        (((1,), (1,)), ((), ())), preferred_element_type=jnp.float32,
    )
    cell = lax.broadcasted_iota(jnp.int32, (1, cells), 1)
    all_x, all_y = nx * wx, ny * wy
    all_cells = float(all_x * all_y)
    x_in = ((cell // (half * wy)) % 2) * wx + 2 * ((cell // wy) % half)
    x_at = (((i - core) * wx + x_in) * all_y).astype(jnp.float32)
    y_at = (((cell // block) * wy + cell % wy) * all_x).astype(jnp.float32)

    def waves(index):
        index = index - all_cells * jnp.round(index * (1.0 / all_cells))
        turn = index * (1.0 / all_cells)
        cosine = sine(0.25 - jnp.abs(turn))
        sines = sine(jnp.where(turn > 0.25, 0.5 - turn, jnp.where(turn < -0.25, -0.5 - turn, turn)))
        return cosine, sines

    part_rows = rows // 2
    for sine_rows, value in zip((0, part_rows), waves(pair[:, 0:1] * x_at + pair[:, 1:2] * y_at)):
        near, far = split(value)[:2]
        for k in range(ny):
            for q, part in enumerate((near, far, near)):
                for n in range(2):
                    place = 2 * n * part_rows + sine_rows
                    table[k, place:place + part_rows, q * block:(q + 1) * block] = part[
                        n * part_rows:(n + 1) * part_rows, k * block:(k + 1) * block
                    ]
    lower = lax.broadcasted_iota(jnp.int32, (rows, 2 * DIRS), 1) < DIRS
    turn_c, turn_s = waves(jnp.where(lower, 0.0, pair[:, 0:1] * float(all_y)))
    scale = 1.0 / math.sqrt(all_x * all_y)
    turn_c, turn_s = turn_c * scale, turn_s * scale

    span_l = (wx + 2 * REACH) * GROUP
    spot = lax.broadcasted_iota(jnp.int32, (1, span_l), 1)
    p = spot % GROUP
    x = spot // GROUP - REACH
    y = jnp.where(p < wy + REACH, p, p - rows_y)
    valid = (p < wy + REACH) | ((p >= rows_y - REACH) & (p < rows_y))
    side_x = jnp.where(x < 0, -1, jnp.where(x >= wx, 1, 0))
    side_y = jnp.where(y < 0, -1, jnp.where(y >= wy, 1, 0))
    lx, ly = x - side_x * wx, y - side_y * wy
    whole = jnp.where(side_x == 0, 0, jnp.where(side_x < 0, 1, 2)) * spots + lx * wy + ly
    which = jnp.where(side_x == 0, 0, jnp.where(side_x < 0, 2, 4)) + jnp.where(side_y > 0, 1, 0)
    strip = 3 * spots + which * GROUP + lx * 4 + jnp.where(ly < 2, ly, ly - (wy - 4))
    origin = jnp.where(valid, jnp.where(side_y == 0, whole, strip), -1)
    choice = ones_where(lax.broadcasted_iota(jnp.int32, (3 * spots + 256, span_l), 0) == origin)
    spread = ones_where(
        lax.broadcasted_iota(jnp.int32, (32, WIDE), 0) % 8 == lax.broadcasted_iota(jnp.int32, (32, WIDE), 1) // DIRS
    )

    for c in f_copies:
        c.wait()
    gathered_strips = []
    for first in (0, 4):
        groups = []
        for g in range(4):
            got = None
            for n in range(first, min(first + 4, 6)):
                v = strip_in[n]
                shift = (GROUP * (n - first - g)) % 128
                v = pltpu.roll(v, shift, 1) if shift else v
                got = v if got is None else jnp.where(lane // GROUP == n - first, v, got)
            groups.append(got)
        gathered_strips.append(jnp.concatenate(groups, 0))
    around = selected(
        jnp.concatenate([mine, block_in[0], block_in[1], *gathered_strips], 1), choice
    )
    pairs = [around[8 * g:8 * g + 8] for g in range(4)]
    fields = [f for v in pairs for f in (v, pltpu.roll(v, 4, 0))]
    f_e, f_h, kind, matter = fields[:3], fields[3:6], fields[6], fields[7]
    layer = sublanes_of((8, span_l))

    def f_next_x(f):
        return pltpu.roll(f, span_l - GROUP, 1)

    def f_prev_x(f):
        return pltpu.roll(f, GROUP, 1)

    def f_next_y(f):
        return jnp.where(p == rows_y - 1, pltpu.roll(f, rows_y - 1, 1), pltpu.roll(f, span_l - 1, 1))

    def f_prev_y(f):
        return jnp.where(p == 0, pltpu.roll(f, span_l - rows_y + 1, 1), pltpu.roll(f, 1, 1))

    def f_next_z(f):
        return jnp.where(layer < LAYERS - 1, pltpu.roll(f, 7, 0), 0.0)

    def f_prev_z(f):
        return jnp.where(layer >= 1, pltpu.roll(f, 1, 0), 0.0)

    eps = jnp.full((8, span_l), permittivity[0])
    slope = jnp.full((8, span_l), contrast[0])
    for k in range(1, permittivity.shape[0]):
        eps = jnp.where(matter == float(k), permittivity[k], eps)
        slope = jnp.where(matter == float(k), contrast[k], slope)
    ratio = time_step / eps
    coef = time_step * slope / (eps * eps)
    sources = []
    for step in range(STEPS):
        curl = curl_f(f_e, lambda c: f_next_x(f_e[c]), f_next_y, f_next_z)
        f_h = [f_h[c] - time_step * curl[c] for c in range(3)]
        curl = curl_b(f_h, lambda c: f_prev_x(f_h[c]), f_prev_y, f_prev_z)
        sources.append([coef * curl[c] for c in range(3)])
        f_e = [f_e[c] + ratio * curl[c] for c in range(3)]

    def wide(v, exact=True):
        v = jnp.where(layer < LAYERS, v, 0.0)
        zero = jnp.zeros_like(v)
        parts = stacked(v) + [zero] if exact else [v, zero, zero, zero]
        return lax.dot_general(
            jnp.concatenate(parts, 0).astype(jnp.bfloat16), spread, (((0,), (0,)), ((), ())),
            preferred_element_type=jnp.float32,
        )

    hot = wide(kind, False) == (lax.broadcasted_iota(jnp.int32, (1, WIDE), 1) % DIRS).astype(jnp.float32)
    v = wide(ratio)
    for x in range(1, wx + 3):
        inverse[x] = v[GROUP * x:GROUP * x + rows_y]
    for c in range(3):
        v = jnp.where(hot, wide(sources[0][c]), 0.0)
        for x in range(1, wx + 3):
            source_1[c, x] = v[GROUP * x:GROUP * x + rows_y]
        v = jnp.where(hot, wide(sources[1][c]), 0.0)
        for x in range(wx):
            source_2[c, x] = v[GROUP * (x + REACH):GROUP * (x + REACH) + wy]

    for c in r_copies:
        c.wait_send()
    arrivals = list(r_copies)
    for c in arrivals:
        c.wait_recv()

    def plane(f, x, lanes=slice(None)):
        return [f[c, x, :, lanes] for c in range(3)]

    low, high = slice(0, HALF), slice(HALF, WIDE)

    def h_first(x):
        f, g = plane(te, x), plane(th, x)
        curl = curl_f(f, lambda c: te[c, x + 1], next_y, next_z)
        for c in range(3):
            th[c, x] = g[c] - time_step * curl[c]

    def e_first(x, lanes):
        f, g = plane(te, x, lanes), plane(th, x, lanes)
        below = [th[c, x, :, :] for c in range(3)]

        def pz(v):
            if lanes is low:
                return prev_z(v)
            n = [k for k in range(3) if g[k] is v][0]
            return prev_z(below[n])[:, HALF:]

        curl = curl_b(g, lambda c: th[c, x - 1, :, lanes], prev_y, pz)
        ratio = inverse[x, :, lanes]
        for c in range(3):
            te[c, x, :, lanes] = f[c] + ratio * curl[c] - source_1[c, x, :, lanes]

    def h_second(x, lanes):
        f, g = plane(te, x, lanes), plane(th, x, lanes)
        above = [te[c, x, :, :] for c in range(3)]

        def nz(v):
            if lanes is high:
                return next_z(v)
            n = [k for k in range(3) if f[k] is v][0]
            return next_z(above[n])[:, :HALF]

        curl = curl_f(f, lambda c: te[c, x + 1, :, lanes], next_y, nz)
        for c in range(3):
            th[c, x, :, lanes] = g[c] - time_step * curl[c]

    def e_second(x, lanes, comps):
        g = plane(th, x, lanes)
        curl = curl_b(g, lambda c: th[c, x - 1, :, lanes], prev_y, prev_z)
        return [
            te[c, x, :wy, lanes] + inverse[x, :wy, lanes] * curl[c][:wy] - source_2[c, x - REACH, :, lanes]
            for c in range(comps)
        ]

    h_first(0)
    h_first(1)
    e_first(1, high)
    h_first(2)
    e_first(2, high)
    h_second(1, high)

    def top_pair(u, carry):
        got = []
        for n in range(2):
            x = 2 * u + 3 + n
            h_first(x)
            e_first(x, high)
            h_second(x - 1, high)
            got.append(e_second(x - 1, high, 2))
        for q in range(2):
            tops[q, pl.ds(pl.multiple_of(u * wy, wy), wy)] = jnp.where(
                lanes_of(got[0][q].shape) < DIRS, pltpu.roll(got[0][q], DIRS, 1), got[1][q]
            )
        return carry

    copies = []
    parts = 2
    for part in range(parts):
        first, last = part * half // parts, (part + 1) * half // parts
        lax.fori_loop(first, last, top_pair, 0)
        span = pl.ds(first * wy, (last - first) * wy)
        for k in reversed(range(len(sheet))):
            to = mate if k % 2 == 0 else i
            q = 1 - core if k % 2 == 0 else core
            n = part * len(sheet) + k
            c = copy(
                tops.at[q, span], gathered.at[(k + 1) // 2, core, span], g_send.at[n], g_recv.at[n], (to, sheet[k][1])
            )
            c.start()
            copies.append(((k + 1) // 2, c))

    e_first(1, low)
    e_first(2, low)
    h_second(1, low)

    def rest(u, carry):
        x = u + 3
        e_first(x, low)
        h_second(x - 1, low)
        new = e_second(x - 1, slice(None), 3)
        for c in range(3):
            out_e[c, u] = new[c]
            out_h[c, u] = th[c, x - 1, :wy]
        return carry

    lax.fori_loop(0, wx, rest, 0)

    gathered[0, core] = tops[core]

    def top_parts(k):
        for at_k, c in copies:
            if at_k == k:
                c.wait_recv()
        near, far = split(gathered[k].reshape(block, 2 * DIRS))[:2]
        return jnp.concatenate([near, near, far], 0)

    def product(k, v, span):
        return jnp.dot(table[paired(j, k, ny), span], v, preferred_element_type=jnp.float32)

    spans = [slice(0, rows), slice(rows, 2 * rows)]
    sums = [0.0, 0.0]
    for k in range(ny):
        v = top_parts(k)
        if k < ny - 1:
            sums = [sums[n] + product(k, v, spans[n]) for n in range(2)]
    out = []
    for n in range(2):
        total = sums[n] + product(ny - 1, v, spans[n])
        cosines, sines = total[:part_rows], total[part_rows:]
        mine = slice(n * part_rows, (n + 1) * part_rows)
        real = cosines * turn_c[mine] - sines * turn_s[mine]
        imag = sines * turn_c[mine] + cosines * turn_s[mine]
        real = real + pltpu.roll(real, DIRS, 1)
        imag = imag + pltpu.roll(imag, DIRS, 1)
        both = jnp.where(lower[mine], real, -imag)
        partial[n * nx // 2:(n + 1) * nx // 2] = both.reshape(nx // 2, own, 2 * DIRS)
        for b in range(n * nx // 2, (n + 1) * nx // 2):
            k = nx - 1 - b
            if k:
                c = copy(partial.at[b], arrived.at[k], p_send.at[k], p_recv.at[k], line[k - 1])
                c.start()
                out.append((k, c))
    totals = [partial[nx - 1], None]
    for k, c in out[::-1]:
        c.wait_recv()
        totals[k % 2] = arrived[k] if totals[k % 2] is None else totals[k % 2] + arrived[k]
    out_s[:, :2 * DIRS] = jnp.where(core == 0, totals[0], totals[1])
    out_s[:, 2 * DIRS:] = jnp.where(core == 0, totals[1], totals[0])
    for _, c in copies + out:
        c.wait_send()


def hand_over(from_e, from_h, from_s, to_e, to_h, to_s, sem):
    copies = [
        pltpu.make_async_copy(src, dst, sem.at[k])
        for k, (src, dst) in enumerate(((from_e, to_e), (from_h, to_h), (from_s, to_s)))
    ]
    for c in copies:
        c.start()
    for c in copies:
        c.wait()


def local(nx, ny, te, th, fe, fh, classes, material, permittivity, contrast, orders):
    wx, wy = te.shape[1], te.shape[2]
    own = orders.shape[0] // (nx * ny)
    rows = nx * own
    f32 = jnp.float32
    vmem = pl.BlockSpec(memory_space=pltpu.VMEM)
    hbm = pl.BlockSpec(memory_space=pltpu.HBM)
    args = (
        te, th, jnp.transpose(fe, (0, 1, 3, 2)), jnp.transpose(fh, (0, 1, 3, 2)),
        jnp.transpose(classes, (0, 2, 1)), jnp.transpose(material, (0, 2, 1)),
        permittivity, contrast, jnp.transpose(orders),
    )
    args = tuple(pltpu.with_memory_space_constraint(v, pltpu.HBM) for v in args)
    out_shape = (
        jax.ShapeDtypeStruct(te.shape, f32),
        jax.ShapeDtypeStruct(th.shape, f32),
        jax.ShapeDtypeStruct((own, 4 * DIRS), f32),
    )
    wide_x, wide_y = wx + 2 * REACH, wy + PAD

    def pair_of(n):
        return [pltpu.SemaphoreType.DMA((n,))] * 2

    results = pl.pallas_call(
        functools.partial(kernel, nx, ny, own),
        out_shape=out_shape,
        in_specs=[hbm] * 9,
        out_specs=(vmem, vmem, vmem),
        scratch_shapes=[
            *[pltpu.VMEM((3, wide_x, wide_y, WIDE), f32)] * 3,
            pltpu.VMEM((3, wx, wy, WIDE), f32),
            pltpu.VMEM((wide_x, wide_y, WIDE), f32),
            pltpu.VMEM((32, wx * wy), f32), pltpu.VMEM((2, 32, wx * wy), f32),
            pltpu.VMEM((8, 128), f32), pltpu.VMEM((6, 8, 128), f32),
            pltpu.VMEM((2, wx // 2 * wy, 2 * DIRS), f32),
            pltpu.VMEM((ny, 2, wx // 2 * wy, 2 * DIRS), f32),
            *[pltpu.VMEM((nx, own, 2 * DIRS), f32)] * 2,
            pltpu.VMEM((ny, 2 * rows, 3 * wx * wy), jnp.bfloat16),
            *pair_of(16), *pair_of(8), *pair_of(4 * ny), *pair_of(nx),
            *[pltpu.VMEM(v.shape, v.dtype) for v in args[2:6]],
            *[pltpu.SMEM(v.shape, v.dtype) for v in args[6:8]],
            pltpu.VMEM(args[8].shape, args[8].dtype),
            pltpu.SemaphoreType.DMA((13,)),
        ],
        compiler_params=pltpu.CompilerParams(
            collective_id=0, has_side_effects=True, vmem_limit_bytes=48 * 1024 * 1024
        ),
        name="slab",
    )(*args)
    return pl.pallas_call(
        hand_over,
        out_shape=out_shape,
        in_specs=[vmem] * 3,
        out_specs=(hbm, hbm, hbm),
        scratch_shapes=[pltpu.SemaphoreType.DMA((3,))],
        compiler_params=pltpu.CompilerParams(vmem_limit_bytes=16 * 1024 * 1024),
        name="hand_over",
    )(*results)


def solution(mesh):
    in_specs = (
        P(None, "gx", "gy", None),
        P(None, "gx", "gy", None),
        P(None, "gx", "gy", None),
        P(None, "gx", "gy", None),
        P("gx", "gy", None),
        P("gx", "gy", None),
        P(),
        P(),
        P(),
    )
    out_specs = (P(None, "gx", "gy", None), P(None, "gx", "gy", None), P(("gx", "gy"), None))
    body = functools.partial(local, mesh.shape["gx"], mesh.shape["gy"])
    return jax.shard_map(body, mesh=mesh, in_specs=in_specs, out_specs=out_specs, check_vma=False)
```

```python
import functools
import math

import jax
import jax.numpy as jnp
from jax import lax
from jax.experimental import pallas as pl
from jax.experimental.pallas import tpu as pltpu
from jax.sharding import PartitionSpec as P

DIRS = 64
STEPS = 2
LAYERS = 4
WIDE = LAYERS * DIRS
HALF = WIDE // 2
time_step = 0.5


REACH = 2
PAD = 8
GROUP = 32


def lanes_of(shape):
    return lax.broadcasted_iota(jnp.int32, shape, len(shape) - 1)


def sublanes_of(shape):
    return lax.broadcasted_iota(jnp.int32, shape, len(shape) - 2)


def next_y(f):
    return pltpu.roll(f, f.shape[0] - 1, 0)


def prev_y(f):
    return pltpu.roll(f, 1, 0)


def next_z(f):
    wide = f.shape[-1]
    return jnp.where(lanes_of(f.shape) < wide - DIRS, pltpu.roll(f, wide - DIRS, 1), 0.0)


def prev_z(f):
    return jnp.where(lanes_of(f.shape) >= DIRS, pltpu.roll(f, DIRS, 1), 0.0)


def curl_f(f, x_next, ny, nz):
    fx, fy, fz = f
    return (
        (ny(fz) - fz) - (nz(fy) - fy),
        (nz(fx) - fx) - (x_next(2) - fz),
        (x_next(1) - fy) - (ny(fx) - fx),
    )


def curl_b(f, x_prev, py, pz):
    fx, fy, fz = f
    return (
        (fz - py(fz)) - (fy - pz(fy)),
        (fx - pz(fx)) - (fz - x_prev(2)),
        (fy - x_prev(1)) - (fx - py(fx)),
    )


def sine(turn):
    u = turn * (2.0 * math.pi)
    s = u * u
    poly = -1.0 / 39916800.0
    for c in (1.0 / 362880.0, -1.0 / 5040.0, 1.0 / 120.0, -1.0 / 6.0):
        poly = poly * s + c
    return u + u * (s * poly)


def split(v):
    parts = []
    for _ in range(3):
        parts.append(v.astype(jnp.bfloat16))
        v = v - parts[-1].astype(jnp.float32)
    return parts


def stacked(v):
    parts = [part.astype(jnp.float32) for part in split(v)]
    return parts


def selected(v, choice):
    n = v.shape[0]
    parts = stacked(v)
    if 3 * n % 16:
        parts.append(jnp.zeros_like(v))
    got = jnp.dot(
        jnp.concatenate(parts, 0).astype(jnp.bfloat16), choice, preferred_element_type=jnp.float32
    )
    return got[:n] + got[n:2 * n] + got[2 * n:3 * n]


def ones_where(hit):
    return hit.astype(jnp.float32).astype(jnp.bfloat16)


def paired(n, k, size):
    out, bit = 0, 1
    while bit < size:
        out = out + bit * ((n // bit + k // bit) % 2)
        bit *= 2
    return out


def kernel(
    nx, ny, own,
    te_at, th_at, fe_at, fh_at, classes_at, material_at, permittivity_at, contrast_at, orders_at,
    out_e, out_h, out_s,
    te, th, source_1, source_2, inverse, block_out, block_in, strip_out, strip_in,
    tops, gathered, partial, arrived, table,
    rim_send, rim_recv, f_send, f_recv, g_send, g_recv, p_send, p_recv,
    fe, fh, classes, material, permittivity, contrast, orders, load,
):
    wx, wy = te_at.shape[1], te_at.shape[2]
    rows_y = te.shape[2]
    inside = (pl.ds(REACH, wx), pl.ds(0, wy))
    i, j = lax.axis_index("gx"), lax.axis_index("gy")
    core = lax.rem(i, 2)
    mate = i + 1 - 2 * core
    beyond = lax.rem(i + nx - 1 + 2 * core, nx)

    def at(dx, dy):
        return (lax.rem(i + nx + dx, nx), lax.rem(j + ny + dy, ny))

    line = [(paired(i, k, nx), j) for k in range(1, nx)]
    sheet = [(mate, j)] + [(n, paired(j, k, ny)) for k in range(1, ny) for n in (i, mate)]
    left, right = at(0, -1)[1], at(0, 1)[1]
    peers = [(beyond, left), (beyond, right), (beyond, j)] + sheet[1:] + line
    barrier = pltpu.get_barrier_semaphore()
    for peer in peers:
        pl.semaphore_signal(barrier, inc=1, device_id=peer, device_id_type=pl.DeviceIdType.MESH)

    def copy(src, dst, send, recv, device):
        return pltpu.make_async_remote_copy(
            src_ref=src, dst_ref=dst, send_sem=send, recv_sem=recv,
            device_id=device, device_id_type=pl.DeviceIdType.MESH,
        )

    small = [
        pltpu.make_async_copy(src, dst, load.at[6 + k])
        for k, (src, dst) in enumerate((
            (fe_at, fe), (fh_at, fh), (classes_at, classes), (material_at, material),
            (permittivity_at, permittivity), (contrast_at, contrast), (orders_at, orders),
        ))
    ]
    large = [
        pltpu.make_async_copy(src.at[c], dst.at[(c, *inside)], load.at[2 * c + k])
        for c in range(3) for k, (src, dst) in enumerate(((te_at, te), (th_at, th)))
    ]
    for c in small[:4] + large + small[4:]:
        c.start()

    spots = wx * wy
    lane = lax.broadcasted_iota(jnp.int32, (1, 128), 1)
    group, in_group = lane // GROUP, lane % GROUP
    k = in_group % 4
    from_lane = group * spots + (in_group // 4) * wy + jnp.where(k < 2, k, wy - 4 + k)
    strip_choice = ones_where(lax.broadcasted_iota(jnp.int32, (4 * spots, 128), 0) == from_lane)
    for c in small[:4]:
        c.wait()
    for x in range(wx):
        cells = slice(x * wy, (x + 1) * wy)
        for c in range(3):
            block_out[4 * c:4 * c + 4, cells] = fe[c, x]
            block_out[12 + 4 * c:16 + 4 * c, cells] = fh[c, x]
        block_out[24:28, cells] = classes[x].astype(jnp.float32)
        block_out[28:32, cells] = material[x].astype(jnp.float32)
    mine = block_out[...]
    strip_out[...] = selected(jnp.concatenate([mine[8 * g:8 * g + 8] for g in range(4)], 1), strip_choice)

    pl.semaphore_wait(barrier, len(peers))
    strips = [(0, -1), (0, 1), (-1, -1), (-1, 1), (1, -1), (1, 1)]
    f_copies = []
    for n, (dx, dy) in enumerate(strips):
        f_copies.append(copy(strip_out, strip_in.at[n], f_send.at[n], f_recv.at[n], at(-dx, -dy)))
    for n, dx in enumerate((-1, 1)):
        f_copies.append(copy(block_out, block_in.at[n], f_send.at[6 + n], f_recv.at[6 + n], at(-dx, 0)))
    for c in f_copies[2:] + f_copies[:2]:
        c.start()

    def span(d, size, before, after, n):
        if d > 0:
            return pl.ds(before[0] + size - n, n), pl.ds(before[1] - n, n)
        if d < 0:
            return pl.ds(before[0], n), pl.ds(after, n)
        return pl.ds(before[0], size), pl.ds(before[0], size)

    r_copies = []
    for c in large:
        c.wait()
    for dx, dy in ((1, 1), (1, -1), (-1, 1), (-1, -1), (0, 1), (0, -1), (1, 0), (-1, 0)):
        for field in range(2):
            if field == 1 and dx < 0 and dy < 0:
                continue
            one = dx * dy > 0
            px = 1 if one or (field == 1 and dx < 0) else REACH
            py = 1 if one or (field == 1 and dy < 0) else REACH
            sx, tx = span(dx, wx, (REACH, REACH), REACH + wx, px)
            sy, ty = span(dy, wy, (0, rows_y), wy, py)
            f = (te, th)[field]
            n = len(r_copies)
            c = copy(f.at[:, sx, sy, :], f.at[:, tx, ty, :], rim_send.at[n], rim_recv.at[n], at(dx, dy))
            c.start()
            r_copies.append(c)

    for c in small[4:]:
        c.wait()
    rows, half = nx * own, wx // 2
    block = 2 * half * wy
    cells = ny * block
    count = orders.shape[1]
    row = lax.broadcasted_iota(jnp.int32, (rows, 1), 0)
    target = paired(i, nx - 1 - row // own, nx) * (ny * own) + j * own + row % own
    pick = ones_where(lax.broadcasted_iota(jnp.int32, (rows, count), 1) == target)
    pair = lax.dot_general(
        pick, orders[...].astype(jnp.float32).astype(jnp.bfloat16),
        (((1,), (1,)), ((), ())), preferred_element_type=jnp.float32,
    )
    cell = lax.broadcasted_iota(jnp.int32, (1, cells), 1)
    all_x, all_y = nx * wx, ny * wy
    all_cells = float(all_x * all_y)
    x_in = ((cell // (half * wy)) % 2) * wx + 2 * ((cell // wy) % half)
    x_at = (((i - core) * wx + x_in) * all_y).astype(jnp.float32)
    y_at = (((cell // block) * wy + cell % wy) * all_x).astype(jnp.float32)

    def waves(index):
        index = index - all_cells * jnp.round(index * (1.0 / all_cells))
        turn = index * (1.0 / all_cells)
        cosine = sine(0.25 - jnp.abs(turn))
        sines = sine(jnp.where(turn > 0.25, 0.5 - turn, jnp.where(turn < -0.25, -0.5 - turn, turn)))
        return cosine, sines

    part_rows = rows // 2
    for sine_rows, value in zip((0, part_rows), waves(pair[:, 0:1] * x_at + pair[:, 1:2] * y_at)):
        near, far = split(value)[:2]
        for k in range(ny):
            for q, part in enumerate((near, far, near)):
                for n in range(2):
                    place = 2 * n * part_rows + sine_rows
                    table[k, place:place + part_rows, q * block:(q + 1) * block] = part[
                        n * part_rows:(n + 1) * part_rows, k * block:(k + 1) * block
                    ]
    lower = lax.broadcasted_iota(jnp.int32, (rows, 2 * DIRS), 1) < DIRS
    turn_c, turn_s = waves(jnp.where(lower, 0.0, pair[:, 0:1] * float(all_y)))
    scale = 1.0 / math.sqrt(all_x * all_y)
    turn_c, turn_s = turn_c * scale, turn_s * scale

    span_l = (wx + 2 * REACH) * GROUP
    spot = lax.broadcasted_iota(jnp.int32, (1, span_l), 1)
    p = spot % GROUP
    x = spot // GROUP - REACH
    y = jnp.where(p < wy + REACH, p, p - rows_y)
    valid = (p < wy + REACH) | ((p >= rows_y - REACH) & (p < rows_y))
    side_x = jnp.where(x < 0, -1, jnp.where(x >= wx, 1, 0))
    side_y = jnp.where(y < 0, -1, jnp.where(y >= wy, 1, 0))
    lx, ly = x - side_x * wx, y - side_y * wy
    whole = jnp.where(side_x == 0, 0, jnp.where(side_x < 0, 1, 2)) * spots + lx * wy + ly
    which = jnp.where(side_x == 0, 0, jnp.where(side_x < 0, 2, 4)) + jnp.where(side_y > 0, 1, 0)
    strip = 3 * spots + which * GROUP + lx * 4 + jnp.where(ly < 2, ly, ly - (wy - 4))
    origin = jnp.where(valid, jnp.where(side_y == 0, whole, strip), -1)
    choice = ones_where(lax.broadcasted_iota(jnp.int32, (3 * spots + 256, span_l), 0) == origin)
    spread = ones_where(
        lax.broadcasted_iota(jnp.int32, (32, WIDE), 0) % 8 == lax.broadcasted_iota(jnp.int32, (32, WIDE), 1) // DIRS
    )

    for c in f_copies:
        c.wait()
    gathered_strips = []
    for first in (0, 4):
        groups = []
        for g in range(4):
            got = None
            for n in range(first, min(first + 4, 6)):
                v = strip_in[n]
                shift = (GROUP * (n - first - g)) % 128
                v = pltpu.roll(v, shift, 1) if shift else v
                got = v if got is None else jnp.where(lane // GROUP == n - first, v, got)
            groups.append(got)
        gathered_strips.append(jnp.concatenate(groups, 0))
    around = selected(
        jnp.concatenate([mine, block_in[0], block_in[1], *gathered_strips], 1), choice
    )
    pairs = [around[8 * g:8 * g + 8] for g in range(4)]
    fields = [f for v in pairs for f in (v, pltpu.roll(v, 4, 0))]
    f_e, f_h, kind, matter = fields[:3], fields[3:6], fields[6], fields[7]
    layer = sublanes_of((8, span_l))

    def f_next_x(f):
        return pltpu.roll(f, span_l - GROUP, 1)

    def f_prev_x(f):
        return pltpu.roll(f, GROUP, 1)

    def f_next_y(f):
        return jnp.where(p == rows_y - 1, pltpu.roll(f, rows_y - 1, 1), pltpu.roll(f, span_l - 1, 1))

    def f_prev_y(f):
        return jnp.where(p == 0, pltpu.roll(f, span_l - rows_y + 1, 1), pltpu.roll(f, 1, 1))

    def f_next_z(f):
        return jnp.where(layer < LAYERS - 1, pltpu.roll(f, 7, 0), 0.0)

    def f_prev_z(f):
        return jnp.where(layer >= 1, pltpu.roll(f, 1, 0), 0.0)

    eps = jnp.full((8, span_l), permittivity[0])
    slope = jnp.full((8, span_l), contrast[0])
    for k in range(1, permittivity.shape[0]):
        eps = jnp.where(matter == float(k), permittivity[k], eps)
        slope = jnp.where(matter == float(k), contrast[k], slope)
    ratio = time_step / eps
    coef = time_step * slope / (eps * eps)
    sources = []
    for step in range(STEPS):
        curl = curl_f(f_e, lambda c: f_next_x(f_e[c]), f_next_y, f_next_z)
        f_h = [f_h[c] - time_step * curl[c] for c in range(3)]
        curl = curl_b(f_h, lambda c: f_prev_x(f_h[c]), f_prev_y, f_prev_z)
        sources.append([coef * curl[c] for c in range(3)])
        f_e = [f_e[c] + ratio * curl[c] for c in range(3)]

    def wide(v, exact=True):
        v = jnp.where(layer < LAYERS, v, 0.0)
        zero = jnp.zeros_like(v)
        parts = stacked(v) + [zero] if exact else [v, zero, zero, zero]
        return lax.dot_general(
            jnp.concatenate(parts, 0).astype(jnp.bfloat16), spread, (((0,), (0,)), ((), ())),
            preferred_element_type=jnp.float32,
        )

    hot = wide(kind, False) == (lax.broadcasted_iota(jnp.int32, (1, WIDE), 1) % DIRS).astype(jnp.float32)
    v = wide(ratio)
    for x in range(1, wx + 3):
        inverse[x] = v[GROUP * x:GROUP * x + rows_y]
    for c in range(3):
        v = jnp.where(hot, wide(sources[0][c]), 0.0)
        for x in range(1, wx + 3):
            source_1[c, x] = v[GROUP * x:GROUP * x + rows_y]
        v = jnp.where(hot, wide(sources[1][c]), 0.0)
        for x in range(wx):
            source_2[c, x] = v[GROUP * (x + REACH):GROUP * (x + REACH) + wy]

    for c in r_copies:
        c.wait_send()
    arrivals = list(r_copies)
    for c in arrivals:
        c.wait_recv()

    def plane(f, x, lanes=slice(None)):
        return [f[c, x, :, lanes] for c in range(3)]

    low, high = slice(0, HALF), slice(HALF, WIDE)

    def h_first(x):
        f, g = plane(te, x), plane(th, x)
        curl = curl_f(f, lambda c: te[c, x + 1], next_y, next_z)
        for c in range(3):
            th[c, x] = g[c] - time_step * curl[c]

    def e_first(x, lanes):
        f, g = plane(te, x, lanes), plane(th, x, lanes)
        below = [th[c, x, :, :] for c in range(3)]

        def pz(v):
            if lanes is low:
                return prev_z(v)
            n = [k for k in range(3) if g[k] is v][0]
            return prev_z(below[n])[:, HALF:]

        curl = curl_b(g, lambda c: th[c, x - 1, :, lanes], prev_y, pz)
        ratio = inverse[x, :, lanes]
        for c in range(3):
            te[c, x, :, lanes] = f[c] + ratio * curl[c] - source_1[c, x, :, lanes]

    def h_second(x, lanes):
        f, g = plane(te, x, lanes), plane(th, x, lanes)
        above = [te[c, x, :, :] for c in range(3)]

        def nz(v):
            if lanes is high:
                return next_z(v)
            n = [k for k in range(3) if f[k] is v][0]
            return next_z(above[n])[:, :HALF]

        curl = curl_f(f, lambda c: te[c, x + 1, :, lanes], next_y, nz)
        for c in range(3):
            th[c, x, :, lanes] = g[c] - time_step * curl[c]

    def e_second(x, lanes, comps):
        g = plane(th, x, lanes)
        curl = curl_b(g, lambda c: th[c, x - 1, :, lanes], prev_y, prev_z)
        return [
            te[c, x, :wy, lanes] + inverse[x, :wy, lanes] * curl[c][:wy] - source_2[c, x - REACH, :, lanes]
            for c in range(comps)
        ]

    h_first(0)
    h_first(1)
    e_first(1, high)
    h_first(2)
    e_first(2, high)
    h_second(1, high)

    def top_pair(u, carry):
        got = []
        for n in range(2):
            x = 2 * u + 3 + n
            h_first(x)
            e_first(x, high)
            h_second(x - 1, high)
            got.append(e_second(x - 1, high, 2))
        for q in range(2):
            tops[q, pl.ds(pl.multiple_of(u * wy, wy), wy)] = jnp.where(
                lanes_of(got[0][q].shape) < DIRS, pltpu.roll(got[0][q], DIRS, 1), got[1][q]
            )
        return carry

    copies = []
    parts = 2
    for part in range(parts):
        first, last = part * half // parts, (part + 1) * half // parts
        lax.fori_loop(first, last, top_pair, 0, unroll=True)
        span = pl.ds(first * wy, (last - first) * wy)
        for k in reversed(range(len(sheet))):
            to = mate if k % 2 == 0 else i
            q = 1 - core if k % 2 == 0 else core
            n = part * len(sheet) + k
            c = copy(
                tops.at[q, span], gathered.at[(k + 1) // 2, core, span], g_send.at[n], g_recv.at[n], (to, sheet[k][1])
            )
            c.start()
            copies.append(((k + 1) // 2, c))

    e_first(1, low)
    e_first(2, low)
    h_second(1, low)

    def rest(u, carry):
        x = u + 3
        e_first(x, low)
        h_second(x - 1, low)
        new = e_second(x - 1, slice(None), 3)
        for c in range(3):
            out_e[c, u] = new[c]
            out_h[c, u] = th[c, x - 1, :wy]
        return carry

    lax.fori_loop(0, wx, rest, 0)

    gathered[0, core] = tops[core]

    def top_parts(k):
        for at_k, c in copies:
            if at_k == k:
                c.wait_recv()
        near, far = split(gathered[k].reshape(block, 2 * DIRS))[:2]
        return jnp.concatenate([near, near, far], 0)

    def product(k, v, span):
        return jnp.dot(table[paired(j, k, ny), span], v, preferred_element_type=jnp.float32)

    spans = [slice(0, rows), slice(rows, 2 * rows)]
    sums = [0.0, 0.0]
    for k in range(ny):
        v = top_parts(k)
        if k < ny - 1:
            sums = [sums[n] + product(k, v, spans[n]) for n in range(2)]
    out = []
    for n in range(2):
        total = sums[n] + product(ny - 1, v, spans[n])
        cosines, sines = total[:part_rows], total[part_rows:]
        mine = slice(n * part_rows, (n + 1) * part_rows)
        real = cosines * turn_c[mine] - sines * turn_s[mine]
        imag = sines * turn_c[mine] + cosines * turn_s[mine]
        real = real + pltpu.roll(real, DIRS, 1)
        imag = imag + pltpu.roll(imag, DIRS, 1)
        both = jnp.where(lower[mine], real, -imag)
        partial[n * nx // 2:(n + 1) * nx // 2] = both.reshape(nx // 2, own, 2 * DIRS)
        for b in range(n * nx // 2, (n + 1) * nx // 2):
            k = nx - 1 - b
            if k:
                c = copy(partial.at[b], arrived.at[k], p_send.at[k], p_recv.at[k], line[k - 1])
                c.start()
                out.append((k, c))
    totals = [partial[nx - 1], None]
    for k, c in out[::-1]:
        c.wait_recv()
        totals[k % 2] = arrived[k] if totals[k % 2] is None else totals[k % 2] + arrived[k]
    out_s[:, :2 * DIRS] = jnp.where(core == 0, totals[0], totals[1])
    out_s[:, 2 * DIRS:] = jnp.where(core == 0, totals[1], totals[0])
    for _, c in copies + out:
        c.wait_send()


def hand_over(from_e, from_h, from_s, to_e, to_h, to_s, sem):
    copies = [
        pltpu.make_async_copy(src, dst, sem.at[k])
        for k, (src, dst) in enumerate(((from_e, to_e), (from_h, to_h), (from_s, to_s)))
    ]
    for c in copies:
        c.start()
    for c in copies:
        c.wait()


def local(nx, ny, te, th, fe, fh, classes, material, permittivity, contrast, orders):
    wx, wy = te.shape[1], te.shape[2]
    own = orders.shape[0] // (nx * ny)
    rows = nx * own
    f32 = jnp.float32
    vmem = pl.BlockSpec(memory_space=pltpu.VMEM)
    hbm = pl.BlockSpec(memory_space=pltpu.HBM)
    args = (
        te, th, jnp.transpose(fe, (0, 1, 3, 2)), jnp.transpose(fh, (0, 1, 3, 2)),
        jnp.transpose(classes, (0, 2, 1)), jnp.transpose(material, (0, 2, 1)),
        permittivity, contrast, jnp.transpose(orders),
    )
    args = tuple(pltpu.with_memory_space_constraint(v, pltpu.HBM) for v in args)
    out_shape = (
        jax.ShapeDtypeStruct(te.shape, f32),
        jax.ShapeDtypeStruct(th.shape, f32),
        jax.ShapeDtypeStruct((own, 4 * DIRS), f32),
    )
    wide_x, wide_y = wx + 2 * REACH, wy + PAD

    def pair_of(n):
        return [pltpu.SemaphoreType.DMA((n,))] * 2

    results = pl.pallas_call(
        functools.partial(kernel, nx, ny, own),
        out_shape=out_shape,
        in_specs=[hbm] * 9,
        out_specs=(vmem, vmem, vmem),
        scratch_shapes=[
            *[pltpu.VMEM((3, wide_x, wide_y, WIDE), f32)] * 3,
            pltpu.VMEM((3, wx, wy, WIDE), f32),
            pltpu.VMEM((wide_x, wide_y, WIDE), f32),
            pltpu.VMEM((32, wx * wy), f32), pltpu.VMEM((2, 32, wx * wy), f32),
            pltpu.VMEM((8, 128), f32), pltpu.VMEM((6, 8, 128), f32),
            pltpu.VMEM((2, wx // 2 * wy, 2 * DIRS), f32),
            pltpu.VMEM((ny, 2, wx // 2 * wy, 2 * DIRS), f32),
            *[pltpu.VMEM((nx, own, 2 * DIRS), f32)] * 2,
            pltpu.VMEM((ny, 2 * rows, 3 * wx * wy), jnp.bfloat16),
            *pair_of(16), *pair_of(8), *pair_of(4 * ny), *pair_of(nx),
            *[pltpu.VMEM(v.shape, v.dtype) for v in args[2:6]],
            *[pltpu.SMEM(v.shape, v.dtype) for v in args[6:8]],
            pltpu.VMEM(args[8].shape, args[8].dtype),
            pltpu.SemaphoreType.DMA((13,)),
        ],
        compiler_params=pltpu.CompilerParams(
            collective_id=0, has_side_effects=True, vmem_limit_bytes=48 * 1024 * 1024
        ),
        name="slab",
    )(*args)
    return pl.pallas_call(
        hand_over,
        out_shape=out_shape,
        in_specs=[vmem] * 3,
        out_specs=(hbm, hbm, hbm),
        scratch_shapes=[pltpu.SemaphoreType.DMA((3,))],
        compiler_params=pltpu.CompilerParams(vmem_limit_bytes=16 * 1024 * 1024),
        name="hand_over",
    )(*results)


def solution(mesh):
    in_specs = (
        P(None, "gx", "gy", None),
        P(None, "gx", "gy", None),
        P(None, "gx", "gy", None),
        P(None, "gx", "gy", None),
        P("gx", "gy", None),
        P("gx", "gy", None),
        P(),
        P(),
        P(),
    )
    out_specs = (P(None, "gx", "gy", None), P(None, "gx", "gy", None), P(("gx", "gy"), None))
    body = functools.partial(local, mesh.shape["gx"], mesh.shape["gy"])
    return jax.shard_map(body, mesh=mesh, in_specs=in_specs, out_specs=out_specs, check_vma=False)
```

```python
import functools
import math

import jax
import jax.numpy as jnp
from jax import lax
from jax.experimental import pallas as pl
from jax.experimental.pallas import tpu as pltpu
from jax.sharding import PartitionSpec as P

DIRS = 64
STEPS = 2
LAYERS = 4
WIDE = LAYERS * DIRS
HALF = WIDE // 2
time_step = 0.5


REACH = 2
PAD = 8
GROUP = 32


def lanes_of(shape):
    return lax.broadcasted_iota(jnp.int32, shape, len(shape) - 1)


def sublanes_of(shape):
    return lax.broadcasted_iota(jnp.int32, shape, len(shape) - 2)


def next_y(f):
    return pltpu.roll(f, f.shape[0] - 1, 0)


def prev_y(f):
    return pltpu.roll(f, 1, 0)


def next_z(f):
    wide = f.shape[-1]
    return jnp.where(lanes_of(f.shape) < wide - DIRS, pltpu.roll(f, wide - DIRS, 1), 0.0)


def prev_z(f):
    return jnp.where(lanes_of(f.shape) >= DIRS, pltpu.roll(f, DIRS, 1), 0.0)


def curl_f(f, x_next, ny, nz):
    fx, fy, fz = f
    return (
        (ny(fz) - fz) - (nz(fy) - fy),
        (nz(fx) - fx) - (x_next(2) - fz),
        (x_next(1) - fy) - (ny(fx) - fx),
    )


def curl_b(f, x_prev, py, pz):
    fx, fy, fz = f
    return (
        (fz - py(fz)) - (fy - pz(fy)),
        (fx - pz(fx)) - (fz - x_prev(2)),
        (fy - x_prev(1)) - (fx - py(fx)),
    )


def sine(turn):
    u = turn * (2.0 * math.pi)
    s = u * u
    poly = -1.0 / 39916800.0
    for c in (1.0 / 362880.0, -1.0 / 5040.0, 1.0 / 120.0, -1.0 / 6.0):
        poly = poly * s + c
    return u + u * (s * poly)


def split(v):
    parts = []
    for _ in range(3):
        parts.append(v.astype(jnp.bfloat16))
        v = v - parts[-1].astype(jnp.float32)
    return parts


def stacked(v):
    parts = [part.astype(jnp.float32) for part in split(v)]
    return parts


def selected(v, choice):
    n = v.shape[0]
    parts = stacked(v)
    if 3 * n % 16:
        parts.append(jnp.zeros_like(v))
    got = jnp.dot(
        jnp.concatenate(parts, 0).astype(jnp.bfloat16), choice, preferred_element_type=jnp.float32
    )
    return got[:n] + got[n:2 * n] + got[2 * n:3 * n]


def ones_where(hit):
    return hit.astype(jnp.float32).astype(jnp.bfloat16)


def paired(n, k, size):
    out, bit = 0, 1
    while bit < size:
        out = out + bit * ((n // bit + k // bit) % 2)
        bit *= 2
    return out


def kernel(
    nx, ny, own,
    te_at, th_at, fe_at, fh_at, classes_at, material_at, permittivity_at, contrast_at, orders_at,
    out_e, out_h, out_s,
    te, th, edge, h_1, e_1, h_2, source_1, source_2, inverse, block_out, block_in, strip_out, strip_in,
    tops, gathered, partial, arrived, table,
    rim_send, rim_recv, f_send, f_recv, g_send, g_recv, p_send, p_recv,
    fe, fh, classes, material, permittivity, contrast, orders, load,
):
    wx, wy = te_at.shape[1], te_at.shape[2]
    rows_y = te.shape[2]
    inside = (pl.ds(REACH, wx), pl.ds(0, wy))
    i, j = lax.axis_index("gx"), lax.axis_index("gy")
    core = lax.rem(i, 2)
    mate = i + 1 - 2 * core
    beyond = lax.rem(i + nx - 1 + 2 * core, nx)

    def at(dx, dy):
        return (lax.rem(i + nx + dx, nx), lax.rem(j + ny + dy, ny))

    line = [(paired(i, k, nx), j) for k in range(1, nx)]
    sheet = [(mate, j)] + [(n, paired(j, k, ny)) for k in range(1, ny) for n in (i, mate)]
    left, right = at(0, -1)[1], at(0, 1)[1]
    peers = [(beyond, left), (beyond, right), (beyond, j)] + sheet[1:] + line
    barrier = pltpu.get_barrier_semaphore()
    for peer in peers:
        pl.semaphore_signal(barrier, inc=1, device_id=peer, device_id_type=pl.DeviceIdType.MESH)

    def copy(src, dst, send, recv, device):
        return pltpu.make_async_remote_copy(
            src_ref=src, dst_ref=dst, send_sem=send, recv_sem=recv,
            device_id=device, device_id_type=pl.DeviceIdType.MESH,
        )

    small = [
        pltpu.make_async_copy(src, dst, load.at[6 + k])
        for k, (src, dst) in enumerate((
            (fe_at, fe), (fh_at, fh), (classes_at, classes), (material_at, material),
            (permittivity_at, permittivity), (contrast_at, contrast), (orders_at, orders),
        ))
    ]
    large = [
        pltpu.make_async_copy(src.at[c], dst.at[(c, *inside)], load.at[2 * c + k])
        for c in range(3) for k, (src, dst) in enumerate(((te_at, te), (th_at, th)))
    ]
    for c in small[:4] + large + small[4:]:
        c.start()

    spots = wx * wy
    lane = lax.broadcasted_iota(jnp.int32, (1, 128), 1)
    group, in_group = lane // GROUP, lane % GROUP
    k = in_group % 4
    from_lane = group * spots + (in_group // 4) * wy + jnp.where(k < 2, k, wy - 4 + k)
    strip_choice = ones_where(lax.broadcasted_iota(jnp.int32, (4 * spots, 128), 0) == from_lane)
    for c in small[:4]:
        c.wait()
    for x in range(wx):
        cells = slice(x * wy, (x + 1) * wy)
        for c in range(3):
            block_out[4 * c:4 * c + 4, cells] = fe[c, x]
            block_out[12 + 4 * c:16 + 4 * c, cells] = fh[c, x]
        block_out[24:28, cells] = classes[x].astype(jnp.float32)
        block_out[28:32, cells] = material[x].astype(jnp.float32)
    mine = block_out[...]
    strip_out[...] = selected(jnp.concatenate([mine[8 * g:8 * g + 8] for g in range(4)], 1), strip_choice)

    pl.semaphore_wait(barrier, len(peers))
    strips = [(0, -1), (0, 1), (-1, -1), (-1, 1), (1, -1), (1, 1)]
    f_copies = []
    for n, (dx, dy) in enumerate(strips):
        f_copies.append(copy(strip_out, strip_in.at[n], f_send.at[n], f_recv.at[n], at(-dx, -dy)))
    for n, dx in enumerate((-1, 1)):
        f_copies.append(copy(block_out, block_in.at[n], f_send.at[6 + n], f_recv.at[6 + n], at(-dx, 0)))
    for c in f_copies[2:] + f_copies[:2]:
        c.start()

    every, top_half, low_half = pl.ds(0, WIDE), pl.ds(HALF, HALF), pl.ds(0, HALF)
    low, high = slice(0, HALF), slice(HALF, WIDE)
    left_half = lax.broadcasted_iota(jnp.int32, (1, HALF), 1) < DIRS
    x0, x1 = REACH, REACH + wx
    same_x, same_y = (pl.ds(x0, wx),) * 2, (pl.ds(0, wy),) * 2
    r_copies = []

    def moved(source, target, n):
        return pl.ds(source, n), pl.ds(target, n)

    def rim(f, x, y, lanes, side):
        (sx, tx), (sy, ty) = x, y
        n = len(r_copies)
        c = copy(
            f.at[:, sx, sy, lanes], f.at[:, tx, ty, lanes], rim_send.at[n], rim_recv.at[n], at(*side)
        )
        r_copies.append(c)
        return c

    def other_layer(v):
        return pltpu.roll(v, DIRS, 1)

    for c in large:
        c.wait()
    for x in range(x0, x1):
        ex, ey, ez = [te[c, x, :wy, low] for c in range(3)]
        part_x = th[0, x, :wy, low] + time_step * (ez + (other_layer(te[1, x, :wy, high]) - ey))
        part_y = th[1, x, :wy, low] - time_step * ((other_layer(te[0, x, :wy, high]) - ex) + ez)
        edge[0, x, :wy] = jnp.where(left_half, other_layer(part_x), part_y)
        edge[1, x, :wy] = jnp.where(left_half, other_layer(ez), ez)
    one_up, two_up = moved(x1 - 1, 1, 1), moved(x1 - 2, 0, 2)
    one_down, two_down = moved(x0, x1, 1), moved(x0, x1, 2)
    one_right, two_right = moved(wy - 1, rows_y - 1, 1), moved(wy - 2, rows_y - 2, 2)
    one_left, two_left = moved(0, wy, 1), moved(0, wy, 2)
    lanes_e = pl.ds(0, HALF)
    early = [
        rim(te, one_up, one_right, every, (1, 1)), rim(th, one_up, one_right, every, (1, 1)),
        rim(edge, one_up, one_right, lanes_e, (1, 1)),
        rim(te, two_up, two_left, every, (1, -1)), rim(th, two_up, one_left, every, (1, -1)),
        rim(edge, one_up, two_left, lanes_e, (1, -1)),
        rim(te, two_down, two_right, every, (-1, 1)), rim(th, one_down, two_right, every, (-1, 1)),
        rim(edge, two_down, one_right, lanes_e, (-1, 1)),
        rim(te, one_down, one_left, every, (-1, -1)),
        rim(edge, one_down, one_left, lanes_e, (-1, -1)),
        rim(te, same_x, two_right, top_half, (0, 1)), rim(th, same_x, two_right, top_half, (0, 1)),
        rim(edge, same_x, one_right, lanes_e, (0, 1)),
        rim(te, same_x, two_left, top_half, (0, -1)), rim(th, same_x, one_left, top_half, (0, -1)),
        rim(edge, same_x, two_left, lanes_e, (0, -1)),
        rim(te, two_up, same_y, top_half, (1, 0)), rim(th, two_up, same_y, top_half, (1, 0)),
        rim(edge, one_up, same_y, lanes_e, (1, 0)),
        rim(te, two_down, same_y, top_half, (-1, 0)), rim(th, one_down, same_y, top_half, (-1, 0)),
        rim(edge, two_down, same_y, lanes_e, (-1, 0)),
    ]
    for c in early:
        c.start()
    late_x = [
        rim(te, two_up, same_y, low_half, (1, 0)), rim(th, two_up, same_y, low_half, (1, 0)),
        rim(te, two_down, same_y, low_half, (-1, 0)), rim(th, one_down, same_y, low_half, (-1, 0)),
    ]
    late_y = [
        rim(te, same_x, two_right, low_half, (0, 1)), rim(th, same_x, two_right, low_half, (0, 1)),
        rim(te, same_x, two_left, low_half, (0, -1)), rim(th, same_x, one_left, low_half, (0, -1)),
    ]

    for c in small[4:]:
        c.wait()
    rows, half = nx * own, wx // 2
    block = 2 * half * wy
    cells = ny * block
    count = orders.shape[1]
    row = lax.broadcasted_iota(jnp.int32, (rows, 1), 0)
    target = paired(i, nx - 1 - row // own, nx) * (ny * own) + j * own + row % own
    pick = ones_where(lax.broadcasted_iota(jnp.int32, (rows, count), 1) == target)
    pair = lax.dot_general(
        pick, orders[...].astype(jnp.float32).astype(jnp.bfloat16),
        (((1,), (1,)), ((), ())), preferred_element_type=jnp.float32,
    )
    cell = lax.broadcasted_iota(jnp.int32, (1, cells), 1)
    all_x, all_y = nx * wx, ny * wy
    all_cells = float(all_x * all_y)
    x_in = ((cell // (half * wy)) % 2) * wx + 2 * ((cell // wy) % half)
    x_at = (((i - core) * wx + x_in) * all_y).astype(jnp.float32)
    y_at = (((cell // block) * wy + cell % wy) * all_x).astype(jnp.float32)

    def waves(index):
        index = index - all_cells * jnp.round(index * (1.0 / all_cells))
        turn = index * (1.0 / all_cells)
        cosine = sine(0.25 - jnp.abs(turn))
        sines = sine(jnp.where(turn > 0.25, 0.5 - turn, jnp.where(turn < -0.25, -0.5 - turn, turn)))
        return cosine, sines

    part_rows = rows // 2
    for sine_rows, value in zip((0, part_rows), waves(pair[:, 0:1] * x_at + pair[:, 1:2] * y_at)):
        near, far = split(value)[:2]
        for k in range(ny):
            for q, part in enumerate((near, far, near)):
                for n in range(2):
                    place = 2 * n * part_rows + sine_rows
                    table[k, place:place + part_rows, q * block:(q + 1) * block] = part[
                        n * part_rows:(n + 1) * part_rows, k * block:(k + 1) * block
                    ]
    lower = lax.broadcasted_iota(jnp.int32, (rows, 2 * DIRS), 1) < DIRS
    turn_c, turn_s = waves(jnp.where(lower, 0.0, pair[:, 0:1] * float(all_y)))
    scale = 1.0 / math.sqrt(all_x * all_y)
    turn_c, turn_s = turn_c * scale, turn_s * scale

    span_l = (wx + 2 * REACH) * GROUP
    spot = lax.broadcasted_iota(jnp.int32, (1, span_l), 1)
    p = spot % GROUP
    x = spot // GROUP - REACH
    y = jnp.where(p < wy + REACH, p, p - rows_y)
    valid = (p < wy + REACH) | ((p >= rows_y - REACH) & (p < rows_y))
    side_x = jnp.where(x < 0, -1, jnp.where(x >= wx, 1, 0))
    side_y = jnp.where(y < 0, -1, jnp.where(y >= wy, 1, 0))
    lx, ly = x - side_x * wx, y - side_y * wy
    whole = jnp.where(side_x == 0, 0, jnp.where(side_x < 0, 1, 2)) * spots + lx * wy + ly
    which = jnp.where(side_x == 0, 0, jnp.where(side_x < 0, 2, 4)) + jnp.where(side_y > 0, 1, 0)
    strip = 3 * spots + which * GROUP + lx * 4 + jnp.where(ly < 2, ly, ly - (wy - 4))
    origin = jnp.where(valid, jnp.where(side_y == 0, whole, strip), -1)
    choice = ones_where(lax.broadcasted_iota(jnp.int32, (3 * spots + 256, span_l), 0) == origin)
    spread = ones_where(
        lax.broadcasted_iota(jnp.int32, (32, WIDE), 0) % 8 == lax.broadcasted_iota(jnp.int32, (32, WIDE), 1) // DIRS
    )

    for c in f_copies:
        c.wait()
    gathered_strips = []
    for first in (0, 4):
        groups = []
        for g in range(4):
            got = None
            for n in range(first, min(first + 4, 6)):
                v = strip_in[n]
                shift = (GROUP * (n - first - g)) % 128
                v = pltpu.roll(v, shift, 1) if shift else v
                got = v if got is None else jnp.where(lane // GROUP == n - first, v, got)
            groups.append(got)
        gathered_strips.append(jnp.concatenate(groups, 0))
    around = selected(
        jnp.concatenate([mine, block_in[0], block_in[1], *gathered_strips], 1), choice
    )
    pairs = [around[8 * g:8 * g + 8] for g in range(4)]
    fields = [f for v in pairs for f in (v, pltpu.roll(v, 4, 0))]
    f_e, f_h, kind, matter = fields[:3], fields[3:6], fields[6], fields[7]
    layer = sublanes_of((8, span_l))

    def f_next_x(f):
        return pltpu.roll(f, span_l - GROUP, 1)

    def f_prev_x(f):
        return pltpu.roll(f, GROUP, 1)

    def f_next_y(f):
        return jnp.where(p == rows_y - 1, pltpu.roll(f, rows_y - 1, 1), pltpu.roll(f, span_l - 1, 1))

    def f_prev_y(f):
        return jnp.where(p == 0, pltpu.roll(f, span_l - rows_y + 1, 1), pltpu.roll(f, 1, 1))

    def f_next_z(f):
        return jnp.where(layer < LAYERS - 1, pltpu.roll(f, 7, 0), 0.0)

    def f_prev_z(f):
        return jnp.where(layer >= 1, pltpu.roll(f, 1, 0), 0.0)

    eps = jnp.full((8, span_l), permittivity[0])
    slope = jnp.full((8, span_l), contrast[0])
    for k in range(1, permittivity.shape[0]):
        eps = jnp.where(matter == float(k), permittivity[k], eps)
        slope = jnp.where(matter == float(k), contrast[k], slope)
    ratio = time_step / eps
    coef = time_step * slope / (eps * eps)
    sources = []
    for step in range(STEPS):
        curl = curl_f(f_e, lambda c: f_next_x(f_e[c]), f_next_y, f_next_z)
        f_h = [f_h[c] - time_step * curl[c] for c in range(3)]
        curl = curl_b(f_h, lambda c: f_prev_x(f_h[c]), f_prev_y, f_prev_z)
        sources.append([coef * curl[c] for c in range(3)])
        f_e = [f_e[c] + ratio * curl[c] for c in range(3)]

    def wide(v, exact=True):
        v = jnp.where(layer < LAYERS, v, 0.0)
        zero = jnp.zeros_like(v)
        parts = stacked(v) + [zero] if exact else [v, zero, zero, zero]
        return lax.dot_general(
            jnp.concatenate(parts, 0).astype(jnp.bfloat16), spread, (((0,), (0,)), ((), ())),
            preferred_element_type=jnp.float32,
        )

    hot = wide(kind, False) == (lax.broadcasted_iota(jnp.int32, (1, WIDE), 1) % DIRS).astype(jnp.float32)
    v = wide(ratio)
    for x in range(1, wx + 3):
        inverse[x] = v[GROUP * x:GROUP * x + rows_y]
    for c in range(3):
        v = jnp.where(hot, wide(sources[0][c]), 0.0)
        for x in range(1, wx + 3):
            source_1[c, x] = v[GROUP * x:GROUP * x + rows_y]
        v = jnp.where(hot, wide(sources[1][c]), 0.0)
        for x in range(wx):
            source_2[c, x] = v[GROUP * (x + REACH):GROUP * (x + REACH) + wy]

    for c in early:
        c.wait()
    for c in late_x:
        c.start()

    def h_first(x):
        f = [te[c, x, :, high] for c in range(3)]
        curl = curl_f(f, lambda c: te[c, x + 1, :, high], next_y, next_z)
        for c in range(3):
            h_1[c, x] = th[c, x, :, high] - time_step * curl[c]

    def e_first(x):
        hx, hy, hz = [h_1[c, x] for c in range(3)]
        below = edge[0, x] + time_step * jnp.where(left_half, -next_y(edge[1, x]), edge[1, x + 1])
        below_x = jnp.where(left_half, below, other_layer(hx))
        below_y = other_layer(jnp.where(left_half, hy, below))
        curl = (
            (hz - prev_y(hz)) - (hy - below_y),
            (hx - below_x) - (hz - h_1[2, x - 1]),
            (hy - h_1[1, x - 1]) - (hx - prev_y(hx)),
        )
        ratio = inverse[x, :, high]
        for c in range(3):
            e_1[c, x] = te[c, x, :, high] + ratio * curl[c] - source_1[c, x, :, high]

    def h_second(x):
        curl = curl_f([e_1[c, x] for c in range(3)], lambda c: e_1[c, x + 1], next_y, next_z)
        for c in range(3):
            h_2[c, x] = h_1[c, x] - time_step * curl[c]

    def e_second(x, curl, comps, lanes, e):
        ratio = inverse[x, :wy, lanes]
        return [e(c) + ratio * curl[c][:wy] - source_2[c, x - x0, :, lanes] for c in range(comps)]

    def top_of(x):
        curl = curl_b([h_2[c, x] for c in range(3)], lambda c: h_2[c, x - 1], prev_y, prev_z)
        return e_second(x, curl, 2, high, lambda c: e_1[c, x, :wy])

    h_first(0)
    h_first(1)
    e_first(1)
    h_first(2)
    e_first(2)
    h_second(1)

    def top_pairs(first, last):
        for u in range(first, last):
            got = []
            for x in (2 * u + 3, 2 * u + 4):
                h_first(x)
                e_first(x)
                h_second(x - 1)
                got.append(top_of(x - 1))
            for q in range(2):
                tops[q, u * wy:(u + 1) * wy] = jnp.where(left_half, other_layer(got[0][q]), got[1][q])

    copies = []
    parts = 2
    for part in range(parts):
        first, last = part * half // parts, (part + 1) * half // parts
        top_pairs(first, last)
        span = pl.ds(first * wy, (last - first) * wy)
        for k in reversed(range(len(sheet))):
            to = mate if k % 2 == 0 else i
            q = 1 - core if k % 2 == 0 else core
            n = part * len(sheet) + k
            c = copy(
                tops.at[q, span], gathered.at[(k + 1) // 2, core, span], g_send.at[n], g_recv.at[n], (to, sheet[k][1])
            )
            c.start()
            copies.append(((k + 1) // 2, c))

    gathered[0, core] = tops[core]

    def top_parts(k):
        for at_k, c in copies:
            if at_k == k:
                c.wait_recv()
        near, far = split(gathered[k].reshape(block, 2 * DIRS))[:2]
        return jnp.concatenate([near, near, far], 0)

    def product(k, v, span):
        return jnp.dot(table[paired(j, k, ny), span], v, preferred_element_type=jnp.float32)

    spans = [slice(0, rows), slice(rows, 2 * rows)]
    sums = [0.0, 0.0]
    for k in range(ny):
        v = top_parts(k)
        if k < ny - 1:
            sums = [sums[n] + product(k, v, spans[n]) for n in range(2)]
    for c in late_y:
        c.start()
    out = []
    for n in range(2):
        total = sums[n] + product(ny - 1, v, spans[n])
        cosines, sines = total[:part_rows], total[part_rows:]
        mine = slice(n * part_rows, (n + 1) * part_rows)
        real = cosines * turn_c[mine] - sines * turn_s[mine]
        imag = sines * turn_c[mine] + cosines * turn_s[mine]
        real = real + pltpu.roll(real, DIRS, 1)
        imag = imag + pltpu.roll(imag, DIRS, 1)
        both = jnp.where(lower[mine], real, -imag)
        partial[n * nx // 2:(n + 1) * nx // 2] = both.reshape(nx // 2, own, 2 * DIRS)
        for b in range(n * nx // 2, (n + 1) * nx // 2):
            k = nx - 1 - b
            if k:
                c = copy(partial.at[b], arrived.at[k], p_send.at[k], p_recv.at[k], line[k - 1])
                c.start()
                out.append((k, c))
    for c in late_x + late_y:
        c.wait()

    def low_h_first(x):
        f = [te[c, x, :, low] for c in range(3)]

        def nz(c):
            return other_layer(jnp.where(left_half, te[c, x, :, high], f[c]))

        fx, fy, fz = f
        curl = (
            (next_y(fz) - fz) - (nz(1) - fy),
            (nz(0) - fx) - (te[2, x + 1, :, low] - fz),
            (te[1, x + 1, :, low] - fy) - (next_y(fx) - fx),
        )
        for c in range(3):
            th[c, x, :, low] = th[c, x, :, low] - time_step * curl[c]

    def low_e_first(x):
        g = [th[c, x, :, low] for c in range(3)]
        curl = curl_b(g, lambda c: th[c, x - 1, :, low], prev_y, prev_z)
        ratio = inverse[x, :, low]
        for c in range(3):
            te[c, x, :, low] = te[c, x, :, low] + ratio * curl[c] - source_1[c, x, :, low]

    def low_h_second(x):
        f = [te[c, x, :, low] for c in range(3)]

        def nz(c):
            return other_layer(jnp.where(left_half, e_1[c, x], f[c]))

        fx, fy, fz = f
        curl = (
            (next_y(fz) - fz) - (nz(1) - fy),
            (nz(0) - fx) - (te[2, x + 1, :, low] - fz),
            (te[1, x + 1, :, low] - fy) - (next_y(fx) - fx),
        )
        for c in range(3):
            th[c, x, :, low] = th[c, x, :, low] - time_step * curl[c]

    def rest(u, carry):
        x = u + 2
        low_h_first(x + 1)
        low_e_first(x + 1)
        low_h_second(x)
        g = [th[c, x, :, low] for c in range(3)]
        curl = curl_b(g, lambda c: th[c, x - 1, :, low], prev_y, prev_z)
        new = e_second(x, curl, 3, low, lambda c: te[c, x, :wy, low])
        hx, hy, hz = [h_2[c, x] for c in range(3)]
        below_x = other_layer(jnp.where(left_half, hx, g[0]))
        below_y = other_layer(jnp.where(left_half, hy, g[1]))
        curl = (
            (hz - prev_y(hz)) - (hy - below_y),
            (hx - below_x) - (hz - h_2[2, x - 1]),
            (hy - h_2[1, x - 1]) - (hx - prev_y(hx)),
        )
        above = e_second(x, curl, 3, high, lambda c: e_1[c, x, :wy])
        for c in range(3):
            out_e[c, u, :, low] = new[c]
            out_e[c, u, :, high] = above[c]
            out_h[c, u, :, low] = g[c][:wy]
            out_h[c, u, :, high] = h_2[c, x, :wy]
        return carry

    low_h_first(0)
    low_h_first(1)
    low_e_first(1)
    low_h_first(2)
    low_e_first(2)
    low_h_second(1)
    lax.fori_loop(0, wx, rest, 0, unroll=True)

    totals = [partial[nx - 1], None]
    for k, c in out[::-1]:
        c.wait_recv()
        totals[k % 2] = arrived[k] if totals[k % 2] is None else totals[k % 2] + arrived[k]
    out_s[:, :2 * DIRS] = jnp.where(core == 0, totals[0], totals[1])
    out_s[:, 2 * DIRS:] = jnp.where(core == 0, totals[1], totals[0])
    for _, c in copies + out:
        c.wait_send()


def hand_over(from_e, from_h, from_s, to_e, to_h, to_s, sem):
    copies = [
        pltpu.make_async_copy(src, dst, sem.at[k])
        for k, (src, dst) in enumerate(((from_e, to_e), (from_h, to_h), (from_s, to_s)))
    ]
    for c in copies:
        c.start()
    for c in copies:
        c.wait()


def local(nx, ny, te, th, fe, fh, classes, material, permittivity, contrast, orders):
    wx, wy = te.shape[1], te.shape[2]
    own = orders.shape[0] // (nx * ny)
    rows = nx * own
    f32 = jnp.float32
    vmem = pl.BlockSpec(memory_space=pltpu.VMEM)
    hbm = pl.BlockSpec(memory_space=pltpu.HBM)
    args = (
        te, th, jnp.transpose(fe, (0, 1, 3, 2)), jnp.transpose(fh, (0, 1, 3, 2)),
        jnp.transpose(classes, (0, 2, 1)), jnp.transpose(material, (0, 2, 1)),
        permittivity, contrast, jnp.transpose(orders),
    )
    args = tuple(pltpu.with_memory_space_constraint(v, pltpu.HBM) for v in args)
    out_shape = (
        jax.ShapeDtypeStruct(te.shape, f32),
        jax.ShapeDtypeStruct(th.shape, f32),
        jax.ShapeDtypeStruct((own, 4 * DIRS), f32),
    )
    wide_x, wide_y = wx + 2 * REACH, wy + PAD

    def pair_of(n):
        return [pltpu.SemaphoreType.DMA((n,))] * 2

    results = pl.pallas_call(
        functools.partial(kernel, nx, ny, own),
        out_shape=out_shape,
        in_specs=[hbm] * 9,
        out_specs=(vmem, vmem, vmem),
        scratch_shapes=[
            *[pltpu.VMEM((3, wide_x, wide_y, WIDE), f32)] * 2,
            pltpu.VMEM((2, wide_x, wide_y, HALF), f32),
            *[pltpu.VMEM((3, wide_x, wide_y, HALF), f32)] * 3,
            pltpu.VMEM((3, wide_x, wide_y, WIDE), f32),
            pltpu.VMEM((3, wx, wy, WIDE), f32),
            pltpu.VMEM((wide_x, wide_y, WIDE), f32),
            pltpu.VMEM((32, wx * wy), f32), pltpu.VMEM((2, 32, wx * wy), f32),
            pltpu.VMEM((8, 128), f32), pltpu.VMEM((6, 8, 128), f32),
            pltpu.VMEM((2, wx // 2 * wy, 2 * DIRS), f32),
            pltpu.VMEM((ny, 2, wx // 2 * wy, 2 * DIRS), f32),
            *[pltpu.VMEM((nx, own, 2 * DIRS), f32)] * 2,
            pltpu.VMEM((ny, 2 * rows, 3 * wx * wy), jnp.bfloat16),
            *pair_of(31), *pair_of(8), *pair_of(4 * ny), *pair_of(nx),
            *[pltpu.VMEM(v.shape, v.dtype) for v in args[2:6]],
            *[pltpu.SMEM(v.shape, v.dtype) for v in args[6:8]],
            pltpu.VMEM(args[8].shape, args[8].dtype),
            pltpu.SemaphoreType.DMA((13,)),
        ],
        compiler_params=pltpu.CompilerParams(
            collective_id=0, has_side_effects=True, vmem_limit_bytes=48 * 1024 * 1024
        ),
        name="slab",
    )(*args)
    return pl.pallas_call(
        hand_over,
        out_shape=out_shape,
        in_specs=[vmem] * 3,
        out_specs=(hbm, hbm, hbm),
        scratch_shapes=[pltpu.SemaphoreType.DMA((3,))],
        compiler_params=pltpu.CompilerParams(vmem_limit_bytes=16 * 1024 * 1024),
        name="hand_over",
    )(*results)


def solution(mesh):
    in_specs = (
        P(None, "gx", "gy", None),
        P(None, "gx", "gy", None),
        P(None, "gx", "gy", None),
        P(None, "gx", "gy", None),
        P("gx", "gy", None),
        P("gx", "gy", None),
        P(),
        P(),
        P(),
    )
    out_specs = (P(None, "gx", "gy", None), P(None, "gx", "gy", None), P(("gx", "gy"), None))
    body = functools.partial(local, mesh.shape["gx"], mesh.shape["gy"])
    return jax.shard_map(body, mesh=mesh, in_specs=in_specs, out_specs=out_specs, check_vma=False)
```

```python
import functools
import math

import jax
import jax.numpy as jnp
from jax import lax
from jax.experimental import pallas as pl
from jax.experimental.pallas import tpu as pltpu
from jax.sharding import PartitionSpec as P

DIRS = 64
STEPS = 2
LAYERS = 4
WIDE = LAYERS * DIRS
HALF = WIDE // 2
time_step = 0.5


REACH = 2
PAD = 8
GROUP = 32


def lanes_of(shape):
    return lax.broadcasted_iota(jnp.int32, shape, len(shape) - 1)


def sublanes_of(shape):
    return lax.broadcasted_iota(jnp.int32, shape, len(shape) - 2)


def next_y(f):
    return pltpu.roll(f, f.shape[0] - 1, 0)


def prev_y(f):
    return pltpu.roll(f, 1, 0)


def next_z(f):
    wide = f.shape[-1]
    return jnp.where(lanes_of(f.shape) < wide - DIRS, pltpu.roll(f, wide - DIRS, 1), 0.0)


def prev_z(f):
    return jnp.where(lanes_of(f.shape) >= DIRS, pltpu.roll(f, DIRS, 1), 0.0)


def curl_f(f, x_next, ny, nz):
    fx, fy, fz = f
    return (
        (ny(fz) - fz) - (nz(fy) - fy),
        (nz(fx) - fx) - (x_next(2) - fz),
        (x_next(1) - fy) - (ny(fx) - fx),
    )


def curl_b(f, x_prev, py, pz):
    fx, fy, fz = f
    return (
        (fz - py(fz)) - (fy - pz(fy)),
        (fx - pz(fx)) - (fz - x_prev(2)),
        (fy - x_prev(1)) - (fx - py(fx)),
    )


def sine(turn):
    u = turn * (2.0 * math.pi)
    s = u * u
    poly = -1.0 / 39916800.0
    for c in (1.0 / 362880.0, -1.0 / 5040.0, 1.0 / 120.0, -1.0 / 6.0):
        poly = poly * s + c
    return u + u * (s * poly)


def split(v):
    parts = []
    for _ in range(3):
        parts.append(v.astype(jnp.bfloat16))
        v = v - parts[-1].astype(jnp.float32)
    return parts


def stacked(v):
    parts = [part.astype(jnp.float32) for part in split(v)]
    return parts


def selected(v, choice):
    n = v.shape[0]
    parts = stacked(v)
    if 3 * n % 16:
        parts.append(jnp.zeros_like(v))
    got = jnp.dot(
        jnp.concatenate(parts, 0).astype(jnp.bfloat16), choice, preferred_element_type=jnp.float32
    )
    return got[:n] + got[n:2 * n] + got[2 * n:3 * n]


def ones_where(hit):
    return hit.astype(jnp.float32).astype(jnp.bfloat16)


def paired(n, k, size):
    out, bit = 0, 1
    while bit < size:
        out = out + bit * ((n // bit + k // bit) % 2)
        bit *= 2
    return out


def kernel(
    nx, ny, own,
    te_at, th_at, fe_at, fh_at, classes_at, material_at, permittivity_at, contrast_at, orders_at,
    out_e, out_h, out_s,
    te, th, edge, h_1, e_1, h_2, source_1, source_2, inverse, block_out, block_in, strip_out, strip_in,
    tops, gathered, partial, arrived, table,
    rim_send, rim_recv, f_send, f_recv, g_send, g_recv, p_send, p_recv,
    fe, fh, classes, material, permittivity, contrast, orders, load,
):
    wx, wy = te_at.shape[1], te_at.shape[2]
    rows_y = te.shape[2]
    inside = (pl.ds(REACH, wx), pl.ds(0, wy))
    i, j = lax.axis_index("gx"), lax.axis_index("gy")
    core = lax.rem(i, 2)
    mate = i + 1 - 2 * core
    beyond = lax.rem(i + nx - 1 + 2 * core, nx)

    def at(dx, dy):
        return (lax.rem(i + nx + dx, nx), lax.rem(j + ny + dy, ny))

    line = [(paired(i, k, nx), j) for k in range(1, nx)]
    sheet = [(mate, j)] + [(n, paired(j, k, ny)) for k in range(1, ny) for n in (i, mate)]
    left, right = at(0, -1)[1], at(0, 1)[1]
    peers = [(beyond, left), (beyond, right), (beyond, j)] + sheet[1:] + line
    barrier = pltpu.get_barrier_semaphore()
    for peer in peers:
        pl.semaphore_signal(barrier, inc=1, device_id=peer, device_id_type=pl.DeviceIdType.MESH)

    def copy(src, dst, send, recv, device):
        return pltpu.make_async_remote_copy(
            src_ref=src, dst_ref=dst, send_sem=send, recv_sem=recv,
            device_id=device, device_id_type=pl.DeviceIdType.MESH,
        )

    small = [
        pltpu.make_async_copy(src, dst, load.at[6 + k])
        for k, (src, dst) in enumerate((
            (fe_at, fe), (fh_at, fh), (classes_at, classes), (material_at, material),
            (permittivity_at, permittivity), (contrast_at, contrast), (orders_at, orders),
        ))
    ]
    large = [
        pltpu.make_async_copy(src.at[c], dst.at[(c, *inside)], load.at[2 * c + k])
        for c in range(3) for k, (src, dst) in enumerate(((te_at, te), (th_at, th)))
    ]
    for c in small[:4] + large + small[4:]:
        c.start()

    spots = wx * wy
    lane = lax.broadcasted_iota(jnp.int32, (1, 128), 1)
    group, in_group = lane // GROUP, lane % GROUP
    k = in_group % 4
    from_lane = group * spots + (in_group // 4) * wy + jnp.where(k < 2, k, wy - 4 + k)
    strip_choice = ones_where(lax.broadcasted_iota(jnp.int32, (4 * spots, 128), 0) == from_lane)
    for c in small[:4]:
        c.wait()
    for x in range(wx):
        cells = slice(x * wy, (x + 1) * wy)
        for c in range(3):
            block_out[4 * c:4 * c + 4, cells] = fe[c, x]
            block_out[12 + 4 * c:16 + 4 * c, cells] = fh[c, x]
        block_out[24:28, cells] = classes[x].astype(jnp.float32)
        block_out[28:32, cells] = material[x].astype(jnp.float32)
    mine = block_out[...]
    strip_out[...] = selected(jnp.concatenate([mine[8 * g:8 * g + 8] for g in range(4)], 1), strip_choice)

    pl.semaphore_wait(barrier, len(peers))
    strips = [(0, -1), (0, 1), (-1, -1), (-1, 1), (1, -1), (1, 1)]
    f_copies = []
    for n, (dx, dy) in enumerate(strips):
        f_copies.append(copy(strip_out, strip_in.at[n], f_send.at[n], f_recv.at[n], at(-dx, -dy)))
    for n, dx in enumerate((-1, 1)):
        f_copies.append(copy(block_out, block_in.at[n], f_send.at[6 + n], f_recv.at[6 + n], at(-dx, 0)))
    for c in f_copies[2:] + f_copies[:2]:
        c.start()

    every, top_half, low_half = pl.ds(0, WIDE), pl.ds(HALF, HALF), pl.ds(0, HALF)
    low, high = slice(0, HALF), slice(HALF, WIDE)
    left_half = lax.broadcasted_iota(jnp.int32, (1, HALF), 1) < DIRS
    x0, x1 = REACH, REACH + wx
    same_x, same_y = (pl.ds(x0, wx),) * 2, (pl.ds(0, wy),) * 2
    r_copies = []

    def moved(source, target, n):
        return pl.ds(source, n), pl.ds(target, n)

    def rim(f, x, y, lanes, side):
        (sx, tx), (sy, ty) = x, y
        n = len(r_copies)
        c = copy(
            f.at[:, sx, sy, lanes], f.at[:, tx, ty, lanes], rim_send.at[n], rim_recv.at[n], at(*side)
        )
        r_copies.append(c)
        return c

    def other_layer(v):
        return pltpu.roll(v, DIRS, 1)

    for c in large:
        c.wait()
    for x in range(x0, x1):
        ex, ey, ez = [te[c, x, :wy, low] for c in range(3)]
        part_x = th[0, x, :wy, low] + time_step * (ez + (other_layer(te[1, x, :wy, high]) - ey))
        part_y = th[1, x, :wy, low] - time_step * ((other_layer(te[0, x, :wy, high]) - ex) + ez)
        edge[0, x, :wy] = jnp.where(left_half, other_layer(part_x), part_y)
        edge[1, x, :wy] = jnp.where(left_half, other_layer(ez), ez)
    one_up, two_up = moved(x1 - 1, 1, 1), moved(x1 - 2, 0, 2)
    one_down, two_down = moved(x0, x1, 1), moved(x0, x1, 2)
    one_right, two_right = moved(wy - 1, rows_y - 1, 1), moved(wy - 2, rows_y - 2, 2)
    one_left, two_left = moved(0, wy, 1), moved(0, wy, 2)
    lanes_e = pl.ds(0, HALF)
    early = [
        rim(te, one_up, one_right, every, (1, 1)), rim(th, one_up, one_right, every, (1, 1)),
        rim(edge, one_up, one_right, lanes_e, (1, 1)),
        rim(te, two_up, two_left, every, (1, -1)), rim(th, two_up, one_left, every, (1, -1)),
        rim(edge, one_up, two_left, lanes_e, (1, -1)),
        rim(te, two_down, two_right, every, (-1, 1)), rim(th, one_down, two_right, every, (-1, 1)),
        rim(edge, two_down, one_right, lanes_e, (-1, 1)),
        rim(te, one_down, one_left, every, (-1, -1)),
        rim(edge, one_down, one_left, lanes_e, (-1, -1)),
        rim(te, same_x, two_right, top_half, (0, 1)), rim(th, same_x, two_right, top_half, (0, 1)),
        rim(edge, same_x, one_right, lanes_e, (0, 1)),
        rim(te, same_x, two_left, top_half, (0, -1)), rim(th, same_x, one_left, top_half, (0, -1)),
        rim(edge, same_x, two_left, lanes_e, (0, -1)),
        rim(te, two_up, same_y, top_half, (1, 0)), rim(th, two_up, same_y, top_half, (1, 0)),
        rim(edge, one_up, same_y, lanes_e, (1, 0)),
        rim(te, two_down, same_y, top_half, (-1, 0)), rim(th, one_down, same_y, top_half, (-1, 0)),
        rim(edge, two_down, same_y, lanes_e, (-1, 0)),
    ]
    for c in early:
        c.start()
    late_x = [
        rim(te, two_up, same_y, low_half, (1, 0)), rim(th, two_up, same_y, low_half, (1, 0)),
        rim(te, two_down, same_y, low_half, (-1, 0)), rim(th, one_down, same_y, low_half, (-1, 0)),
    ]
    late_y = [
        rim(te, same_x, two_right, low_half, (0, 1)), rim(th, same_x, two_right, low_half, (0, 1)),
        rim(te, same_x, two_left, low_half, (0, -1)), rim(th, same_x, one_left, low_half, (0, -1)),
    ]

    for c in small[4:]:
        c.wait()
    rows, half = nx * own, wx // 2
    block = 2 * half * wy
    cells = ny * block
    count = orders.shape[1]
    row = lax.broadcasted_iota(jnp.int32, (rows, 1), 0)
    target = paired(i, nx - 1 - row // own, nx) * (ny * own) + j * own + row % own
    pick = ones_where(lax.broadcasted_iota(jnp.int32, (rows, count), 1) == target)
    pair = lax.dot_general(
        pick, orders[...].astype(jnp.float32).astype(jnp.bfloat16),
        (((1,), (1,)), ((), ())), preferred_element_type=jnp.float32,
    )
    cell = lax.broadcasted_iota(jnp.int32, (1, cells), 1)
    all_x, all_y = nx * wx, ny * wy
    all_cells = float(all_x * all_y)
    inner_pairs, inner = half - 2, wy - 2 * REACH
    spot_in = cell % (half * wy)
    tail = inner_pairs * inner
    edge_rows = spot_in - tail
    outer = edge_rows - inner_pairs * 2 * REACH
    inner_u = jnp.zeros_like(cell)
    for n in range(1, inner_pairs):
        inner_u = inner_u + jnp.where(spot_in >= n * inner, 1, 0)
    pair_u = jnp.where(spot_in < tail, 1 + inner_u, jnp.where(
        outer < 0, 1 + edge_rows // (2 * REACH), jnp.where(outer < wy, 0, half - 1)))
    y_in = jnp.where(spot_in < tail, REACH + spot_in - inner * inner_u, jnp.where(
        outer < 0, (wy - REACH + edge_rows % (2 * REACH)) % wy, outer % wy))
    x_in = ((cell // (half * wy)) % 2) * wx + 2 * pair_u
    x_at = (((i - core) * wx + x_in) * all_y).astype(jnp.float32)
    y_at = (((cell // block) * wy + y_in) * all_x).astype(jnp.float32)

    def waves(index):
        index = index - all_cells * jnp.round(index * (1.0 / all_cells))
        turn = index * (1.0 / all_cells)
        cosine = sine(0.25 - jnp.abs(turn))
        sines = sine(jnp.where(turn > 0.25, 0.5 - turn, jnp.where(turn < -0.25, -0.5 - turn, turn)))
        return cosine, sines

    part_rows = rows // 2
    for sine_rows, value in zip((0, part_rows), waves(pair[:, 0:1] * x_at + pair[:, 1:2] * y_at)):
        near, far = split(value)[:2]
        for k in range(ny):
            for q, part in enumerate((near, far, near)):
                for n in range(2):
                    place = 2 * n * part_rows + sine_rows
                    table[k, place:place + part_rows, q * block:(q + 1) * block] = part[
                        n * part_rows:(n + 1) * part_rows, k * block:(k + 1) * block
                    ]
    lower = lax.broadcasted_iota(jnp.int32, (rows, 2 * DIRS), 1) < DIRS
    turn_c, turn_s = waves(jnp.where(lower, 0.0, pair[:, 0:1] * float(all_y)))
    scale = 1.0 / math.sqrt(all_x * all_y)
    turn_c, turn_s = turn_c * scale, turn_s * scale

    span_l = (wx + 2 * REACH) * GROUP
    spot = lax.broadcasted_iota(jnp.int32, (1, span_l), 1)
    p = spot % GROUP
    x = spot // GROUP - REACH
    y = jnp.where(p < wy + REACH, p, p - rows_y)
    valid = (p < wy + REACH) | ((p >= rows_y - REACH) & (p < rows_y))
    side_x = jnp.where(x < 0, -1, jnp.where(x >= wx, 1, 0))
    side_y = jnp.where(y < 0, -1, jnp.where(y >= wy, 1, 0))
    lx, ly = x - side_x * wx, y - side_y * wy
    whole = jnp.where(side_x == 0, 0, jnp.where(side_x < 0, 1, 2)) * spots + lx * wy + ly
    which = jnp.where(side_x == 0, 0, jnp.where(side_x < 0, 2, 4)) + jnp.where(side_y > 0, 1, 0)
    strip = 3 * spots + which * GROUP + lx * 4 + jnp.where(ly < 2, ly, ly - (wy - 4))
    origin = jnp.where(valid, jnp.where(side_y == 0, whole, strip), -1)
    choice = ones_where(lax.broadcasted_iota(jnp.int32, (3 * spots + 256, span_l), 0) == origin)
    spread = ones_where(
        lax.broadcasted_iota(jnp.int32, (32, WIDE), 0) % 8 == lax.broadcasted_iota(jnp.int32, (32, WIDE), 1) // DIRS
    )

    for c in f_copies:
        c.wait()
    gathered_strips = []
    for first in (0, 4):
        groups = []
        for g in range(4):
            got = None
            for n in range(first, min(first + 4, 6)):
                v = strip_in[n]
                shift = (GROUP * (n - first - g)) % 128
                v = pltpu.roll(v, shift, 1) if shift else v
                got = v if got is None else jnp.where(lane // GROUP == n - first, v, got)
            groups.append(got)
        gathered_strips.append(jnp.concatenate(groups, 0))
    around = selected(
        jnp.concatenate([mine, block_in[0], block_in[1], *gathered_strips], 1), choice
    )
    pairs = [around[8 * g:8 * g + 8] for g in range(4)]
    fields = [f for v in pairs for f in (v, pltpu.roll(v, 4, 0))]
    f_e, f_h, kind, matter = fields[:3], fields[3:6], fields[6], fields[7]
    layer = sublanes_of((8, span_l))

    def f_next_x(f):
        return pltpu.roll(f, span_l - GROUP, 1)

    def f_prev_x(f):
        return pltpu.roll(f, GROUP, 1)

    def f_next_y(f):
        return jnp.where(p == rows_y - 1, pltpu.roll(f, rows_y - 1, 1), pltpu.roll(f, span_l - 1, 1))

    def f_prev_y(f):
        return jnp.where(p == 0, pltpu.roll(f, span_l - rows_y + 1, 1), pltpu.roll(f, 1, 1))

    def f_next_z(f):
        return jnp.where(layer < LAYERS - 1, pltpu.roll(f, 7, 0), 0.0)

    def f_prev_z(f):
        return jnp.where(layer >= 1, pltpu.roll(f, 1, 0), 0.0)

    eps = jnp.full((8, span_l), permittivity[0])
    slope = jnp.full((8, span_l), contrast[0])
    for k in range(1, permittivity.shape[0]):
        eps = jnp.where(matter == float(k), permittivity[k], eps)
        slope = jnp.where(matter == float(k), contrast[k], slope)
    ratio = time_step / eps
    coef = time_step * slope / (eps * eps)
    sources = []
    for step in range(STEPS):
        curl = curl_f(f_e, lambda c: f_next_x(f_e[c]), f_next_y, f_next_z)
        f_h = [f_h[c] - time_step * curl[c] for c in range(3)]
        curl = curl_b(f_h, lambda c: f_prev_x(f_h[c]), f_prev_y, f_prev_z)
        sources.append([coef * curl[c] for c in range(3)])
        f_e = [f_e[c] + ratio * curl[c] for c in range(3)]

    def wide(v, exact=True):
        v = jnp.where(layer < LAYERS, v, 0.0)
        zero = jnp.zeros_like(v)
        parts = stacked(v) + [zero] if exact else [v, zero, zero, zero]
        return lax.dot_general(
            jnp.concatenate(parts, 0).astype(jnp.bfloat16), spread, (((0,), (0,)), ((), ())),
            preferred_element_type=jnp.float32,
        )

    hot = wide(kind, False) == (lax.broadcasted_iota(jnp.int32, (1, WIDE), 1) % DIRS).astype(jnp.float32)
    v = wide(ratio)
    for x in range(1, wx + 3):
        inverse[x] = v[GROUP * x:GROUP * x + rows_y]
    for c in range(3):
        v = jnp.where(hot, wide(sources[0][c]), 0.0)
        for x in range(1, wx + 3):
            source_1[c, x] = v[GROUP * x:GROUP * x + rows_y]
        v = jnp.where(hot, wide(sources[1][c]), 0.0)
        for x in range(wx):
            source_2[c, x] = v[GROUP * (x + REACH):GROUP * (x + REACH) + wy]

    def h_first(x, rows):
        f = [te[c, x, rows, high] for c in range(3)]
        curl = curl_f(f, lambda c: te[c, x + 1, rows, high], next_y, next_z)
        for c in range(3):
            h_1[c, x, rows] = th[c, x, rows, high] - time_step * curl[c]

    def e_first(x, rows):
        hx, hy, hz = [h_1[c, x, rows] for c in range(3)]
        below = edge[0, x, rows] + time_step * jnp.where(left_half, -next_y(edge[1, x, rows]), edge[1, x + 1, rows])
        below_x = jnp.where(left_half, below, other_layer(hx))
        below_y = other_layer(jnp.where(left_half, hy, below))
        curl = (
            (hz - prev_y(hz)) - (hy - below_y),
            (hx - below_x) - (hz - h_1[2, x - 1, rows]),
            (hy - h_1[1, x - 1, rows]) - (hx - prev_y(hx)),
        )
        ratio = inverse[x, rows, high]
        for c in range(3):
            e_1[c, x, rows] = te[c, x, rows, high] + ratio * curl[c] - source_1[c, x, rows, high]

    def h_second(x, rows):
        curl = curl_f([e_1[c, x, rows] for c in range(3)], lambda c: e_1[c, x + 1, rows], next_y, next_z)
        for c in range(3):
            h_2[c, x, rows] = h_1[c, x, rows] - time_step * curl[c]

    def e_second(x, curl, comps, lanes, e):
        ratio = inverse[x, :wy, lanes]
        return [e(c) + ratio * curl[c][:wy] - source_2[c, x - x0, :, lanes] for c in range(comps)]

    def top_of(x, rows):
        curl = curl_b([h_2[c, x, rows] for c in range(3)], lambda c: h_2[c, x - 1, rows], prev_y, prev_z)
        return e_second(x, curl, 2, high, lambda c: e_1[c, x, :wy])

    copies = []

    def send_tops(first, last):
        span = pl.ds(first, last - first)
        for k in reversed(range(len(sheet))):
            to = mate if k % 2 == 0 else i
            q = 1 - core if k % 2 == 0 else core
            n = len(copies)
            c = copy(
                tops.at[q, span], gathered.at[(k + 1) // 2, core, span], g_send.at[n], g_recv.at[n], (to, sheet[k][1])
            )
            c.start()
            copies.append(((k + 1) // 2, c))

    def keep_top(u, got, inside):
        for q in range(2):
            v = jnp.where(left_half, other_layer(got[0][q]), got[1][q])
            if 0 < u < half - 1:
                v = pltpu.roll(v, wy - REACH, 0)
                if inside:
                    tops[q, (u - 1) * inner:u * inner] = v[:inner]
                else:
                    to = tail + (u - 1) * 2 * REACH
                    tops[q, to:to + 2 * REACH] = v[inner:]
            else:
                to = (half - 2) * wy + (wy if u else 0)
                tops[q, to:to + wy] = v

    mine_only = slice(0, wy)
    h_first(x0, mine_only)
    h_first(x0 + 1, mine_only)
    e_first(x0 + 1, mine_only)
    got = []
    for x in range(x0 + 2, x1 - 1):
        h_first(x, mine_only)
        e_first(x, mine_only)
        h_second(x - 1, mine_only)
        if x > x0 + 2:
            got.append(top_of(x - 1, mine_only))
    for u in range(1, half - 1):
        keep_top(u, got[2 * u - 2:2 * u], True)
    send_tops(0, tail)

    for c in early:
        c.wait()
    for c in late_x:
        c.start()

    every_row = slice(0, rows_y)
    h_first(0, every_row)
    h_first(1, every_row)
    e_first(1, every_row)
    h_first(2, every_row)
    e_first(2, every_row)
    h_second(1, every_row)
    for u in range(half):
        got = []
        for x in (2 * u + 3, 2 * u + 4):
            h_first(x, every_row)
            e_first(x, every_row)
            h_second(x - 1, every_row)
            got.append(top_of(x - 1, every_row))
        keep_top(u, got, False)
    send_tops(tail, half * wy)

    gathered[0, core] = tops[core]

    def top_parts(k):
        for at_k, c in copies:
            if at_k == k:
                c.wait_recv()
        near, far = split(gathered[k].reshape(block, 2 * DIRS))[:2]
        return jnp.concatenate([near, near, far], 0)

    def product(k, v, span):
        return jnp.dot(table[paired(j, k, ny), span], v, preferred_element_type=jnp.float32)

    spans = [slice(0, rows), slice(rows, 2 * rows)]
    sums = [0.0, 0.0]
    for k in range(ny):
        v = top_parts(k)
        if k < ny - 1:
            sums = [sums[n] + product(k, v, spans[n]) for n in range(2)]
    for c in late_y:
        c.start()
    out = []
    for n in range(2):
        total = sums[n] + product(ny - 1, v, spans[n])
        cosines, sines = total[:part_rows], total[part_rows:]
        mine = slice(n * part_rows, (n + 1) * part_rows)
        real = cosines * turn_c[mine] - sines * turn_s[mine]
        imag = sines * turn_c[mine] + cosines * turn_s[mine]
        real = real + pltpu.roll(real, DIRS, 1)
        imag = imag + pltpu.roll(imag, DIRS, 1)
        both = jnp.where(lower[mine], real, -imag)
        partial[n * nx // 2:(n + 1) * nx // 2] = both.reshape(nx // 2, own, 2 * DIRS)
        for b in range(n * nx // 2, (n + 1) * nx // 2):
            k = nx - 1 - b
            if k:
                c = copy(partial.at[b], arrived.at[k], p_send.at[k], p_recv.at[k], line[k - 1])
                c.start()
                out.append((k, c))
    for c in late_x + late_y:
        c.wait()

    def low_h_first(x):
        f = [te[c, x, :, low] for c in range(3)]

        def nz(c):
            return other_layer(jnp.where(left_half, te[c, x, :, high], f[c]))

        fx, fy, fz = f
        curl = (
            (next_y(fz) - fz) - (nz(1) - fy),
            (nz(0) - fx) - (te[2, x + 1, :, low] - fz),
            (te[1, x + 1, :, low] - fy) - (next_y(fx) - fx),
        )
        for c in range(3):
            th[c, x, :, low] = th[c, x, :, low] - time_step * curl[c]

    def low_e_first(x):
        g = [th[c, x, :, low] for c in range(3)]
        curl = curl_b(g, lambda c: th[c, x - 1, :, low], prev_y, prev_z)
        ratio = inverse[x, :, low]
        for c in range(3):
            te[c, x, :, low] = te[c, x, :, low] + ratio * curl[c] - source_1[c, x, :, low]

    def low_h_second(x):
        f = [te[c, x, :, low] for c in range(3)]

        def nz(c):
            return other_layer(jnp.where(left_half, e_1[c, x], f[c]))

        fx, fy, fz = f
        curl = (
            (next_y(fz) - fz) - (nz(1) - fy),
            (nz(0) - fx) - (te[2, x + 1, :, low] - fz),
            (te[1, x + 1, :, low] - fy) - (next_y(fx) - fx),
        )
        for c in range(3):
            th[c, x, :, low] = th[c, x, :, low] - time_step * curl[c]

    def rest(u, carry):
        x = u + 2
        low_h_first(x + 1)
        low_e_first(x + 1)
        low_h_second(x)
        g = [th[c, x, :, low] for c in range(3)]
        curl = curl_b(g, lambda c: th[c, x - 1, :, low], prev_y, prev_z)
        new = e_second(x, curl, 3, low, lambda c: te[c, x, :wy, low])
        hx, hy, hz = [h_2[c, x] for c in range(3)]
        below_x = other_layer(jnp.where(left_half, hx, g[0]))
        below_y = other_layer(jnp.where(left_half, hy, g[1]))
        curl = (
            (hz - prev_y(hz)) - (hy - below_y),
            (hx - below_x) - (hz - h_2[2, x - 1]),
            (hy - h_2[1, x - 1]) - (hx - prev_y(hx)),
        )
        above = e_second(x, curl, 3, high, lambda c: e_1[c, x, :wy])
        for c in range(3):
            out_e[c, u, :, low] = new[c]
            out_e[c, u, :, high] = above[c]
            out_h[c, u, :, low] = g[c][:wy]
            out_h[c, u, :, high] = h_2[c, x, :wy]
        return carry

    low_h_first(0)
    low_h_first(1)
    low_e_first(1)
    low_h_first(2)
    low_e_first(2)
    low_h_second(1)
    lax.fori_loop(0, wx, rest, 0, unroll=True)

    totals = [partial[nx - 1], None]
    for k, c in out[::-1]:
        c.wait_recv()
        totals[k % 2] = arrived[k] if totals[k % 2] is None else totals[k % 2] + arrived[k]
    out_s[:, :2 * DIRS] = jnp.where(core == 0, totals[0], totals[1])
    out_s[:, 2 * DIRS:] = jnp.where(core == 0, totals[1], totals[0])
    for _, c in copies + out:
        c.wait_send()


def hand_over(from_e, from_h, from_s, to_e, to_h, to_s, sem):
    copies = [
        pltpu.make_async_copy(src, dst, sem.at[k])
        for k, (src, dst) in enumerate(((from_e, to_e), (from_h, to_h), (from_s, to_s)))
    ]
    for c in copies:
        c.start()
    for c in copies:
        c.wait()


def local(nx, ny, te, th, fe, fh, classes, material, permittivity, contrast, orders):
    wx, wy = te.shape[1], te.shape[2]
    own = orders.shape[0] // (nx * ny)
    rows = nx * own
    f32 = jnp.float32
    vmem = pl.BlockSpec(memory_space=pltpu.VMEM)
    hbm = pl.BlockSpec(memory_space=pltpu.HBM)
    args = (
        te, th, jnp.transpose(fe, (0, 1, 3, 2)), jnp.transpose(fh, (0, 1, 3, 2)),
        jnp.transpose(classes, (0, 2, 1)), jnp.transpose(material, (0, 2, 1)),
        permittivity, contrast, jnp.transpose(orders),
    )
    args = tuple(pltpu.with_memory_space_constraint(v, pltpu.HBM) for v in args)
    out_shape = (
        jax.ShapeDtypeStruct(te.shape, f32),
        jax.ShapeDtypeStruct(th.shape, f32),
        jax.ShapeDtypeStruct((own, 4 * DIRS), f32),
    )
    wide_x, wide_y = wx + 2 * REACH, wy + PAD

    def pair_of(n):
        return [pltpu.SemaphoreType.DMA((n,))] * 2

    results = pl.pallas_call(
        functools.partial(kernel, nx, ny, own),
        out_shape=out_shape,
        in_specs=[hbm] * 9,
        out_specs=(vmem, vmem, vmem),
        scratch_shapes=[
            *[pltpu.VMEM((3, wide_x, wide_y, WIDE), f32)] * 2,
            pltpu.VMEM((2, wide_x, wide_y, HALF), f32),
            *[pltpu.VMEM((3, wide_x, wide_y, HALF), f32)] * 3,
            pltpu.VMEM((3, wide_x, wide_y, WIDE), f32),
            pltpu.VMEM((3, wx, wy, WIDE), f32),
            pltpu.VMEM((wide_x, wide_y, WIDE), f32),
            pltpu.VMEM((32, wx * wy), f32), pltpu.VMEM((2, 32, wx * wy), f32),
            pltpu.VMEM((8, 128), f32), pltpu.VMEM((6, 8, 128), f32),
            pltpu.VMEM((2, wx // 2 * wy, 2 * DIRS), f32),
            pltpu.VMEM((ny, 2, wx // 2 * wy, 2 * DIRS), f32),
            *[pltpu.VMEM((nx, own, 2 * DIRS), f32)] * 2,
            pltpu.VMEM((ny, 2 * rows, 3 * wx * wy), jnp.bfloat16),
            *pair_of(31), *pair_of(8), *pair_of(4 * ny), *pair_of(nx),
            *[pltpu.VMEM(v.shape, v.dtype) for v in args[2:6]],
            *[pltpu.SMEM(v.shape, v.dtype) for v in args[6:8]],
            pltpu.VMEM(args[8].shape, args[8].dtype),
            pltpu.SemaphoreType.DMA((13,)),
        ],
        compiler_params=pltpu.CompilerParams(
            collective_id=0, has_side_effects=True, vmem_limit_bytes=48 * 1024 * 1024
        ),
        name="slab",
    )(*args)
    return pl.pallas_call(
        hand_over,
        out_shape=out_shape,
        in_specs=[vmem] * 3,
        out_specs=(hbm, hbm, hbm),
        scratch_shapes=[pltpu.SemaphoreType.DMA((3,))],
        compiler_params=pltpu.CompilerParams(vmem_limit_bytes=16 * 1024 * 1024),
        name="hand_over",
    )(*results)


def solution(mesh):
    in_specs = (
        P(None, "gx", "gy", None),
        P(None, "gx", "gy", None),
        P(None, "gx", "gy", None),
        P(None, "gx", "gy", None),
        P("gx", "gy", None),
        P("gx", "gy", None),
        P(),
        P(),
        P(),
    )
    out_specs = (P(None, "gx", "gy", None), P(None, "gx", "gy", None), P(("gx", "gy"), None))
    body = functools.partial(local, mesh.shape["gx"], mesh.shape["gy"])
    return jax.shard_map(body, mesh=mesh, in_specs=in_specs, out_specs=out_specs, check_vma=False)
```

```python
import functools
import math

import jax
import jax.numpy as jnp
from jax import lax
from jax.experimental import pallas as pl
from jax.experimental.pallas import tpu as pltpu
from jax.sharding import PartitionSpec as P

DIRS = 64
STEPS = 2
LAYERS = 4
WIDE = LAYERS * DIRS
HALF = WIDE // 2
time_step = 0.5


REACH = 2
PAD = 8
GROUP = 32


def lanes_of(shape):
    return lax.broadcasted_iota(jnp.int32, shape, len(shape) - 1)


def sublanes_of(shape):
    return lax.broadcasted_iota(jnp.int32, shape, len(shape) - 2)


def next_y(f):
    return pltpu.roll(f, f.shape[0] - 1, 0)


def prev_y(f):
    return pltpu.roll(f, 1, 0)


def next_z(f):
    wide = f.shape[-1]
    return jnp.where(lanes_of(f.shape) < wide - DIRS, pltpu.roll(f, wide - DIRS, 1), 0.0)


def prev_z(f):
    return jnp.where(lanes_of(f.shape) >= DIRS, pltpu.roll(f, DIRS, 1), 0.0)


def curl_f(f, x_next, ny, nz):
    fx, fy, fz = f
    return (
        (ny(fz) - fz) - (nz(fy) - fy),
        (nz(fx) - fx) - (x_next(2) - fz),
        (x_next(1) - fy) - (ny(fx) - fx),
    )


def curl_b(f, x_prev, py, pz):
    fx, fy, fz = f
    return (
        (fz - py(fz)) - (fy - pz(fy)),
        (fx - pz(fx)) - (fz - x_prev(2)),
        (fy - x_prev(1)) - (fx - py(fx)),
    )


def sine(turn):
    u = turn * (2.0 * math.pi)
    s = u * u
    poly = -1.0 / 39916800.0
    for c in (1.0 / 362880.0, -1.0 / 5040.0, 1.0 / 120.0, -1.0 / 6.0):
        poly = poly * s + c
    return u + u * (s * poly)


def split(v):
    parts = []
    for _ in range(3):
        parts.append(v.astype(jnp.bfloat16))
        v = v - parts[-1].astype(jnp.float32)
    return parts


def stacked(v):
    parts = [part.astype(jnp.float32) for part in split(v)]
    return parts


def selected(v, choice):
    n = v.shape[0]
    parts = stacked(v)
    if 3 * n % 16:
        parts.append(jnp.zeros_like(v))
    got = jnp.dot(
        jnp.concatenate(parts, 0).astype(jnp.bfloat16), choice, preferred_element_type=jnp.float32
    )
    return got[:n] + got[n:2 * n] + got[2 * n:3 * n]


def ones_where(hit):
    return hit.astype(jnp.float32).astype(jnp.bfloat16)


def paired(n, k, size):
    out, bit = 0, 1
    while bit < size:
        out = out + bit * ((n // bit + k // bit) % 2)
        bit *= 2
    return out


def kernel(
    nx, ny, own,
    te_at, th_at, fe_at, fh_at, classes_at, material_at, permittivity_at, contrast_at, orders_at,
    out_e, out_h, out_s,
    te, th, edge, h_1, e_1, h_2, source_1, source_2, inverse, block_out, block_in, strip_out, strip_in,
    tops, gathered, partial, arrived, table,
    rim_send, rim_recv, f_send, f_recv, g_send, g_recv, p_send, p_recv,
    fe, fh, classes, material, permittivity, contrast, orders, load,
):
    wx, wy = te_at.shape[1], te_at.shape[2]
    rows_y = te.shape[2]
    inside = (pl.ds(REACH, wx), pl.ds(0, wy))
    i, j = lax.axis_index("gx"), lax.axis_index("gy")
    core = lax.rem(i, 2)
    mate = i + 1 - 2 * core
    beyond = lax.rem(i + nx - 1 + 2 * core, nx)

    def at(dx, dy):
        return (lax.rem(i + nx + dx, nx), lax.rem(j + ny + dy, ny))

    line = [(paired(i, k, nx), j) for k in range(1, nx)]
    sheet = [(mate, j)] + [(n, paired(j, k, ny)) for k in range(1, ny) for n in (i, mate)]
    left, right = at(0, -1)[1], at(0, 1)[1]
    peers = [(beyond, left), (beyond, right), (beyond, j)] + sheet[1:] + line
    barrier = pltpu.get_barrier_semaphore()
    for peer in peers:
        pl.semaphore_signal(barrier, inc=1, device_id=peer, device_id_type=pl.DeviceIdType.MESH)

    def copy(src, dst, send, recv, device):
        return pltpu.make_async_remote_copy(
            src_ref=src, dst_ref=dst, send_sem=send, recv_sem=recv,
            device_id=device, device_id_type=pl.DeviceIdType.MESH,
        )

    small = [
        pltpu.make_async_copy(src, dst, load.at[6 + k])
        for k, (src, dst) in enumerate((
            (fe_at, fe), (fh_at, fh), (classes_at, classes), (material_at, material),
            (permittivity_at, permittivity), (contrast_at, contrast), (orders_at, orders),
        ))
    ]
    large = [
        pltpu.make_async_copy(src.at[c], dst.at[(c, *inside)], load.at[2 * c + k])
        for c in range(3) for k, (src, dst) in enumerate(((te_at, te), (th_at, th)))
    ]
    for c in small[:4] + large + small[4:]:
        c.start()

    spots = wx * wy
    lane = lax.broadcasted_iota(jnp.int32, (1, 128), 1)
    group, in_group = lane // GROUP, lane % GROUP
    k = in_group % 4
    from_lane = group * spots + (in_group // 4) * wy + jnp.where(k < 2, k, wy - 4 + k)
    strip_choice = ones_where(lax.broadcasted_iota(jnp.int32, (4 * spots, 128), 0) == from_lane)
    for c in small[:4]:
        c.wait()
    for x in range(wx):
        cells = slice(x * wy, (x + 1) * wy)
        for c in range(3):
            block_out[4 * c:4 * c + 4, cells] = fe[c, x]
            block_out[12 + 4 * c:16 + 4 * c, cells] = fh[c, x]
        block_out[24:28, cells] = classes[x].astype(jnp.float32)
        block_out[28:32, cells] = material[x].astype(jnp.float32)
    mine = block_out[...]
    strip_out[...] = selected(jnp.concatenate([mine[8 * g:8 * g + 8] for g in range(4)], 1), strip_choice)

    pl.semaphore_wait(barrier, len(peers))
    strips = [(0, -1), (0, 1), (-1, -1), (-1, 1), (1, -1), (1, 1)]
    f_copies = []
    for n, (dx, dy) in enumerate(strips):
        f_copies.append(copy(strip_out, strip_in.at[n], f_send.at[n], f_recv.at[n], at(-dx, -dy)))
    for n, dx in enumerate((-1, 1)):
        f_copies.append(copy(block_out, block_in.at[n], f_send.at[6 + n], f_recv.at[6 + n], at(-dx, 0)))
    for c in f_copies[2:] + f_copies[:2]:
        c.start()

    every, top_half, low_half = pl.ds(0, WIDE), pl.ds(HALF, HALF), pl.ds(0, HALF)
    low, high = slice(0, HALF), slice(HALF, WIDE)
    left_half = lax.broadcasted_iota(jnp.int32, (1, HALF), 1) < DIRS
    x0, x1 = REACH, REACH + wx
    same_x, same_y = (pl.ds(x0, wx),) * 2, (pl.ds(0, wy),) * 2
    r_copies = []

    def moved(source, target, n):
        return pl.ds(source, n), pl.ds(target, n)

    def rim(f, x, y, lanes, side, comps=None):
        (sx, tx), (sy, ty) = x, y
        n = len(r_copies)
        comps = pl.ds(*comps) if comps else slice(None)
        c = copy(
            f.at[comps, sx, sy, lanes], f.at[comps, tx, ty, lanes], rim_send.at[n], rim_recv.at[n], at(*side)
        )
        r_copies.append(c)
        return c

    def other_layer(v):
        return pltpu.roll(v, DIRS, 1)

    for c in large:
        c.wait()
    for x in range(x0, x1):
        ex, ey, ez = [te[c, x, :wy, low] for c in range(3)]
        part_x = th[0, x, :wy, low] + time_step * (ez + (other_layer(te[1, x, :wy, high]) - ey))
        part_y = th[1, x, :wy, low] - time_step * ((other_layer(te[0, x, :wy, high]) - ex) + ez)
        edge[0, x, :wy] = jnp.where(left_half, other_layer(part_x), part_y)
        edge[1, x, :wy] = jnp.where(left_half, other_layer(ez), ez)
    one_up, two_up = moved(x1 - 1, 1, 1), moved(x1 - 2, 0, 2)
    one_down, two_down = moved(x0, x1, 1), moved(x0, x1, 2)
    one_right, two_right = moved(wy - 1, rows_y - 1, 1), moved(wy - 2, rows_y - 2, 2)
    one_left, two_left = moved(0, wy, 1), moved(0, wy, 2)
    lanes_e = pl.ds(0, HALF)
    early = [
        rim(te, one_up, one_right, every, (1, 1)), rim(th, one_up, one_right, every, (1, 1)),
        rim(edge, one_up, one_right, lanes_e, (1, 1)),
        rim(te, two_up, two_left, every, (1, -1)), rim(th, two_up, one_left, every, (1, -1)),
        rim(edge, one_up, two_left, lanes_e, (1, -1)),
        rim(te, two_down, two_right, every, (-1, 1)), rim(th, one_down, two_right, every, (-1, 1)),
        rim(edge, two_down, one_right, lanes_e, (-1, 1)),
        rim(te, one_down, one_left, every, (-1, -1)),
        rim(edge, one_down, one_left, lanes_e, (-1, -1)),
        rim(te, same_x, two_right, top_half, (0, 1)), rim(th, same_x, one_right, top_half, (0, 1)),
        *[rim(th, same_x, moved(wy - 2, rows_y - 2, 1), top_half, (0, 1), (c, 1)) for c in (0, 2)],
        rim(edge, same_x, one_right, lanes_e, (0, 1)),
        rim(te, same_x, one_left, top_half, (0, -1)),
        *[rim(te, same_x, moved(1, wy + 1, 1), top_half, (0, -1), (c, 1)) for c in (0, 2)], rim(th, same_x, one_left, top_half, (0, -1)),
        rim(edge, same_x, one_left, lanes_e, (0, -1)), rim(edge, same_x, moved(1, wy + 1, 1), lanes_e, (0, -1), (1, 1)),
        rim(te, two_up, same_y, top_half, (1, 0)), rim(th, two_up, same_y, top_half, (1, 0)),
        rim(edge, one_up, same_y, lanes_e, (1, 0)),
        rim(te, two_down, same_y, top_half, (-1, 0)), rim(th, one_down, same_y, top_half, (-1, 0)),
        rim(edge, two_down, same_y, lanes_e, (-1, 0)),
    ]
    for c in early:
        c.start()
    late_x = [
        rim(te, two_up, same_y, low_half, (1, 0)), rim(th, two_up, same_y, low_half, (1, 0)),
        rim(te, two_down, same_y, low_half, (-1, 0)), rim(th, one_down, same_y, low_half, (-1, 0)),
    ]
    late_y = [
        rim(te, same_x, two_right, low_half, (0, 1)), rim(th, same_x, two_right, low_half, (0, 1)),
        rim(te, same_x, two_left, low_half, (0, -1)), rim(th, same_x, one_left, low_half, (0, -1)),
    ]

    for c in small[4:]:
        c.wait()
    rows, half = nx * own, wx // 2
    block = 2 * half * wy
    cells = ny * block
    count = orders.shape[1]
    row = lax.broadcasted_iota(jnp.int32, (rows, 1), 0)
    target = paired(i, nx - 1 - row // own, nx) * (ny * own) + j * own + row % own
    pick = ones_where(lax.broadcasted_iota(jnp.int32, (rows, count), 1) == target)
    pair = lax.dot_general(
        pick, orders[...].astype(jnp.float32).astype(jnp.bfloat16),
        (((1,), (1,)), ((), ())), preferred_element_type=jnp.float32,
    )
    cell = lax.broadcasted_iota(jnp.int32, (1, cells), 1)
    all_x, all_y = nx * wx, ny * wy
    all_cells = float(all_x * all_y)
    inner_pairs, inner = half - 2, wy - 2 * REACH
    spot_in = cell % (half * wy)
    tail = inner_pairs * inner
    edge_rows = spot_in - tail
    outer = edge_rows - inner_pairs * 2 * REACH
    inner_u = jnp.zeros_like(cell)
    for n in range(1, inner_pairs):
        inner_u = inner_u + jnp.where(spot_in >= n * inner, 1, 0)
    pair_u = jnp.where(spot_in < tail, 1 + inner_u, jnp.where(
        outer < 0, 1 + edge_rows // (2 * REACH), jnp.where(outer < wy, 0, half - 1)))
    y_in = jnp.where(spot_in < tail, REACH + spot_in - inner * inner_u, jnp.where(
        outer < 0, (wy - REACH + edge_rows % (2 * REACH)) % wy, outer % wy))
    x_in = ((cell // (half * wy)) % 2) * wx + 2 * pair_u
    x_at = (((i - core) * wx + x_in) * all_y).astype(jnp.float32)
    y_at = (((cell // block) * wy + y_in) * all_x).astype(jnp.float32)

    def waves(index):
        index = index - all_cells * jnp.round(index * (1.0 / all_cells))
        turn = index * (1.0 / all_cells)
        cosine = sine(0.25 - jnp.abs(turn))
        sines = sine(jnp.where(turn > 0.25, 0.5 - turn, jnp.where(turn < -0.25, -0.5 - turn, turn)))
        return cosine, sines

    part_rows = rows // 2
    for sine_rows, value in zip((0, part_rows), waves(pair[:, 0:1] * x_at + pair[:, 1:2] * y_at)):
        near, far = split(value)[:2]
        for k in range(ny):
            for q, part in enumerate((near, far, near)):
                for n in range(2):
                    place = 2 * n * part_rows + sine_rows
                    table[k, place:place + part_rows, q * block:(q + 1) * block] = part[
                        n * part_rows:(n + 1) * part_rows, k * block:(k + 1) * block
                    ]
    lower = lax.broadcasted_iota(jnp.int32, (rows, 2 * DIRS), 1) < DIRS
    turn_c, turn_s = waves(jnp.where(lower, 0.0, pair[:, 0:1] * float(all_y)))
    scale = 1.0 / math.sqrt(all_x * all_y)
    turn_c, turn_s = turn_c * scale, turn_s * scale

    span_l = (wx + 2 * REACH) * GROUP
    spot = lax.broadcasted_iota(jnp.int32, (1, span_l), 1)
    p = spot % GROUP
    x = spot // GROUP - REACH
    y = jnp.where(p < wy + REACH, p, p - rows_y)
    valid = (p < wy + REACH) | ((p >= rows_y - REACH) & (p < rows_y))
    side_x = jnp.where(x < 0, -1, jnp.where(x >= wx, 1, 0))
    side_y = jnp.where(y < 0, -1, jnp.where(y >= wy, 1, 0))
    lx, ly = x - side_x * wx, y - side_y * wy
    whole = jnp.where(side_x == 0, 0, jnp.where(side_x < 0, 1, 2)) * spots + lx * wy + ly
    which = jnp.where(side_x == 0, 0, jnp.where(side_x < 0, 2, 4)) + jnp.where(side_y > 0, 1, 0)
    strip = 3 * spots + which * GROUP + lx * 4 + jnp.where(ly < 2, ly, ly - (wy - 4))
    origin = jnp.where(valid, jnp.where(side_y == 0, whole, strip), -1)
    choice = ones_where(lax.broadcasted_iota(jnp.int32, (3 * spots + 256, span_l), 0) == origin)
    spread = ones_where(
        lax.broadcasted_iota(jnp.int32, (32, WIDE), 0) % 8 == lax.broadcasted_iota(jnp.int32, (32, WIDE), 1) // DIRS
    )

    for c in f_copies:
        c.wait()
    gathered_strips = []
    for first in (0, 4):
        groups = []
        for g in range(4):
            got = None
            for n in range(first, min(first + 4, 6)):
                v = strip_in[n]
                shift = (GROUP * (n - first - g)) % 128
                v = pltpu.roll(v, shift, 1) if shift else v
                got = v if got is None else jnp.where(lane // GROUP == n - first, v, got)
            groups.append(got)
        gathered_strips.append(jnp.concatenate(groups, 0))
    around = selected(
        jnp.concatenate([mine, block_in[0], block_in[1], *gathered_strips], 1), choice
    )
    pairs = [around[8 * g:8 * g + 8] for g in range(4)]
    fields = [f for v in pairs for f in (v, pltpu.roll(v, 4, 0))]
    f_e, f_h, kind, matter = fields[:3], fields[3:6], fields[6], fields[7]
    layer = sublanes_of((8, span_l))

    def f_next_x(f):
        return pltpu.roll(f, span_l - GROUP, 1)

    def f_prev_x(f):
        return pltpu.roll(f, GROUP, 1)

    def f_next_y(f):
        return jnp.where(p == rows_y - 1, pltpu.roll(f, rows_y - 1, 1), pltpu.roll(f, span_l - 1, 1))

    def f_prev_y(f):
        return jnp.where(p == 0, pltpu.roll(f, span_l - rows_y + 1, 1), pltpu.roll(f, 1, 1))

    def f_next_z(f):
        return jnp.where(layer < LAYERS - 1, pltpu.roll(f, 7, 0), 0.0)

    def f_prev_z(f):
        return jnp.where(layer >= 1, pltpu.roll(f, 1, 0), 0.0)

    eps = jnp.full((8, span_l), permittivity[0])
    slope = jnp.full((8, span_l), contrast[0])
    for k in range(1, permittivity.shape[0]):
        eps = jnp.where(matter == float(k), permittivity[k], eps)
        slope = jnp.where(matter == float(k), contrast[k], slope)
    ratio = time_step / eps
    coef = time_step * slope / (eps * eps)
    sources = []
    for step in range(STEPS):
        curl = curl_f(f_e, lambda c: f_next_x(f_e[c]), f_next_y, f_next_z)
        f_h = [f_h[c] - time_step * curl[c] for c in range(3)]
        curl = curl_b(f_h, lambda c: f_prev_x(f_h[c]), f_prev_y, f_prev_z)
        sources.append([coef * curl[c] for c in range(3)])
        f_e = [f_e[c] + ratio * curl[c] for c in range(3)]

    def wide(v, exact=True):
        v = jnp.where(layer < LAYERS, v, 0.0)
        zero = jnp.zeros_like(v)
        parts = stacked(v) + [zero] if exact else [v, zero, zero, zero]
        return lax.dot_general(
            jnp.concatenate(parts, 0).astype(jnp.bfloat16), spread, (((0,), (0,)), ((), ())),
            preferred_element_type=jnp.float32,
        )

    hot = wide(kind, False) == (lax.broadcasted_iota(jnp.int32, (1, WIDE), 1) % DIRS).astype(jnp.float32)
    v = wide(ratio)
    for x in range(1, wx + 3):
        inverse[x] = v[GROUP * x:GROUP * x + rows_y]
    for c in range(3):
        v = jnp.where(hot, wide(sources[0][c]), 0.0)
        for x in range(1, wx + 3):
            source_1[c, x] = v[GROUP * x:GROUP * x + rows_y]
        v = jnp.where(hot, wide(sources[1][c]), 0.0)
        for x in range(wx):
            source_2[c, x] = v[GROUP * (x + REACH):GROUP * (x + REACH) + wy]

    def h_first(x, rows):
        f = [te[c, x, rows, high] for c in range(3)]
        curl = curl_f(f, lambda c: te[c, x + 1, rows, high], next_y, next_z)
        for c in range(3):
            h_1[c, x, rows] = th[c, x, rows, high] - time_step * curl[c]

    def e_first(x, rows):
        hx, hy, hz = [h_1[c, x, rows] for c in range(3)]
        below = edge[0, x, rows] + time_step * jnp.where(left_half, -next_y(edge[1, x, rows]), edge[1, x + 1, rows])
        below_x = jnp.where(left_half, below, other_layer(hx))
        below_y = other_layer(jnp.where(left_half, hy, below))
        curl = (
            (hz - prev_y(hz)) - (hy - below_y),
            (hx - below_x) - (hz - h_1[2, x - 1, rows]),
            (hy - h_1[1, x - 1, rows]) - (hx - prev_y(hx)),
        )
        ratio = inverse[x, rows, high]
        for c in range(3):
            e_1[c, x, rows] = te[c, x, rows, high] + ratio * curl[c] - source_1[c, x, rows, high]

    def h_second(x, rows):
        curl = curl_f([e_1[c, x, rows] for c in range(3)], lambda c: e_1[c, x + 1, rows], next_y, next_z)
        for c in range(3):
            h_2[c, x, rows] = h_1[c, x, rows] - time_step * curl[c]

    def e_second(x, curl, comps, lanes, e):
        ratio = inverse[x, :wy, lanes]
        return [e(c) + ratio * curl[c][:wy] - source_2[c, x - x0, :, lanes] for c in range(comps)]

    def top_of(x, rows):
        curl = curl_b([h_2[c, x, rows] for c in range(3)], lambda c: h_2[c, x - 1, rows], prev_y, prev_z)
        return e_second(x, curl, 2, high, lambda c: e_1[c, x, :wy])

    copies = []

    def send_tops(first, last):
        span = pl.ds(first, last - first)
        for k in reversed(range(len(sheet))):
            to = mate if k % 2 == 0 else i
            q = 1 - core if k % 2 == 0 else core
            n = len(copies)
            c = copy(
                tops.at[q, span], gathered.at[(k + 1) // 2, core, span], g_send.at[n], g_recv.at[n], (to, sheet[k][1])
            )
            c.start()
            copies.append(((k + 1) // 2, c))

    def keep_top(u, got, inside):
        for q in range(2):
            v = jnp.where(left_half, other_layer(got[0][q]), got[1][q])
            if 0 < u < half - 1:
                v = pltpu.roll(v, wy - REACH, 0)
                if inside:
                    tops[q, (u - 1) * inner:u * inner] = v[:inner]
                else:
                    to = tail + (u - 1) * 2 * REACH
                    tops[q, to:to + 2 * REACH] = v[inner:]
            else:
                to = (half - 2) * wy + (wy if u else 0)
                tops[q, to:to + wy] = v

    mine_only = slice(0, wy)
    h_first(x0, mine_only)
    h_first(x0 + 1, mine_only)
    e_first(x0 + 1, mine_only)
    got = []
    for x in range(x0 + 2, x1 - 1):
        h_first(x, mine_only)
        e_first(x, mine_only)
        h_second(x - 1, mine_only)
        if x > x0 + 2:
            got.append(top_of(x - 1, mine_only))
    for u in range(1, half - 1):
        keep_top(u, got[2 * u - 2:2 * u], True)
    send_tops(0, tail)

    for c in early:
        c.wait()
    for c in late_x:
        c.start()

    every_row = slice(0, rows_y)
    h_first(0, every_row)
    h_first(1, every_row)
    e_first(1, every_row)
    h_first(2, every_row)
    e_first(2, every_row)
    h_second(1, every_row)
    for u in range(half):
        got = []
        for x in (2 * u + 3, 2 * u + 4):
            h_first(x, every_row)
            e_first(x, every_row)
            h_second(x - 1, every_row)
            got.append(top_of(x - 1, every_row))
        keep_top(u, got, False)
    send_tops(tail, half * wy)

    gathered[0, core] = tops[core]

    def top_parts(k):
        for at_k, c in copies:
            if at_k == k:
                c.wait_recv()
        near, far = split(gathered[k].reshape(block, 2 * DIRS))[:2]
        return jnp.concatenate([near, near, far], 0)

    def product(k, v, span):
        return jnp.dot(table[paired(j, k, ny), span], v, preferred_element_type=jnp.float32)

    spans = [slice(0, rows), slice(rows, 2 * rows)]
    sums = [0.0, 0.0]
    for k in range(ny):
        v = top_parts(k)
        if k < ny - 1:
            sums = [sums[n] + product(k, v, spans[n]) for n in range(2)]
    for c in late_y:
        c.start()
    out = []
    for n in range(2):
        total = sums[n] + product(ny - 1, v, spans[n])
        cosines, sines = total[:part_rows], total[part_rows:]
        mine = slice(n * part_rows, (n + 1) * part_rows)
        real = cosines * turn_c[mine] - sines * turn_s[mine]
        imag = sines * turn_c[mine] + cosines * turn_s[mine]
        real = real + pltpu.roll(real, DIRS, 1)
        imag = imag + pltpu.roll(imag, DIRS, 1)
        both = jnp.where(lower[mine], real, -imag)
        partial[n * nx // 2:(n + 1) * nx // 2] = both.reshape(nx // 2, own, 2 * DIRS)
        for b in range(n * nx // 2, (n + 1) * nx // 2):
            k = nx - 1 - b
            if k:
                c = copy(partial.at[b], arrived.at[k], p_send.at[k], p_recv.at[k], line[k - 1])
                c.start()
                out.append((k, c))
    for c in late_x + late_y:
        c.wait()

    def low_h_first(x):
        f = [te[c, x, :, low] for c in range(3)]

        def nz(c):
            return other_layer(jnp.where(left_half, te[c, x, :, high], f[c]))

        fx, fy, fz = f
        curl = (
            (next_y(fz) - fz) - (nz(1) - fy),
            (nz(0) - fx) - (te[2, x + 1, :, low] - fz),
            (te[1, x + 1, :, low] - fy) - (next_y(fx) - fx),
        )
        for c in range(3):
            th[c, x, :, low] = th[c, x, :, low] - time_step * curl[c]

    def low_e_first(x):
        g = [th[c, x, :, low] for c in range(3)]
        curl = curl_b(g, lambda c: th[c, x - 1, :, low], prev_y, prev_z)
        ratio = inverse[x, :, low]
        for c in range(3):
            te[c, x, :, low] = te[c, x, :, low] + ratio * curl[c] - source_1[c, x, :, low]

    def low_h_second(x):
        f = [te[c, x, :, low] for c in range(3)]

        def nz(c):
            return other_layer(jnp.where(left_half, e_1[c, x], f[c]))

        fx, fy, fz = f
        curl = (
            (next_y(fz) - fz) - (nz(1) - fy),
            (nz(0) - fx) - (te[2, x + 1, :, low] - fz),
            (te[1, x + 1, :, low] - fy) - (next_y(fx) - fx),
        )
        for c in range(3):
            th[c, x, :, low] = th[c, x, :, low] - time_step * curl[c]

    def rest(u, carry):
        x = u + 2
        low_h_first(x + 1)
        low_e_first(x + 1)
        low_h_second(x)
        g = [th[c, x, :, low] for c in range(3)]
        curl = curl_b(g, lambda c: th[c, x - 1, :, low], prev_y, prev_z)
        new = e_second(x, curl, 3, low, lambda c: te[c, x, :wy, low])
        hx, hy, hz = [h_2[c, x] for c in range(3)]
        below_x = other_layer(jnp.where(left_half, hx, g[0]))
        below_y = other_layer(jnp.where(left_half, hy, g[1]))
        curl = (
            (hz - prev_y(hz)) - (hy - below_y),
            (hx - below_x) - (hz - h_2[2, x - 1]),
            (hy - h_2[1, x - 1]) - (hx - prev_y(hx)),
        )
        above = e_second(x, curl, 3, high, lambda c: e_1[c, x, :wy])
        for c in range(3):
            out_e[c, u, :, low] = new[c]
            out_e[c, u, :, high] = above[c]
            out_h[c, u, :, low] = g[c][:wy]
            out_h[c, u, :, high] = h_2[c, x, :wy]
        return carry

    low_h_first(0)
    low_h_first(1)
    low_e_first(1)
    low_h_first(2)
    low_e_first(2)
    low_h_second(1)
    lax.fori_loop(0, wx, rest, 0, unroll=True)

    totals = [partial[nx - 1], None]
    for k, c in out[::-1]:
        c.wait_recv()
        totals[k % 2] = arrived[k] if totals[k % 2] is None else totals[k % 2] + arrived[k]
    out_s[:, :2 * DIRS] = jnp.where(core == 0, totals[0], totals[1])
    out_s[:, 2 * DIRS:] = jnp.where(core == 0, totals[1], totals[0])
    for _, c in copies + out:
        c.wait_send()


def hand_over(from_e, from_h, from_s, to_e, to_h, to_s, sem):
    copies = [
        pltpu.make_async_copy(src, dst, sem.at[k])
        for k, (src, dst) in enumerate(((from_e, to_e), (from_h, to_h), (from_s, to_s)))
    ]
    for c in copies:
        c.start()
    for c in copies:
        c.wait()


def local(nx, ny, te, th, fe, fh, classes, material, permittivity, contrast, orders):
    wx, wy = te.shape[1], te.shape[2]
    own = orders.shape[0] // (nx * ny)
    rows = nx * own
    f32 = jnp.float32
    vmem = pl.BlockSpec(memory_space=pltpu.VMEM)
    hbm = pl.BlockSpec(memory_space=pltpu.HBM)
    args = (
        te, th, jnp.transpose(fe, (0, 1, 3, 2)), jnp.transpose(fh, (0, 1, 3, 2)),
        jnp.transpose(classes, (0, 2, 1)), jnp.transpose(material, (0, 2, 1)),
        permittivity, contrast, jnp.transpose(orders),
    )
    args = tuple(pltpu.with_memory_space_constraint(v, pltpu.HBM) for v in args)
    out_shape = (
        jax.ShapeDtypeStruct(te.shape, f32),
        jax.ShapeDtypeStruct(th.shape, f32),
        jax.ShapeDtypeStruct((own, 4 * DIRS), f32),
    )
    wide_x, wide_y = wx + 2 * REACH, wy + PAD

    def pair_of(n):
        return [pltpu.SemaphoreType.DMA((n,))] * 2

    results = pl.pallas_call(
        functools.partial(kernel, nx, ny, own),
        out_shape=out_shape,
        in_specs=[hbm] * 9,
        out_specs=(vmem, vmem, vmem),
        scratch_shapes=[
            *[pltpu.VMEM((3, wide_x, wide_y, WIDE), f32)] * 2,
            pltpu.VMEM((2, wide_x, wide_y, HALF), f32),
            *[pltpu.VMEM((3, wide_x, wide_y, HALF), f32)] * 3,
            pltpu.VMEM((3, wide_x, wide_y, WIDE), f32),
            pltpu.VMEM((3, wx, wy, WIDE), f32),
            pltpu.VMEM((wide_x, wide_y, WIDE), f32),
            pltpu.VMEM((32, wx * wy), f32), pltpu.VMEM((2, 32, wx * wy), f32),
            pltpu.VMEM((8, 128), f32), pltpu.VMEM((6, 8, 128), f32),
            pltpu.VMEM((2, wx // 2 * wy, 2 * DIRS), f32),
            pltpu.VMEM((ny, 2, wx // 2 * wy, 2 * DIRS), f32),
            *[pltpu.VMEM((nx, own, 2 * DIRS), f32)] * 2,
            pltpu.VMEM((ny, 2 * rows, 3 * wx * wy), jnp.bfloat16),
            *pair_of(36), *pair_of(8), *pair_of(4 * ny), *pair_of(nx),
            *[pltpu.VMEM(v.shape, v.dtype) for v in args[2:6]],
            *[pltpu.SMEM(v.shape, v.dtype) for v in args[6:8]],
            pltpu.VMEM(args[8].shape, args[8].dtype),
            pltpu.SemaphoreType.DMA((13,)),
        ],
        compiler_params=pltpu.CompilerParams(
            collective_id=0, has_side_effects=True, vmem_limit_bytes=48 * 1024 * 1024
        ),
        name="slab",
    )(*args)
    return pl.pallas_call(
        hand_over,
        out_shape=out_shape,
        in_specs=[vmem] * 3,
        out_specs=(hbm, hbm, hbm),
        scratch_shapes=[pltpu.SemaphoreType.DMA((3,))],
        compiler_params=pltpu.CompilerParams(vmem_limit_bytes=16 * 1024 * 1024),
        name="hand_over",
    )(*results)


def solution(mesh):
    in_specs = (
        P(None, "gx", "gy", None),
        P(None, "gx", "gy", None),
        P(None, "gx", "gy", None),
        P(None, "gx", "gy", None),
        P("gx", "gy", None),
        P("gx", "gy", None),
        P(),
        P(),
        P(),
    )
    out_specs = (P(None, "gx", "gy", None), P(None, "gx", "gy", None), P(("gx", "gy"), None))
    body = functools.partial(local, mesh.shape["gx"], mesh.shape["gy"])
    return jax.shard_map(body, mesh=mesh, in_specs=in_specs, out_specs=out_specs, check_vma=False)
```

```python
import functools
import math

import jax
import jax.numpy as jnp
from jax import lax
from jax.experimental import pallas as pl
from jax.experimental.pallas import tpu as pltpu
from jax.sharding import PartitionSpec as P

DIRS = 64
STEPS = 2
LAYERS = 4
WIDE = LAYERS * DIRS
HALF = WIDE // 2
time_step = 0.5


REACH = 2
PAD = 8
GROUP = 32


def lanes_of(shape):
    return lax.broadcasted_iota(jnp.int32, shape, len(shape) - 1)


def sublanes_of(shape):
    return lax.broadcasted_iota(jnp.int32, shape, len(shape) - 2)


def next_y(f):
    return pltpu.roll(f, f.shape[0] - 1, 0)


def prev_y(f):
    return pltpu.roll(f, 1, 0)


def next_z(f):
    wide = f.shape[-1]
    return jnp.where(lanes_of(f.shape) < wide - DIRS, pltpu.roll(f, wide - DIRS, 1), 0.0)


def prev_z(f):
    return jnp.where(lanes_of(f.shape) >= DIRS, pltpu.roll(f, DIRS, 1), 0.0)


def curl_f(f, x_next, ny, nz):
    fx, fy, fz = f
    return (
        (ny(fz) - fz) - (nz(fy) - fy),
        (nz(fx) - fx) - (x_next(2) - fz),
        (x_next(1) - fy) - (ny(fx) - fx),
    )


def curl_b(f, x_prev, py, pz):
    fx, fy, fz = f
    return (
        (fz - py(fz)) - (fy - pz(fy)),
        (fx - pz(fx)) - (fz - x_prev(2)),
        (fy - x_prev(1)) - (fx - py(fx)),
    )


def sine(turn):
    u = turn * (2.0 * math.pi)
    s = u * u
    poly = -1.0 / 39916800.0
    for c in (1.0 / 362880.0, -1.0 / 5040.0, 1.0 / 120.0, -1.0 / 6.0):
        poly = poly * s + c
    return u + u * (s * poly)


def split(v):
    parts = []
    for _ in range(3):
        parts.append(v.astype(jnp.bfloat16))
        v = v - parts[-1].astype(jnp.float32)
    return parts


def stacked(v):
    parts = [part.astype(jnp.float32) for part in split(v)]
    return parts


def selected(v, choice):
    n = v.shape[0]
    parts = stacked(v)
    if 3 * n % 16:
        parts.append(jnp.zeros_like(v))
    got = jnp.dot(
        jnp.concatenate(parts, 0).astype(jnp.bfloat16), choice, preferred_element_type=jnp.float32
    )
    return got[:n] + got[n:2 * n] + got[2 * n:3 * n]


def ones_where(hit):
    return hit.astype(jnp.float32).astype(jnp.bfloat16)


def paired(n, k, size):
    out, bit = 0, 1
    while bit < size:
        out = out + bit * ((n // bit + k // bit) % 2)
        bit *= 2
    return out


def kernel(
    nx, ny, own,
    te_at, th_at, fe_at, fh_at, classes_at, material_at, permittivity_at, contrast_at, orders_at,
    out_e, out_h, out_s,
    te, th, edge, h_1, e_1, h_2, source_1, source_2, inverse, block_out, block_in, strip_out, strip_in,
    tops, gathered, partial, arrived, table,
    rim_send, rim_recv, f_send, f_recv, g_send, g_recv, p_send, p_recv,
    fe, fh, classes, material, permittivity, contrast, orders, load,
):
    wx, wy = te_at.shape[1], te_at.shape[2]
    rows_y = te.shape[2]
    inside = (pl.ds(REACH, wx), pl.ds(0, wy))
    i, j = lax.axis_index("gx"), lax.axis_index("gy")
    core = lax.rem(i, 2)
    mate = i + 1 - 2 * core
    beyond = lax.rem(i + nx - 1 + 2 * core, nx)

    def at(dx, dy):
        return (lax.rem(i + nx + dx, nx), lax.rem(j + ny + dy, ny))

    line = [(paired(i, k, nx), j) for k in range(1, nx)]
    sheet = [(mate, j)] + [(n, paired(j, k, ny)) for k in range(1, ny) for n in (i, mate)]
    left, right = at(0, -1)[1], at(0, 1)[1]
    peers = [(beyond, left), (beyond, right), (beyond, j)] + sheet[1:] + line
    barrier = pltpu.get_barrier_semaphore()
    for peer in peers:
        pl.semaphore_signal(barrier, inc=1, device_id=peer, device_id_type=pl.DeviceIdType.MESH)

    def copy(src, dst, send, recv, device):
        return pltpu.make_async_remote_copy(
            src_ref=src, dst_ref=dst, send_sem=send, recv_sem=recv,
            device_id=device, device_id_type=pl.DeviceIdType.MESH,
        )

    small = [
        pltpu.make_async_copy(src, dst, load.at[6 + k])
        for k, (src, dst) in enumerate((
            (fe_at, fe), (fh_at, fh), (classes_at, classes), (material_at, material),
            (permittivity_at, permittivity), (contrast_at, contrast), (orders_at, orders),
        ))
    ]
    large = [
        pltpu.make_async_copy(src.at[c], dst.at[(c, *inside)], load.at[2 * c + k])
        for c in range(3) for k, (src, dst) in enumerate(((te_at, te), (th_at, th)))
    ]
    for c in small[:4] + large + small[4:]:
        c.start()

    spots = wx * wy
    lane = lax.broadcasted_iota(jnp.int32, (1, 128), 1)
    group, in_group = lane // GROUP, lane % GROUP
    k = in_group % 4
    from_lane = group * spots + (in_group // 4) * wy + jnp.where(k < 2, k, wy - 4 + k)
    strip_choice = ones_where(lax.broadcasted_iota(jnp.int32, (4 * spots, 128), 0) == from_lane)
    for c in small[:4]:
        c.wait()
    for x in range(wx):
        cells = slice(x * wy, (x + 1) * wy)
        for c in range(3):
            block_out[4 * c:4 * c + 4, cells] = fe[c, x]
            block_out[12 + 4 * c:16 + 4 * c, cells] = fh[c, x]
        block_out[24:28, cells] = classes[x].astype(jnp.float32)
        block_out[28:32, cells] = material[x].astype(jnp.float32)
    mine = block_out[...]
    strip_out[...] = selected(jnp.concatenate([mine[8 * g:8 * g + 8] for g in range(4)], 1), strip_choice)

    pl.semaphore_wait(barrier, len(peers))
    strips = [(0, -1), (0, 1), (-1, -1), (-1, 1), (1, -1), (1, 1)]
    f_copies = []
    for n, (dx, dy) in enumerate(strips):
        f_copies.append(copy(strip_out, strip_in.at[n], f_send.at[n], f_recv.at[n], at(-dx, -dy)))
    for n, dx in enumerate((-1, 1)):
        f_copies.append(copy(block_out, block_in.at[n], f_send.at[6 + n], f_recv.at[6 + n], at(-dx, 0)))
    for c in f_copies[2:] + f_copies[:2]:
        c.start()

    top_half, low_half = pl.ds(HALF, HALF), pl.ds(0, HALF)
    low, high = slice(0, HALF), slice(HALF, WIDE)
    left_half = lax.broadcasted_iota(jnp.int32, (1, HALF), 1) < DIRS
    x0, x1 = REACH, REACH + wx
    same_x, same_y = (pl.ds(x0, wx),) * 2, (pl.ds(0, wy),) * 2
    r_copies = []

    def moved(source, target, n):
        return pl.ds(source, n), pl.ds(target, n)

    def rim(f, x, y, lanes, side, comps=None):
        (sx, tx), (sy, ty) = x, y
        n = len(r_copies)
        comps = pl.ds(*comps) if comps else slice(None)
        c = copy(
            f.at[comps, sx, sy, lanes], f.at[comps, tx, ty, lanes], rim_send.at[n], rim_recv.at[n], at(*side)
        )
        r_copies.append(c)
        return c

    def other_layer(v):
        return pltpu.roll(v, DIRS, 1)

    for c in large:
        c.wait()
    for x in range(x0, x1):
        ex, ey, ez = [te[c, x, :wy, low] for c in range(3)]
        part_x = th[0, x, :wy, low] + time_step * (ez + (other_layer(te[1, x, :wy, high]) - ey))
        part_y = th[1, x, :wy, low] - time_step * ((other_layer(te[0, x, :wy, high]) - ex) + ez)
        edge[0, x, :wy] = jnp.where(left_half, other_layer(part_x), part_y)
        edge[1, x, :wy] = jnp.where(left_half, other_layer(ez), ez)
    one_up, two_up = moved(x1 - 1, 1, 1), moved(x1 - 2, 0, 2)
    one_down, two_down = moved(x0, x1, 1), moved(x0, x1, 2)
    one_right, two_right = moved(wy - 1, rows_y - 1, 1), moved(wy - 2, rows_y - 2, 2)
    one_left, two_left = moved(0, wy, 1), moved(0, wy, 2)
    lanes_e = pl.ds(0, HALF)
    early = [
        rim(te, one_up, one_right, top_half, (1, 1)), rim(th, one_up, one_right, top_half, (1, 1)),
        rim(edge, one_up, one_right, lanes_e, (1, 1)),
        rim(te, two_up, two_left, top_half, (1, -1)), rim(th, two_up, one_left, top_half, (1, -1)),
        rim(edge, one_up, two_left, lanes_e, (1, -1)),
        rim(te, two_down, two_right, top_half, (-1, 1)), rim(th, one_down, two_right, top_half, (-1, 1)),
        rim(edge, two_down, one_right, lanes_e, (-1, 1)),
        rim(te, one_down, one_left, top_half, (-1, -1)),
        rim(edge, one_down, one_left, lanes_e, (-1, -1)),
        rim(te, same_x, two_right, top_half, (0, 1)), rim(th, same_x, one_right, top_half, (0, 1)),
        *[rim(th, same_x, moved(wy - 2, rows_y - 2, 1), top_half, (0, 1), (c, 1)) for c in (0, 2)],
        rim(edge, same_x, one_right, lanes_e, (0, 1)),
        rim(te, same_x, one_left, top_half, (0, -1)),
        *[rim(te, same_x, moved(1, wy + 1, 1), top_half, (0, -1), (c, 1)) for c in (0, 2)], rim(th, same_x, one_left, top_half, (0, -1)),
        rim(edge, same_x, one_left, lanes_e, (0, -1)), rim(edge, same_x, moved(1, wy + 1, 1), lanes_e, (0, -1), (1, 1)),
        rim(te, two_up, same_y, top_half, (1, 0)), rim(th, two_up, same_y, top_half, (1, 0)),
        rim(edge, one_up, same_y, lanes_e, (1, 0)),
        rim(te, two_down, same_y, top_half, (-1, 0)), rim(th, one_down, same_y, top_half, (-1, 0)),
        rim(edge, two_down, same_y, lanes_e, (-1, 0)),
    ]
    for c in early:
        c.start()
    late_x = [
        rim(te, one_up, one_right, low_half, (1, 1)), rim(th, one_up, one_right, low_half, (1, 1)),
        rim(te, two_up, two_left, low_half, (1, -1)), rim(th, two_up, one_left, low_half, (1, -1)),
        rim(te, two_down, two_right, low_half, (-1, 1)), rim(th, one_down, two_right, low_half, (-1, 1)),
        rim(te, one_down, one_left, low_half, (-1, -1)),
        rim(te, two_up, same_y, low_half, (1, 0)), rim(th, two_up, same_y, low_half, (1, 0)),
        rim(te, two_down, same_y, low_half, (-1, 0)), rim(th, one_down, same_y, low_half, (-1, 0)),
    ]
    late_y = [
        rim(te, same_x, two_right, low_half, (0, 1)), rim(th, same_x, two_right, low_half, (0, 1)),
        rim(te, same_x, two_left, low_half, (0, -1)), rim(th, same_x, one_left, low_half, (0, -1)),
    ]

    for c in small[4:]:
        c.wait()
    rows, half = nx * own, wx // 2
    block = 2 * half * wy
    cells = ny * block
    count = orders.shape[1]
    row = lax.broadcasted_iota(jnp.int32, (rows, 1), 0)
    target = paired(i, nx - 1 - row // own, nx) * (ny * own) + j * own + row % own
    pick = ones_where(lax.broadcasted_iota(jnp.int32, (rows, count), 1) == target)
    pair = lax.dot_general(
        pick, orders[...].astype(jnp.float32).astype(jnp.bfloat16),
        (((1,), (1,)), ((), ())), preferred_element_type=jnp.float32,
    )
    cell = lax.broadcasted_iota(jnp.int32, (1, cells), 1)
    all_x, all_y = nx * wx, ny * wy
    all_cells = float(all_x * all_y)
    inner_pairs, inner = half - 2, wy - 2 * REACH
    spot_in = cell % (half * wy)
    tail = inner_pairs * inner
    edge_rows = spot_in - tail
    outer = edge_rows - inner_pairs * 2 * REACH
    inner_u = jnp.zeros_like(cell)
    for n in range(1, inner_pairs):
        inner_u = inner_u + jnp.where(spot_in >= n * inner, 1, 0)
    pair_u = jnp.where(spot_in < tail, 1 + inner_u, jnp.where(
        outer < 0, 1 + edge_rows // (2 * REACH), jnp.where(outer < wy, 0, half - 1)))
    y_in = jnp.where(spot_in < tail, REACH + spot_in - inner * inner_u, jnp.where(
        outer < 0, (wy - REACH + edge_rows % (2 * REACH)) % wy, outer % wy))
    x_in = ((cell // (half * wy)) % 2) * wx + 2 * pair_u
    x_at = (((i - core) * wx + x_in) * all_y).astype(jnp.float32)
    y_at = (((cell // block) * wy + y_in) * all_x).astype(jnp.float32)

    def waves(index):
        index = index - all_cells * jnp.round(index * (1.0 / all_cells))
        turn = index * (1.0 / all_cells)
        cosine = sine(0.25 - jnp.abs(turn))
        sines = sine(jnp.where(turn > 0.25, 0.5 - turn, jnp.where(turn < -0.25, -0.5 - turn, turn)))
        return cosine, sines

    part_rows = rows // 2
    for sine_rows, value in zip((0, part_rows), waves(pair[:, 0:1] * x_at + pair[:, 1:2] * y_at)):
        near, far = split(value)[:2]
        for k in range(ny):
            for q, part in enumerate((near, far, near)):
                for n in range(2):
                    place = 2 * n * part_rows + sine_rows
                    table[k, place:place + part_rows, q * block:(q + 1) * block] = part[
                        n * part_rows:(n + 1) * part_rows, k * block:(k + 1) * block
                    ]
    lower = lax.broadcasted_iota(jnp.int32, (rows, 2 * DIRS), 1) < DIRS
    turn_c, turn_s = waves(jnp.where(lower, 0.0, pair[:, 0:1] * float(all_y)))
    scale = 1.0 / math.sqrt(all_x * all_y)
    turn_c, turn_s = turn_c * scale, turn_s * scale

    span_l = (wx + 2 * REACH) * GROUP
    spot = lax.broadcasted_iota(jnp.int32, (1, span_l), 1)
    p = spot % GROUP
    x = spot // GROUP - REACH
    y = jnp.where(p < wy + REACH, p, p - rows_y)
    valid = (p < wy + REACH) | ((p >= rows_y - REACH) & (p < rows_y))
    side_x = jnp.where(x < 0, -1, jnp.where(x >= wx, 1, 0))
    side_y = jnp.where(y < 0, -1, jnp.where(y >= wy, 1, 0))
    lx, ly = x - side_x * wx, y - side_y * wy
    whole = jnp.where(side_x == 0, 0, jnp.where(side_x < 0, 1, 2)) * spots + lx * wy + ly
    which = jnp.where(side_x == 0, 0, jnp.where(side_x < 0, 2, 4)) + jnp.where(side_y > 0, 1, 0)
    strip = 3 * spots + which * GROUP + lx * 4 + jnp.where(ly < 2, ly, ly - (wy - 4))
    origin = jnp.where(valid, jnp.where(side_y == 0, whole, strip), -1)
    choice = ones_where(lax.broadcasted_iota(jnp.int32, (3 * spots + 256, span_l), 0) == origin)
    spread = ones_where(
        lax.broadcasted_iota(jnp.int32, (32, WIDE), 0) % 8 == lax.broadcasted_iota(jnp.int32, (32, WIDE), 1) // DIRS
    )

    for c in f_copies:
        c.wait()
    gathered_strips = []
    for first in (0, 4):
        groups = []
        for g in range(4):
            got = None
            for n in range(first, min(first + 4, 6)):
                v = strip_in[n]
                shift = (GROUP * (n - first - g)) % 128
                v = pltpu.roll(v, shift, 1) if shift else v
                got = v if got is None else jnp.where(lane // GROUP == n - first, v, got)
            groups.append(got)
        gathered_strips.append(jnp.concatenate(groups, 0))
    around = selected(
        jnp.concatenate([mine, block_in[0], block_in[1], *gathered_strips], 1), choice
    )
    pairs = [around[8 * g:8 * g + 8] for g in range(4)]
    fields = [f for v in pairs for f in (v, pltpu.roll(v, 4, 0))]
    f_e, f_h, kind, matter = fields[:3], fields[3:6], fields[6], fields[7]
    layer = sublanes_of((8, span_l))

    def f_next_x(f):
        return pltpu.roll(f, span_l - GROUP, 1)

    def f_prev_x(f):
        return pltpu.roll(f, GROUP, 1)

    def f_next_y(f):
        return jnp.where(p == rows_y - 1, pltpu.roll(f, rows_y - 1, 1), pltpu.roll(f, span_l - 1, 1))

    def f_prev_y(f):
        return jnp.where(p == 0, pltpu.roll(f, span_l - rows_y + 1, 1), pltpu.roll(f, 1, 1))

    def f_next_z(f):
        return jnp.where(layer < LAYERS - 1, pltpu.roll(f, 7, 0), 0.0)

    def f_prev_z(f):
        return jnp.where(layer >= 1, pltpu.roll(f, 1, 0), 0.0)

    eps = jnp.full((8, span_l), permittivity[0])
    slope = jnp.full((8, span_l), contrast[0])
    for k in range(1, permittivity.shape[0]):
        eps = jnp.where(matter == float(k), permittivity[k], eps)
        slope = jnp.where(matter == float(k), contrast[k], slope)
    ratio = time_step / eps
    coef = time_step * slope / (eps * eps)
    sources = []
    for step in range(STEPS):
        curl = curl_f(f_e, lambda c: f_next_x(f_e[c]), f_next_y, f_next_z)
        f_h = [f_h[c] - time_step * curl[c] for c in range(3)]
        curl = curl_b(f_h, lambda c: f_prev_x(f_h[c]), f_prev_y, f_prev_z)
        sources.append([coef * curl[c] for c in range(3)])
        f_e = [f_e[c] + ratio * curl[c] for c in range(3)]

    def wide(v, exact=True):
        v = jnp.where(layer < LAYERS, v, 0.0)
        zero = jnp.zeros_like(v)
        parts = stacked(v) + [zero] if exact else [v, zero, zero, zero]
        return lax.dot_general(
            jnp.concatenate(parts, 0).astype(jnp.bfloat16), spread, (((0,), (0,)), ((), ())),
            preferred_element_type=jnp.float32,
        )

    hot = wide(kind, False) == (lax.broadcasted_iota(jnp.int32, (1, WIDE), 1) % DIRS).astype(jnp.float32)
    v = wide(ratio)
    for x in range(1, wx + 3):
        inverse[x] = v[GROUP * x:GROUP * x + rows_y]
    for c in range(3):
        v = jnp.where(hot, wide(sources[0][c]), 0.0)
        for x in range(1, wx + 3):
            source_1[c, x] = v[GROUP * x:GROUP * x + rows_y]
        v = jnp.where(hot, wide(sources[1][c]), 0.0)
        for x in range(wx):
            source_2[c, x] = v[GROUP * (x + REACH):GROUP * (x + REACH) + wy]

    def h_first(x, rows):
        f = [te[c, x, rows, high] for c in range(3)]
        curl = curl_f(f, lambda c: te[c, x + 1, rows, high], next_y, next_z)
        for c in range(3):
            h_1[c, x, rows] = th[c, x, rows, high] - time_step * curl[c]

    def e_first(x, rows):
        hx, hy, hz = [h_1[c, x, rows] for c in range(3)]
        below = edge[0, x, rows] + time_step * jnp.where(left_half, -next_y(edge[1, x, rows]), edge[1, x + 1, rows])
        below_x = jnp.where(left_half, below, other_layer(hx))
        below_y = other_layer(jnp.where(left_half, hy, below))
        curl = (
            (hz - prev_y(hz)) - (hy - below_y),
            (hx - below_x) - (hz - h_1[2, x - 1, rows]),
            (hy - h_1[1, x - 1, rows]) - (hx - prev_y(hx)),
        )
        ratio = inverse[x, rows, high]
        for c in range(3):
            e_1[c, x, rows] = te[c, x, rows, high] + ratio * curl[c] - source_1[c, x, rows, high]

    def h_second(x, rows):
        curl = curl_f([e_1[c, x, rows] for c in range(3)], lambda c: e_1[c, x + 1, rows], next_y, next_z)
        for c in range(3):
            h_2[c, x, rows] = h_1[c, x, rows] - time_step * curl[c]

    def e_second(x, curl, comps, lanes, e):
        ratio = inverse[x, :wy, lanes]
        return [e(c) + ratio * curl[c][:wy] - source_2[c, x - x0, :, lanes] for c in range(comps)]

    def top_of(x, rows):
        curl = curl_b([h_2[c, x, rows] for c in range(3)], lambda c: h_2[c, x - 1, rows], prev_y, prev_z)
        return e_second(x, curl, 2, high, lambda c: e_1[c, x, :wy])

    copies = []

    def send_tops(first, last):
        span = pl.ds(first, last - first)
        for k in reversed(range(len(sheet))):
            to = mate if k % 2 == 0 else i
            q = 1 - core if k % 2 == 0 else core
            n = len(copies)
            c = copy(
                tops.at[q, span], gathered.at[(k + 1) // 2, core, span], g_send.at[n], g_recv.at[n], (to, sheet[k][1])
            )
            c.start()
            copies.append(((k + 1) // 2, c))

    def keep_top(u, got, inside):
        for q in range(2):
            v = jnp.where(left_half, other_layer(got[0][q]), got[1][q])
            if 0 < u < half - 1:
                v = pltpu.roll(v, wy - REACH, 0)
                if inside:
                    tops[q, (u - 1) * inner:u * inner] = v[:inner]
                else:
                    to = tail + (u - 1) * 2 * REACH
                    tops[q, to:to + 2 * REACH] = v[inner:]
            else:
                to = (half - 2) * wy + (wy if u else 0)
                tops[q, to:to + wy] = v

    mine_only = slice(0, wy)
    h_first(x0, mine_only)
    h_first(x0 + 1, mine_only)
    e_first(x0 + 1, mine_only)
    got = []
    for x in range(x0 + 2, x1 - 1):
        h_first(x, mine_only)
        e_first(x, mine_only)
        h_second(x - 1, mine_only)
        if x > x0 + 2:
            got.append(top_of(x - 1, mine_only))
    for u in range(1, half - 1):
        keep_top(u, got[2 * u - 2:2 * u], True)
    send_tops(0, tail)

    for c in early:
        c.wait()
    for c in late_x:
        c.start()

    every_row = slice(0, rows_y)
    h_first(0, every_row)
    h_first(1, every_row)
    e_first(1, every_row)
    h_first(2, every_row)
    e_first(2, every_row)
    h_second(1, every_row)
    for u in range(half):
        got = []
        for x in (2 * u + 3, 2 * u + 4):
            h_first(x, every_row)
            e_first(x, every_row)
            h_second(x - 1, every_row)
            got.append(top_of(x - 1, every_row))
        keep_top(u, got, False)
    send_tops(tail, half * wy)

    gathered[0, core] = tops[core]

    def top_parts(k):
        for at_k, c in copies:
            if at_k == k:
                c.wait_recv()
        near, far = split(gathered[k].reshape(block, 2 * DIRS))[:2]
        return jnp.concatenate([near, near, far], 0)

    def product(k, v, span):
        return jnp.dot(table[paired(j, k, ny), span], v, preferred_element_type=jnp.float32)

    spans = [slice(0, rows), slice(rows, 2 * rows)]
    sums = [0.0, 0.0]
    for k in range(ny):
        v = top_parts(k)
        if k < ny - 1:
            sums = [sums[n] + product(k, v, spans[n]) for n in range(2)]
    for c in late_y:
        c.start()
    out = []
    for n in range(2):
        total = sums[n] + product(ny - 1, v, spans[n])
        cosines, sines = total[:part_rows], total[part_rows:]
        mine = slice(n * part_rows, (n + 1) * part_rows)
        real = cosines * turn_c[mine] - sines * turn_s[mine]
        imag = sines * turn_c[mine] + cosines * turn_s[mine]
        real = real + pltpu.roll(real, DIRS, 1)
        imag = imag + pltpu.roll(imag, DIRS, 1)
        both = jnp.where(lower[mine], real, -imag)
        partial[n * nx // 2:(n + 1) * nx // 2] = both.reshape(nx // 2, own, 2 * DIRS)
        for b in range(n * nx // 2, (n + 1) * nx // 2):
            k = nx - 1 - b
            if k:
                c = copy(partial.at[b], arrived.at[k], p_send.at[k], p_recv.at[k], line[k - 1])
                c.start()
                out.append((k, c))
    for c in late_x + late_y:
        c.wait()

    def low_h_first(x):
        f = [te[c, x, :, low] for c in range(3)]

        def nz(c):
            return other_layer(jnp.where(left_half, te[c, x, :, high], f[c]))

        fx, fy, fz = f
        curl = (
            (next_y(fz) - fz) - (nz(1) - fy),
            (nz(0) - fx) - (te[2, x + 1, :, low] - fz),
            (te[1, x + 1, :, low] - fy) - (next_y(fx) - fx),
        )
        for c in range(3):
            th[c, x, :, low] = th[c, x, :, low] - time_step * curl[c]

    def low_e_first(x):
        g = [th[c, x, :, low] for c in range(3)]
        curl = curl_b(g, lambda c: th[c, x - 1, :, low], prev_y, prev_z)
        ratio = inverse[x, :, low]
        for c in range(3):
            te[c, x, :, low] = te[c, x, :, low] + ratio * curl[c] - source_1[c, x, :, low]

    def low_h_second(x):
        f = [te[c, x, :, low] for c in range(3)]

        def nz(c):
            return other_layer(jnp.where(left_half, e_1[c, x], f[c]))

        fx, fy, fz = f
        curl = (
            (next_y(fz) - fz) - (nz(1) - fy),
            (nz(0) - fx) - (te[2, x + 1, :, low] - fz),
            (te[1, x + 1, :, low] - fy) - (next_y(fx) - fx),
        )
        for c in range(3):
            th[c, x, :, low] = th[c, x, :, low] - time_step * curl[c]

    def rest(u, carry):
        x = u + 2
        low_h_first(x + 1)
        low_e_first(x + 1)
        low_h_second(x)
        g = [th[c, x, :, low] for c in range(3)]
        curl = curl_b(g, lambda c: th[c, x - 1, :, low], prev_y, prev_z)
        new = e_second(x, curl, 3, low, lambda c: te[c, x, :wy, low])
        hx, hy, hz = [h_2[c, x] for c in range(3)]
        below_x = other_layer(jnp.where(left_half, hx, g[0]))
        below_y = other_layer(jnp.where(left_half, hy, g[1]))
        curl = (
            (hz - prev_y(hz)) - (hy - below_y),
            (hx - below_x) - (hz - h_2[2, x - 1]),
            (hy - h_2[1, x - 1]) - (hx - prev_y(hx)),
        )
        above = e_second(x, curl, 3, high, lambda c: e_1[c, x, :wy])
        for c in range(3):
            out_e[c, u, :, low] = new[c]
            out_e[c, u, :, high] = above[c]
            out_h[c, u, :, low] = g[c][:wy]
            out_h[c, u, :, high] = h_2[c, x, :wy]
        return carry

    low_h_first(0)
    low_h_first(1)
    low_e_first(1)
    low_h_first(2)
    low_e_first(2)
    low_h_second(1)
    lax.fori_loop(0, wx, rest, 0, unroll=True)

    totals = [partial[nx - 1], None]
    for k, c in out[::-1]:
        c.wait_recv()
        totals[k % 2] = arrived[k] if totals[k % 2] is None else totals[k % 2] + arrived[k]
    out_s[:, :2 * DIRS] = jnp.where(core == 0, totals[0], totals[1])
    out_s[:, 2 * DIRS:] = jnp.where(core == 0, totals[1], totals[0])
    for _, c in copies + out:
        c.wait_send()


def hand_over(from_e, from_h, from_s, to_e, to_h, to_s, sem):
    copies = [
        pltpu.make_async_copy(src, dst, sem.at[k])
        for k, (src, dst) in enumerate(((from_e, to_e), (from_h, to_h), (from_s, to_s)))
    ]
    for c in copies:
        c.start()
    for c in copies:
        c.wait()


def local(nx, ny, te, th, fe, fh, classes, material, permittivity, contrast, orders):
    wx, wy = te.shape[1], te.shape[2]
    own = orders.shape[0] // (nx * ny)
    rows = nx * own
    f32 = jnp.float32
    vmem = pl.BlockSpec(memory_space=pltpu.VMEM)
    hbm = pl.BlockSpec(memory_space=pltpu.HBM)
    args = (
        te, th, jnp.transpose(fe, (0, 1, 3, 2)), jnp.transpose(fh, (0, 1, 3, 2)),
        jnp.transpose(classes, (0, 2, 1)), jnp.transpose(material, (0, 2, 1)),
        permittivity, contrast, jnp.transpose(orders),
    )
    args = tuple(pltpu.with_memory_space_constraint(v, pltpu.HBM) for v in args)
    out_shape = (
        jax.ShapeDtypeStruct(te.shape, f32),
        jax.ShapeDtypeStruct(th.shape, f32),
        jax.ShapeDtypeStruct((own, 4 * DIRS), f32),
    )
    wide_x, wide_y = wx + 2 * REACH, wy + PAD

    def pair_of(n):
        return [pltpu.SemaphoreType.DMA((n,))] * 2

    results = pl.pallas_call(
        functools.partial(kernel, nx, ny, own),
        out_shape=out_shape,
        in_specs=[hbm] * 9,
        out_specs=(vmem, vmem, vmem),
        scratch_shapes=[
            *[pltpu.VMEM((3, wide_x, wide_y, WIDE), f32)] * 2,
            pltpu.VMEM((2, wide_x, wide_y, HALF), f32),
            *[pltpu.VMEM((3, wide_x, wide_y, HALF), f32)] * 3,
            pltpu.VMEM((3, wide_x, wide_y, WIDE), f32),
            pltpu.VMEM((3, wx, wy, WIDE), f32),
            pltpu.VMEM((wide_x, wide_y, WIDE), f32),
            pltpu.VMEM((32, wx * wy), f32), pltpu.VMEM((2, 32, wx * wy), f32),
            pltpu.VMEM((8, 128), f32), pltpu.VMEM((6, 8, 128), f32),
            pltpu.VMEM((2, wx // 2 * wy, 2 * DIRS), f32),
            pltpu.VMEM((ny, 2, wx // 2 * wy, 2 * DIRS), f32),
            *[pltpu.VMEM((nx, own, 2 * DIRS), f32)] * 2,
            pltpu.VMEM((ny, 2 * rows, 3 * wx * wy), jnp.bfloat16),
            *pair_of(43), *pair_of(8), *pair_of(4 * ny), *pair_of(nx),
            *[pltpu.VMEM(v.shape, v.dtype) for v in args[2:6]],
            *[pltpu.SMEM(v.shape, v.dtype) for v in args[6:8]],
            pltpu.VMEM(args[8].shape, args[8].dtype),
            pltpu.SemaphoreType.DMA((13,)),
        ],
        compiler_params=pltpu.CompilerParams(
            collective_id=0, has_side_effects=True, vmem_limit_bytes=48 * 1024 * 1024
        ),
        name="slab",
    )(*args)
    return pl.pallas_call(
        hand_over,
        out_shape=out_shape,
        in_specs=[vmem] * 3,
        out_specs=(hbm, hbm, hbm),
        scratch_shapes=[pltpu.SemaphoreType.DMA((3,))],
        compiler_params=pltpu.CompilerParams(vmem_limit_bytes=16 * 1024 * 1024),
        name="hand_over",
    )(*results)


def solution(mesh):
    in_specs = (
        P(None, "gx", "gy", None),
        P(None, "gx", "gy", None),
        P(None, "gx", "gy", None),
        P(None, "gx", "gy", None),
        P("gx", "gy", None),
        P("gx", "gy", None),
        P(),
        P(),
        P(),
    )
    out_specs = (P(None, "gx", "gy", None), P(None, "gx", "gy", None), P(("gx", "gy"), None))
    body = functools.partial(local, mesh.shape["gx"], mesh.shape["gy"])
    return jax.shard_map(body, mesh=mesh, in_specs=in_specs, out_specs=out_specs, check_vma=False)
```
